128 devices in a mesh: front: 8 (over z, core), panel: 16 (over x, y).
Axes of the slice: x: 4, y: 4, z: 4, core: 2. Of those that a mesh axis runs over, the one named last changes fastest.
Arguments:
- pivot_columns: float32 [8, 8192, 1024], P('front', 'panel')
- child_rows: bfloat16 [8, 16, 16, 4, 8192], P('front', 'panel'), may hold values from -0.375 to 0.375
- slot_rows: int32 [8, 16, 16, 4], P('front', 'panel'), may hold values from -1 to 511, as said below
- parents: int32 [8], replicated, may hold values from 0 to 7, as said below
- pivot_rhs: float32 [8, 1024, 128], P('front'), may hold values from -6 to 6
- boundary_solution: float32 [8, 8192, 128], P('front', 'panel'), may hold values from -6 to 6
Outputs:
- panel_factor: float32 [8, 8192, 1024], P('front', 'panel')
- update_matrix: bfloat16 [8, 8192, 7168], P('front', 'panel')
- front_solution: float32 [8, 8192, 128], P('front', 'panel')
- child_solution: float32 [8, 16, 16, 4, 128], P('front', 'panel')
The draws below stay inside these ranges and needn't reach their ends.
Inputs may be any that keep to these rules, and one draw needn't show every extreme that they name: parents[c] is the front of this level into which child front c's rows are added; a front may take several children or none. `slot_rows`: the live slots of each tile of 4 slots come first; the rows that one child front sends to one destination device are distinct; for each child front one destination device receives full tiles from every source device.
All inputs are finite; a program needn't handle non-finite values.
Results may differ from the reference program's by a relative error of at most 0.007.
Values may be sent and summed in bfloat16 or wider, within the bound.
A program may use at most 192 MiB of HBM per device.

```python
import math
import jax
import jax.numpy as jnp
from jax import lax

FR = 8192
K = 512
NSTEP = 2
CAP = 4
NRHS = 128
RD = 512
PIV = 1024
N_FRONT = 8
N_PANEL = 16


def draw_pivot_columns(key, part):

    def one_front(front_key):
        noise_key, diag_key = jax.random.split(front_key, 2)
        noise = jax.random.normal(noise_key, (FR, PIV), jnp.float32)
        square = noise[:PIV]
        symmetric = (square + square.T) * (0.70710678 * 0.9 / math.sqrt(PIV))
        diagonal = jax.random.uniform(diag_key, (PIV,), jnp.float32, 3.0, 6.0)
        positions = jnp.arange(PIV)
        pivot_part = jnp.where(positions[:, None] == positions[None, :], diagonal[None, :], symmetric)
        coupling = noise[PIV:] * (4.0 / math.sqrt(PIV))
        return jnp.concatenate([pivot_part, coupling], axis=0)
    return lax.map(one_front, jax.random.split(key, N_FRONT))


def draw_slot_rows(key, part):
    perm_key, count_key, full_key, short_key = jax.random.split(jax.random.fold_in(key, 11), 4)
    perm_keys = jax.random.split(perm_key, N_FRONT * N_PANEL)
    perms = jax.vmap(lambda one_key: jax.random.permutation(one_key, RD))(perm_keys)
    perms = (perms - perms[:, :1] + RD - 1) % RD
    taken = perms[:, :N_PANEL * CAP].reshape(N_FRONT, N_PANEL, N_PANEL, CAP)
    rows_cpqs = jnp.transpose(taken, (0, 2, 1, 3))
    counts = jax.random.randint(count_key, (N_FRONT, N_PANEL, N_PANEL), 0, CAP + 1)
    full_dest = jax.random.randint(full_key, (N_FRONT,), 0, N_PANEL)
    dest_ids = jnp.arange(N_PANEL)[None, None, :]
    source_ids = jnp.arange(N_PANEL)[None, :, None]
    counts = jnp.where(dest_ids == full_dest[:, None, None], CAP, counts)
    short_dest = (full_dest + 1) % N_PANEL
    short_count = jax.random.randint(short_key, (N_FRONT, N_PANEL, N_PANEL), 0, CAP)
    counts = jnp.where((source_ids == 0) & (dest_ids == short_dest[:, None, None]), short_count, counts)
    live = jnp.arange(CAP)[None, None, None, :] < counts[..., None]
    return jnp.where(live, rows_cpqs, -1).astype(jnp.int32)


def draw_parents(key, part):
    hub_key, spread_key, coin_key, order_key = jax.random.split(jax.random.fold_in(key, 23), 4)
    hub_front = jax.random.randint(hub_key, (), 0, N_FRONT)
    spread = jax.random.randint(spread_key, (N_FRONT,), 0, N_FRONT)
    coin = jax.random.randint(coin_key, (N_FRONT,), 0, 2)
    result = jnp.where(coin == 1, hub_front, spread)
    order = jax.random.permutation(order_key, N_FRONT)
    result = result.at[order[0]].set(0).at[order[1]].set(N_FRONT - 1)
    return result.astype(jnp.int32)


def steps_of(own_key, shape, cuts, smallest, largest):
    def one(position, parts):
        heights = jax.random.uniform(jax.random.fold_in(jax.random.fold_in(own_key, 6), position), (parts,), jnp.float32, smallest / len(cuts), largest / len(cuts))
        return jnp.repeat(jnp.exp(heights), shape[position] // parts).reshape((-1,) + (1,) * (len(shape) - position - 1))

    level = one(*cuts[0])
    for cut in cuts[1:]:
        level = level * one(*cut)
    return level


def centred(rng, extent, scale, bound, shards=(), held_as=jnp.bfloat16):
    loudness = steps_of(rng, extent, shards, -0.22, 0.18) if shards else 1.0
    values = jax.random.normal(rng, extent, jnp.float32) * scale * loudness
    return jnp.minimum(jnp.maximum(values, -bound), bound).astype(held_as)


def setup_inputs(seed: int = 0) -> dict:
    streams_of = jax.random.split(jax.random.key(seed), 7)
    return {
        "pivot_columns": draw_pivot_columns(jax.random.fold_in(streams_of[6], 71), 0),
        "child_rows": centred(streams_of[1], (N_FRONT, N_PANEL, N_PANEL, CAP, FR), 0.025, 0.375, ((0, 8), (1, 16))),
        "slot_rows": draw_slot_rows(jax.random.fold_in(streams_of[6], 71), 0),
        "parents": draw_parents(jax.random.fold_in(streams_of[6], 71), 0),
        "pivot_rhs": centred(streams_of[4], (N_FRONT, PIV, NRHS), 1.0, 6.0, ((0, 8),), jnp.float32),
        "boundary_solution": centred(streams_of[5], (N_FRONT, FR, NRHS), 1.0, 6.0, ((0, 8), (1, 16)), jnp.float32),
    }


def reference(pivot_columns, child_rows, slot_rows, parents, pivot_rhs, boundary_solution):
    row_ids = jnp.arange(FR, dtype=jnp.int32)
    dest_panel = jnp.arange(N_PANEL, dtype=jnp.int32)[None, None, :, None]
    global_rows = (dest_panel * RD + slot_rows).astype(jnp.int32)
    live = slot_rows >= 0
    child_front = jnp.broadcast_to(parents[:, None, None, None], slot_rows.shape).astype(jnp.int32)
    rows_flat = child_rows.astype(jnp.float32).reshape(-1, FR)
    identity_block = jnp.eye(K, dtype=jnp.float32)
    highest = lax.Precision.HIGHEST

    def one_front(front_index):
        target = jnp.where(live & (child_front == front_index), global_rows, FR).reshape(-1).astype(jnp.int32)
        current = jnp.zeros((FR, FR), jnp.float32).at[target].add(rows_flat, mode='drop')
        current = current.at[:, :PIV].add(pivot_columns[front_index])
        factors = []
        inverses = []
        for panel_step in range(NSTEP):
            low_edge = panel_step * K
            high_edge = low_edge + K
            lower = jnp.linalg.cholesky(current[low_edge:high_edge, low_edge:high_edge])
            inverse = lax.linalg.triangular_solve(lower, identity_block, left_side=True, lower=True)
            column = jnp.dot(current[:, low_edge:high_edge], inverse.T, precision=highest)
            column = jnp.where(row_ids[:, None] >= low_edge, column, 0.0)
            packed = lax.optimization_barrier(column.astype(jnp.bfloat16)).astype(jnp.float32)
            current = current - jnp.dot(packed, packed.T, precision=highest)
            factors.append(column)
            inverses.append(inverse)
        update = jnp.where(row_ids[:, None] >= PIV, current[:, PIV:], 0.0).astype(jnp.bfloat16)
        right_side = pivot_rhs[front_index]
        solution = boundary_solution[front_index]
        for panel_step in reversed(range(NSTEP)):
            low_edge = panel_step * K
            high_edge = low_edge + K
            masked = jnp.where(row_ids[:, None] >= high_edge, factors[panel_step], 0.0)
            carried = jnp.dot(masked.T, solution, precision=highest)
            value = jnp.dot(inverses[panel_step].T, right_side[low_edge:high_edge] - carried, precision=highest)
            solution = solution.at[low_edge:high_edge].set(value)
        return (jnp.concatenate(factors, axis=1), update, solution)
    panel_factor, update_matrix, front_solution = lax.map(one_front, jnp.arange(N_FRONT, dtype=jnp.int32))
    picked = jnp.where(live, global_rows, 0).astype(jnp.int32)
    values = front_solution[child_front, picked]
    child_solution = jnp.where(live[..., None], values, 0.0)
    return (panel_factor, update_matrix, front_solution, child_solution)
```

```python
import jax
import jax.numpy as jnp
from jax import lax
from jax.experimental import pallas as pl
from jax.experimental.pallas import tpu as pltpu
from jax.sharding import PartitionSpec as P

K = 512
NB = 128
PIV = 1024
HIGHEST = lax.Precision.HIGHEST
HIGH = lax.Precision.HIGH
MESH = pl.DeviceIdType.MESH
F32 = jnp.float32
BF16 = jnp.bfloat16


def product(left, right, left_dim, right_dim, precision=HIGHEST):
    dims = (((left_dim,), (right_dim,)), ((), ()))
    return lax.dot_general(left, right, dims, precision=precision, preferred_element_type=F32)


def base_inverse(work, inverse):
    sub = lax.broadcasted_iota(jnp.int32, (8, NB), 0)
    lane = lax.broadcasted_iota(jnp.int32, (8, NB), 1)
    for tile in range(NB // 8):
        inverse[8 * tile : 8 * tile + 8, :] = (lane == sub + 8 * tile).astype(F32)
    for step in range(NB // 8):
        low = 8 * step
        left = work[low : low + 8, :]
        right = inverse[low : low + 8, :]
        columns = [jnp.broadcast_to(left[:, low + i : low + i + 1], (8, NB)) for i in range(8)]
        pivots = jnp.ones((8, NB), F32)
        recips, splats, rows = [], [], []
        for i in range(8):
            pivot = jnp.broadcast_to(columns[i][i : i + 1, :], (8, NB))
            recip = 1.0 / pivot
            recips.append(recip)
            pivots = jnp.where(sub == i, pivot, pivots)
            ratio = jnp.where(sub > i, columns[i] * recip, 0.0)
            splat = {}
            for j in range(i + 1, 8):
                splat[j] = jnp.broadcast_to(columns[j][i : i + 1, :], (8, NB))
                columns[j] = columns[j] - ratio * splat[j]
            splats.append(splat)
            left_row = jnp.broadcast_to(left[i : i + 1, :], (8, NB))
            right_row = jnp.broadcast_to(right[i : i + 1, :], (8, NB))
            rows.append((left_row, right_row))
            left = left - ratio * left_row
            right = right - ratio * right_row
        for tile in range(step + 1, NB // 8):
            at = 8 * tile
            left_tile = work[at : at + 8, :]
            right_tile = inverse[at : at + 8, :]
            ratios = []
            for i in range(8):
                value = jnp.broadcast_to(left_tile[:, low + i : low + i + 1], (8, NB))
                for j in range(i):
                    value = value - ratios[j] * splats[j][i]
                ratios.append(value * recips[i])
            for i in range(8):
                left_tile = left_tile - ratios[i] * rows[i][0]
                right_tile = right_tile - ratios[i] * rows[i][1]
            work[at : at + 8, :] = left_tile
            inverse[at : at + 8, :] = right_tile
        inverse[low : low + 8, :] = right * lax.rsqrt(pivots)


def factor_inverse(work, inverse, base_work, base_out):
    inverse[...] = jnp.zeros_like(inverse)
    for block in range(K // NB):
        low, high = block * NB, block * NB + NB
        base_work[...] = work[low:high, low:high]
        base_inverse(base_work, base_out)
        base = base_out[...]
        if block:
            inverse[low:high, 0:low] = product(base, inverse[low:high, 0:low], 1, 0)
        inverse[low:high, low:high] = base
        if high < K:
            upper = product(base, work[low:high, high:], 1, 0)
            work[high:, high:] = work[high:, high:] - product(upper, upper, 0, 0)
            inverse[high:, 0:high] = inverse[high:, 0:high] - product(upper, inverse[low:high, 0:high], 0, 0)


def pivot_kernel(top, inverse0, inverse1, factor10, work, base_work, base_out):
    block = top[0, :, 0:K]
    work[...] = (block + block.T) * 0.5
    factor_inverse(work, inverse0, base_work, base_out)
    lower = product(top[1, :, 0:K], inverse0[...], 1, 1)
    factor10[...] = lower
    packed = lower.astype(BF16)
    block = top[1, :, K:] - product(packed, packed, 1, 1, None)
    work[...] = (block + block.T) * 0.5
    factor_inverse(work, inverse1, base_work, base_out)


def factor_pivots(top):
    square = jax.ShapeDtypeStruct((K, K), F32)
    return pl.pallas_call(
        pivot_kernel,
        out_shape=(square, square, square),
        in_specs=[pl.BlockSpec(memory_space=pltpu.VMEM)],
        out_specs=[pl.BlockSpec(memory_space=pltpu.VMEM)] * 3,
        scratch_shapes=[pltpu.VMEM((K, K), F32), pltpu.VMEM((NB, NB), F32), pltpu.VMEM((NB, NB), F32)],
        compiler_params=pltpu.CompilerParams(vmem_limit_bytes=40 << 20),
        cost_estimate=pl.CostEstimate(flops=60_000_000_000, bytes_accessed=8 << 20, transcendentals=0),
    )(top)


def spread_kernel(count, mine, top, chunk, scatter_send, scatter_recv, gather_send, gather_recv, local_sem):
    me = lax.axis_index("panel")
    part = mine.shape[0] // count
    barrier = pltpu.get_barrier_semaphore()
    for shift in range(1, count):
        peer = lax.rem(me + shift, count)
        pl.semaphore_signal(barrier, inc=1, device_id={"panel": peer}, device_id_type=MESH)
    pl.semaphore_wait(barrier, count - 1)

    def scatter(shift, root):
        peer = lax.rem(me + shift, count)
        return pltpu.make_async_remote_copy(
            src_ref=mine.at[pl.ds(pl.multiple_of(peer * part, 8), part)],
            dst_ref=chunk.at[root],
            send_sem=scatter_send.at[root, shift],
            recv_sem=scatter_recv.at[root],
            device_id={"panel": peer},
            device_id_type=MESH,
        )

    for root in range(2):

        @pl.when(me == root)
        def _():
            for shift in range(1, count):
                scatter(shift, root).start()
            own = pltpu.make_async_copy(
                mine.at[pl.ds(pl.multiple_of(me * part, 8), part)], chunk.at[root], local_sem
            )
            own.start()
            own.wait()

        @pl.when(me != root)
        def _():
            scatter(1, root).wait_recv()

    def gather(shift):
        peer = lax.rem(me + shift, count)
        return pltpu.make_async_remote_copy(
            src_ref=chunk,
            dst_ref=top.at[:, pl.ds(pl.multiple_of(me * part, 8), part)],
            send_sem=gather_send.at[shift],
            recv_sem=gather_recv.at[shift],
            device_id={"panel": peer},
            device_id_type=MESH,
        )

    for shift in range(1, count):
        gather(shift).start()
    own = pltpu.make_async_copy(chunk, top.at[:, pl.ds(pl.multiple_of(me * part, 8), part)], local_sem)
    own.start()
    own.wait()
    for shift in range(1, count):
        gather(shift).wait()
    for root in range(2):

        @pl.when(me == root)
        def _():
            for shift in range(1, count):
                scatter(shift, root).wait_send()


def spread_pivots(count, mine):
    rows, width = mine.shape
    return pl.pallas_call(
        lambda *refs: spread_kernel(count, *refs),
        name="spread",
        out_shape=jax.ShapeDtypeStruct((2, rows, width), F32),
        in_specs=[pl.BlockSpec(memory_space=pl.ANY)],
        out_specs=pl.BlockSpec(memory_space=pl.ANY),
        scratch_shapes=[
            pltpu.VMEM((2, rows // count, width), F32),
            pltpu.SemaphoreType.DMA((2, count)),
            pltpu.SemaphoreType.DMA((2,)),
            pltpu.SemaphoreType.DMA((count,)),
            pltpu.SemaphoreType.DMA((count,)),
            pltpu.SemaphoreType.DMA,
        ],
        compiler_params=pltpu.CompilerParams(collective_id=0, has_side_effects=True),
    )(mine)


def on_device(panel_count, pivot_columns, child_rows, slot_rows, parents, pivot_rhs, boundary_solution):
    panel_index = lax.axis_index("panel")
    front_index = lax.axis_index("front")
    piv_cols = pivot_columns[0]
    row_count = piv_cols.shape[0]
    pivots = piv_cols.shape[1]
    rows_out = child_rows[0, 0]
    cap = rows_out.shape[1]
    local_ids = jnp.arange(row_count, dtype=jnp.int32)

    def exchange(value):
        moved = lax.all_to_all(value, "panel", split_axis=0, concat_axis=0, tiled=True)
        return lax.all_gather(moved, "front", axis=0)

    slots = exchange(slot_rows[0, 0])
    keeping = parents == front_index
    kept = jnp.where(keeping[:, None, None], slots, -1).reshape(-1)
    onehot = (kept[None, :] == local_ids[:, None]).astype(BF16)
    early = exchange(rows_out[:, :, :pivots])
    known = boundary_solution[0]
    columns = piv_cols + jnp.dot(onehot, early.reshape(-1, pivots), preferred_element_type=F32)
    gathered = lax.all_gather(columns.astype(BF16), "panel", axis=0, tiled=True)
    late = exchange(rows_out[:, :, pivots:])
    below = panel_index >= pivots // row_count
    sums = lax.psum(product(columns, jnp.where(below, known, 0.0), 0, 0), "panel")

    top = spread_pivots(panel_count, columns)
    inverse0, inverse1, factor10 = factor_pivots(top)
    packed10 = factor10.astype(BF16)

    factor0 = product(columns[:, :K], inverse0, 1, 1, HIGH)
    current = columns[:, K:] - product(factor0.astype(BF16), packed10, 1, 1, None)
    factor1 = jnp.where(panel_index >= 1, product(current, inverse1, 1, 1, HIGH), 0.0)
    weight1 = product(factor1, inverse1, 1, 0, HIGH)
    weight0 = product(factor0 - product(weight1, factor10, 1, 0, HIGH), inverse0, 1, 0, HIGH)
    weights = jnp.concatenate([weight0, weight1], axis=1).astype(BF16)
    factor_all = jnp.concatenate([factor0, factor1], axis=1)

    trailing = jnp.dot(onehot, late.reshape(-1, late.shape[-1]), preferred_element_type=F32)
    trailing = trailing - product(weights, gathered[pivots:], 1, 1, None)
    update_matrix = jnp.where(below, trailing, 0.0).astype(BF16)

    sums0, sums1 = sums[:K], sums[K:]
    right_side = pivot_rhs[0]
    half = product(inverse0, sums0, 1, 0)
    carried1 = product(inverse1, sums1 - product(factor10, half, 1, 0), 1, 0)
    solved1 = product(inverse1, right_side[K:] - carried1, 0, 0)
    carried0 = half + product(factor10, solved1, 0, 0)
    solved0 = product(inverse0, right_side[:K] - carried0, 0, 0)
    front_values = jnp.where(below, known, jnp.where(panel_index == 0, solved0, solved1))

    pick = (kept[:, None] == local_ids[None, :]).astype(F32)
    picked = product(pick, front_values, 1, 0).reshape(slots.shape[0], -1, front_values.shape[-1])
    picked = jnp.sum(lax.all_to_all(picked, "front", split_axis=0, concat_axis=0, tiled=True), axis=0)
    picked = picked.reshape(-1, cap, picked.shape[-1])
    child_values = lax.all_to_all(picked, "panel", split_axis=0, concat_axis=0, tiled=True)
    return (factor_all[None], update_matrix[None], front_values[None], child_values[None, None])


def solution(mesh):
    in_specs = (
        P("front", "panel", None),
        P("front", "panel", None, None, None),
        P("front", "panel", None, None),
        P(),
        P("front", None, None),
        P("front", "panel", None),
    )
    out_specs = (
        P("front", "panel", None),
        P("front", "panel", None),
        P("front", "panel", None),
        P("front", "panel", None, None, None),
    )
    panel_count = mesh.shape["panel"]
    return jax.shard_map(
        lambda *arrays: on_device(panel_count, *arrays),
        mesh=mesh,
        in_specs=in_specs,
        out_specs=out_specs,
        check_vma=False,
    )
```

```python
import math

import jax
import jax.numpy as jnp
from jax import lax
from jax.experimental import pallas as pl
from jax.experimental.pallas import tpu as pltpu
from jax.sharding import PartitionSpec as P

K = 512
NB = 128
PIV = 1024
HIGHEST = lax.Precision.HIGHEST
HIGH = lax.Precision.HIGH
MESH = pl.DeviceIdType.MESH
F32 = jnp.float32
BF16 = jnp.bfloat16


def product(left, right, left_dim, right_dim, precision=HIGHEST):
    dims = (((left_dim,), (right_dim,)), ((), ()))
    return lax.dot_general(left, right, dims, precision=precision, preferred_element_type=F32)


def base_inverse(work, inverse):
    sub = lax.broadcasted_iota(jnp.int32, (8, NB), 0)
    lane = lax.broadcasted_iota(jnp.int32, (NB, NB), 1)
    row = lax.broadcasted_iota(jnp.int32, (NB, NB), 0)
    inverse[...] = (lane == row).astype(F32)
    for step in range(NB // 8):
        low = 8 * step
        left = work[low : low + 8, :]
        right = inverse[low : low + 8, :]
        columns = [jnp.broadcast_to(left[:, low + i : low + i + 1], (8, NB)) for i in range(8)]
        pivots = jnp.ones((8, NB), F32)
        recips, splats, rows = [], [], []
        for i in range(8):
            pivot = columns[i][i : i + 1, :]
            recip = 1.0 / pivot
            recips.append(recip)
            pivots = jnp.where(sub == i, pivot, pivots)
            ratio = jnp.where(sub > i, columns[i] * recip, 0.0)
            splat = {}
            for j in range(i + 1, 8):
                splat[j] = columns[j][i : i + 1, :]
                columns[j] = columns[j] - ratio * splat[j]
            splats.append(splat)
            rows.append((left[i : i + 1, :], right[i : i + 1, :]))
            left = left - ratio * rows[i][0]
            right = right - ratio * rows[i][1]
        at = low + 8
        while at < NB:
            size = min(32 - at % 32, NB - at)
            left_tile = work[at : at + size, :]
            right_tile = inverse[at : at + size, :]
            ratios = []
            for i in range(8):
                value = jnp.broadcast_to(left_tile[:, low + i : low + i + 1], (size, NB))
                for j in range(i):
                    value = value - ratios[j] * splats[j][i]
                ratios.append(value * recips[i])
            for i in range(8):
                left_tile = left_tile - ratios[i] * rows[i][0]
                right_tile = right_tile - ratios[i] * rows[i][1]
            work[at : at + size, :] = left_tile
            inverse[at : at + size, :] = right_tile
            at += size
        inverse[low : low + 8, :] = right * lax.rsqrt(pivots)


def symmetric_part(block):
    return (block + block.T) * 0.5


def factor_block(low, work, inverse, base_work, base_out):
    rows = pl.ds(low, NB)
    base_work[...] = work[rows, rows]
    base_inverse(base_work, base_out)
    base = base_out[...]
    upper = product(base, work[rows, :], 1, 0)
    lane = lax.broadcasted_iota(jnp.int32, upper.shape, 1)
    upper = jnp.where(lane >= low + NB, upper, 0.0)
    solved = product(base, inverse[rows, :], 1, 0)
    work[...] = work[...] - product(upper, upper, 0, 0)
    inverse[...] = inverse[...] - product(upper, solved, 0, 0)
    inverse[rows, :] = solved


def exchange_kernel(
    counts, rows, slots, early, late, table, send_a, recv_a, send_b, recv_b, send_s, recv_s,
    front_send, front_recv, front_send_s, front_recv_s, local_sem
):
    panels, fronts = counts
    me = lax.axis_index("panel")
    front = lax.axis_index("front")
    tiles = early.shape[1]
    barrier = pltpu.get_barrier_semaphore()
    for shift in range(1, panels):
        peer = lax.rem(me + shift, panels)
        pl.semaphore_signal(barrier, inc=1, device_id={"panel": peer}, device_id_type=MESH)
    for shift in range(1, fronts):
        peer = lax.rem(front + shift, fronts)
        pl.semaphore_signal(barrier, inc=1, device_id={"front": peer}, device_id_type=MESH)
    pl.semaphore_wait(barrier, panels + fronts - 2)

    def to_panel(source, target, send, recv, shift):
        peer = lax.rem(me + shift, panels)
        return pltpu.make_async_remote_copy(
            src_ref=source(peer),
            dst_ref=target,
            send_sem=send.at[shift],
            recv_sem=recv.at[shift],
            device_id={"panel": peer},
            device_id_type=MESH,
        )

    def early_copy(shift):
        return to_panel(lambda p: rows.at[p, pl.ds(0, tiles)], early.at[front, :, me], send_a, recv_a, shift)

    def slot_copy(shift):
        return to_panel(lambda p: slots.at[p], table.at[front, me], send_s, recv_s, shift)

    def late_copy(shift):
        return to_panel(lambda p: rows.at[p, pl.ds(tiles, late.shape[0])], late.at[:, me], send_b, recv_b, shift)

    for shift in range(1, panels):
        slot_copy(shift).start()
        early_copy(shift).start()
    own = [
        pltpu.make_async_copy(rows.at[me, pl.ds(0, tiles)], early.at[front, :, me], local_sem.at[0]),
        pltpu.make_async_copy(slots.at[me], table.at[front, me], local_sem.at[1]),
        pltpu.make_async_copy(rows.at[me, pl.ds(tiles, late.shape[0])], late.at[:, me], local_sem.at[2]),
    ]
    for copy in own:
        copy.start()
    for shift in range(1, panels):
        late_copy(shift).start()
    for copy in own:
        copy.wait()
    for shift in range(1, panels):
        slot_copy(shift).wait_recv()
        early_copy(shift).wait_recv()

    def to_front(array, send, recv, shift):
        peer = lax.rem(front + shift, fronts)
        return pltpu.make_async_remote_copy(
            src_ref=array.at[front],
            dst_ref=array.at[front],
            send_sem=send.at[shift],
            recv_sem=recv.at[shift],
            device_id={"front": peer},
            device_id_type=MESH,
        )

    for shift in range(1, fronts):
        to_front(table, front_send_s, front_recv_s, shift).start()
        to_front(early, front_send, front_recv, shift).start()
    for shift in range(1, panels):
        slot_copy(shift).wait_send()
        early_copy(shift).wait_send()
        late_copy(shift).wait()
    for shift in range(1, fronts):
        to_front(table, front_send_s, front_recv_s, shift).wait()
        to_front(early, front_send, front_recv, shift).wait()


def exchange_rows(panels, fronts, rows, slots, tiles):
    _, all_tiles, cap, lanes = rows.shape
    sem = pltpu.SemaphoreType.DMA
    return pl.pallas_call(
        lambda *refs: exchange_kernel((panels, fronts), *refs),
        name="exchange",
        out_shape=(
            jax.ShapeDtypeStruct((fronts, tiles, panels, cap, lanes), BF16),
            jax.ShapeDtypeStruct((all_tiles - tiles, panels, cap, lanes), BF16),
            jax.ShapeDtypeStruct((fronts, panels, cap, lanes), jnp.int32),
        ),
        in_specs=[pl.BlockSpec(memory_space=pl.ANY)] * 2,
        out_specs=[pl.BlockSpec(memory_space=pl.ANY)] * 3,
        scratch_shapes=[sem((panels,))] * 6 + [sem((fronts,))] * 4 + [sem((3,))],
        compiler_params=pltpu.CompilerParams(collective_id=1, has_side_effects=True),
    )(rows, slots)


def panel_kernel(
    counts, side, halves, columns, partial, late, blocks, inverses, factor10, sums, late_all,
    top, chunk, pieces, work, base_work, base_out,
    scatter_send, scatter_recv, whole_send, whole_recv, half_send, half_recv,
    far_send, far_recv, farther_send, farther_recv,
    piece_send, piece_recv, sum_send, sum_recv, late_send, late_recv, local_sem,
):
    panels, fronts = counts
    me = lax.axis_index("panel")
    front = lax.axis_index("front")
    across, along = me // side, lax.rem(me, side)
    part = top.shape[1] // panels
    barrier = pltpu.get_barrier_semaphore()
    for shift in range(1, panels):
        peer = lax.rem(me + shift, panels)
        pl.semaphore_signal(barrier, inc=1, device_id={"panel": peer}, device_id_type=MESH)
    for shift in range(1, fronts):
        peer = lax.rem(front + shift, fronts)
        pl.semaphore_signal(barrier, inc=1, device_id={"front": peer}, device_id_type=MESH)
    pl.semaphore_wait(barrier, panels + fronts - 2)

    def chunk_rows(who):
        return pl.ds(pl.multiple_of(who * part, 8), part)

    def scatter(shift, index):
        peer = lax.rem(me + shift, panels)
        lanes = pl.ds(K if index == 2 else 0, K)
        return pltpu.make_async_remote_copy(
            src_ref=columns.at[chunk_rows(peer), lanes],
            dst_ref=chunk.at[index],
            send_sem=scatter_send.at[index, shift],
            recv_sem=scatter_recv.at[index],
            device_id={"panel": peer},
            device_id_type=MESH,
        )

    def own_chunk(index):
        lanes = pl.ds(K if index == 2 else 0, K)
        return pltpu.make_async_copy(columns.at[chunk_rows(me), lanes], chunk.at[index], local_sem.at[index])

    roots = ((0, (0,)), (1, (1, 2)))
    for root, indices in roots:

        @pl.when(me == root)
        def _():
            for shift in range(1, panels):
                for index in indices:
                    scatter(shift, index).start()
            for index in indices:
                own_chunk(index).start()

    def place(half, first, second):
        first, second = lax.rem(first + side, side), lax.rem(second + side, side)
        return first * side + second if half == 0 else second * side + first

    spots = (across, along), (along, across)

    def view(kind, half, who, rows):
        if kind == 0:
            size = part if rows is None else part // 2
            low = who * part + (part // 2 if rows == 1 else 0)
            return top.at[:, pl.ds(pl.multiple_of(low, 8), size), pl.ds(half * (K // 2), K // 2)]
        ref = blocks.at[half, who]
        return ref if rows is None else ref.at[pl.ds(rows * (K // 2), K // 2)]

    def move(kind, half, who, rows, target, send, recv, slot):
        ref = view(kind, half, who, rows)
        return pltpu.make_async_remote_copy(
            src_ref=ref,
            dst_ref=ref,
            send_sem=send.at[slot],
            recv_sem=recv.at[slot],
            device_id={"panel": target},
            device_id_type=MESH,
        )

    def whole(kind, half, way):
        u, v = spots[half]
        target = place(half, u + (1 if way == 0 else -1), v)
        return move(kind, half, me, None, target, whole_send, whole_recv, (kind, half, way))

    def halved(kind, half, way):
        u, v = spots[half]
        step = 1 if way == 0 else -1
        return move(
            kind, half, place(half, u - step, v), way, place(half, u + step, v), half_send, half_recv, (kind, half, way)
        )

    def far(kind, half, offset, way):
        u, v = spots[half]
        target = place(half, u, v + (1 if way == 0 else -1))
        return move(
            kind, half, place(half, u + offset, v), None, target, far_send, far_recv, (kind, half, offset, way)
        )

    def farther(kind, half, offset, way):
        u, v = spots[half]
        step = 1 if way == 0 else -1
        return move(
            kind, half, place(half, u + offset, v - step), way, place(half, u, v + step),
            farther_send, farther_recv, (kind, half, offset, way),
        )

    both = [(half, way) for half in range(2) for way in range(2)]

    def begin(kind):
        for half, way in both:
            whole(kind, half, way).start()
        for half, way in both:
            far(kind, half, 0, way).start()

    def second(kind):
        for half, way in both:
            whole(kind, half, way).wait_recv()
            halved(kind, half, way).start()
        for half, way in both:
            far(kind, half, 1, way).start()
            far(kind, half, 3, way).start()

    def third(kind):
        for half in range(2):
            for way in range(2):
                halved(kind, half, way).wait_recv()
            for way in range(2):
                far(kind, half, 2, way).start()

    def relay(kind, offset):
        for half, way in both:
            far(kind, half, offset, way).wait_recv()
            farther(kind, half, offset, way).start()

    def finish(kind):
        for half, way in both:
            for offset in range(4):
                farther(kind, half, offset, way).wait_recv()

    def drain(kind):
        for half, way in both:
            whole(kind, half, way).wait_send()
            halved(kind, half, way).wait_send()
            for offset in range(4):
                far(kind, half, offset, way).wait_send()
                farther(kind, half, offset, way).wait_send()

    def late_copy(shift):
        peer = lax.rem(front + shift, fronts)
        return pltpu.make_async_remote_copy(
            src_ref=late,
            dst_ref=late_all.at[front],
            send_sem=late_send.at[shift],
            recv_sem=late_recv.at[shift],
            device_id={"front": peer},
            device_id_type=MESH,
        )

    def piece_copy(shift):
        peer = lax.rem(me + shift, panels)
        return pltpu.make_async_remote_copy(
            src_ref=partial.at[peer],
            dst_ref=pieces.at[me],
            send_sem=piece_send.at[shift],
            recv_sem=piece_recv.at[shift],
            device_id={"panel": peer},
            device_id_type=MESH,
        )

    def sum_copy(shift):
        peer = lax.rem(me + shift, panels)
        return pltpu.make_async_remote_copy(
            src_ref=sums.at[me],
            dst_ref=sums.at[me],
            send_sem=sum_send.at[shift],
            recv_sem=sum_recv.at[shift],
            device_id={"panel": peer},
            device_id_type=MESH,
        )

    own = [
        pltpu.make_async_copy(halves, blocks.at[:, me], local_sem.at[3]),
        pltpu.make_async_copy(partial.at[me], pieces.at[me], local_sem.at[4]),
        pltpu.make_async_copy(late, late_all.at[front], local_sem.at[5]),
    ]
    for copy in own:
        copy.start()
    for copy in own:
        copy.wait()
    for root, indices in roots:
        for index in indices:

            @pl.when(me == root)
            def _():
                own_chunk(index).wait()

            @pl.when(me != root)
            def _():
                scatter(1, index).wait_recv()

    top[:, chunk_rows(me), :] = chunk[...]
    begin(0)
    begin(1)
    for shift in range(1, fronts):
        late_copy(shift).start()
    for shift in range(1, panels):
        piece_copy(shift).start()
    second(0)
    third(0)
    for offset in (0, 1, 3, 2):
        relay(0, offset)
    finish(0)
    second(1)

    lane = lax.broadcasted_iota(jnp.int32, (K, K), 1)
    row = lax.broadcasted_iota(jnp.int32, (K, K), 0)

    def block_step(index, carry):
        which = index // (K // NB)

        @pl.when(index == 0)
        def _():
            work[...] = symmetric_part(top[0])
            inverses[0] = (lane == row).astype(F32)

        @pl.when(index == K // NB)
        def _():
            lower = product(top[1], inverses[0], 1, 1)
            factor10[...] = lower
            packed = lower.astype(BF16)
            work[...] = symmetric_part(top[2] - product(packed, packed, 1, 1, None))
            inverses[1] = (lane == row).astype(F32)

        low = pl.multiple_of((index - which * (K // NB)) * NB, NB)
        factor_block(low, work, inverses.at[which], base_work, base_out)

        @pl.when(index == 1)
        def _():
            third(1)
            relay(1, 0)

        @pl.when(index == 2)
        def _():
            for shift in range(1, panels):
                piece_copy(shift).wait_recv()
            total = pieces[0]
            for who in range(1, panels):
                total = total + pieces[who]
            sums[me] = total
            for shift in range(1, panels):
                sum_copy(shift).start()

        @pl.when(index == 3)
        def _():
            relay(1, 1)
            relay(1, 3)

        @pl.when(index == 6)
        def _():
            relay(1, 2)

        return carry

    lax.fori_loop(0, 2 * (K // NB), block_step, 0)
    finish(1)
    drain(0)
    drain(1)
    for shift in range(1, panels):
        piece_copy(shift).wait_send()
        sum_copy(shift).wait()
    for shift in range(1, fronts):
        late_copy(shift).wait()
    for root, indices in roots:

        @pl.when(me == root)
        def _():
            for shift in range(1, panels):
                for index in indices:
                    scatter(shift, index).wait_send()


def panel_step(panels, fronts, side, halves, columns, partial, late):
    sem = pltpu.SemaphoreType.DMA
    part = K // panels
    anywhere = pl.BlockSpec(memory_space=pl.ANY)
    vmem = pl.BlockSpec(memory_space=pltpu.VMEM)
    return pl.pallas_call(
        lambda *refs: panel_kernel((panels, fronts), side, *refs),
        name="panel_step",
        out_shape=(
            jax.ShapeDtypeStruct((2, panels, K, K), BF16),
            jax.ShapeDtypeStruct((2, K, K), F32),
            jax.ShapeDtypeStruct((K, K), F32),
            jax.ShapeDtypeStruct(partial.shape, F32),
            jax.ShapeDtypeStruct((fronts,) + late.shape, BF16),
        ),
        in_specs=[anywhere] * 4,
        out_specs=[anywhere, vmem, vmem, vmem, anywhere],
        scratch_shapes=[
            pltpu.VMEM((3, K, K), F32),
            pltpu.VMEM((3, part, K), F32),
            pltpu.VMEM(partial.shape, F32),
            pltpu.VMEM((K, K), F32),
            pltpu.VMEM((NB, NB), F32),
            pltpu.VMEM((NB, NB), F32),
            sem((3, panels)),
            sem((3,)),
        ]
        + [sem((2, 2, 2))] * 4
        + [sem((2, 2, 4, 2))] * 4
        + [sem((panels,))] * 4
        + [sem((fronts,))] * 2
        + [sem((6,))],
        compiler_params=pltpu.CompilerParams(
            collective_id=2, has_side_effects=True, vmem_limit_bytes=40 << 20
        ),
    )(halves, columns, partial, late)


def on_device(sizes, pivot_columns, child_rows, slot_rows, parents, pivot_rhs, boundary_solution):
    panels, fronts, side = sizes
    panel_index = lax.axis_index("panel")
    front_index = lax.axis_index("front")
    piv_cols = pivot_columns[0]
    row_count, pivots = piv_cols.shape
    rows_out = child_rows[0, 0]
    cap, width = rows_out.shape[1:]
    lanes = NB
    local_ids = jnp.arange(row_count, dtype=jnp.int32)

    rows_tiled = rows_out.reshape(panels, cap, width // lanes, lanes).transpose(0, 2, 1, 3)
    slots_wide = jnp.broadcast_to(slot_rows[0, 0][:, :, None], (panels, cap, lanes))
    early, late, table = exchange_rows(panels, fronts, rows_tiled, slots_wide, pivots // lanes)
    slots = table[:, :, :, 0].reshape(fronts, panels * cap)
    keeping = parents == front_index
    kept = jnp.where(keeping[:, None], slots, -1).reshape(-1)
    onehot = (kept[None, :] == local_ids[:, None]).astype(BF16)
    early = early.reshape(fronts, pivots // lanes, panels * cap, lanes)
    spread = jnp.einsum(
        "rck,ctkl->rtl", onehot.reshape(row_count, fronts, panels * cap), early, preferred_element_type=F32
    )
    columns = piv_cols + spread.reshape(row_count, pivots)
    known = boundary_solution[0]
    below = panel_index >= pivots // row_count
    halves = jnp.stack([columns[:, :K], columns[:, K:]]).astype(BF16)
    partial = product(columns, jnp.where(below, known, 0.0), 0, 0, HIGH)
    partial = partial.reshape(panels, pivots // panels, -1)

    blocks, inverses, factor10, sums, late_all = panel_step(
        panels, fronts, side, halves, columns, partial, late
    )
    inverse0, inverse1 = inverses[0], inverses[1]
    packed10 = factor10.astype(BF16)

    factor0 = product(columns[:, :K], inverse0, 1, 1, HIGH)
    current = columns[:, K:] - product(factor0.astype(BF16), packed10, 1, 1, None)
    factor1 = jnp.where(panel_index >= 1, product(current, inverse1, 1, 1, HIGH), 0.0)
    weight1 = product(factor1, inverse1, 1, 0, HIGH)
    weight0 = product(factor0 - product(weight1, factor10, 1, 0, HIGH), inverse0, 1, 0, HIGH)
    factor_all = jnp.concatenate([factor0, factor1], axis=1)
    first = pivots // K
    trailing = jnp.einsum(
        "rck,ctkl->rtl",
        onehot.reshape(row_count, fronts, panels * cap),
        late_all.reshape(fronts, -1, panels * cap, lanes),
        preferred_element_type=F32,
    ).reshape(row_count, -1)
    gathered = blocks[:, first:].reshape(2, -1, K)
    trailing = trailing - product(weight0.astype(BF16), gathered[0], 1, 1, None)
    trailing = trailing - product(weight1.astype(BF16), gathered[1], 1, 1, None)
    update_matrix = jnp.where(below, trailing, 0.0).astype(BF16)

    sums = sums.reshape(pivots, -1)
    sums0, sums1 = sums[:K], sums[K:]
    right_side = pivot_rhs[0]
    half = product(inverse0, sums0, 1, 0)
    carried1 = product(inverse1, sums1 - product(factor10, half, 1, 0), 1, 0)
    solved1 = product(inverse1, right_side[K:] - carried1, 0, 0)
    carried0 = half + product(factor10, solved1, 0, 0)
    solved0 = product(inverse0, right_side[:K] - carried0, 0, 0)
    front_values = jnp.where(below, known, jnp.where(panel_index == 0, solved0, solved1))

    pick = (kept[:, None] == local_ids[None, :]).astype(F32)
    picked = product(pick, front_values, 1, 0).reshape(fronts, panels * cap, -1)
    picked = jnp.sum(lax.all_to_all(picked, "front", split_axis=0, concat_axis=0, tiled=True), axis=0)
    picked = picked.reshape(panels, cap, -1)
    child_values = lax.all_to_all(picked, "panel", split_axis=0, concat_axis=0, tiled=True)
    return (factor_all[None], update_matrix[None], front_values[None], child_values[None, None])


def solution(mesh):
    in_specs = (
        P("front", "panel", None),
        P("front", "panel", None, None, None),
        P("front", "panel", None, None),
        P(),
        P("front", None, None),
        P("front", "panel", None),
    )
    out_specs = (
        P("front", "panel", None),
        P("front", "panel", None),
        P("front", "panel", None),
        P("front", "panel", None, None, None),
    )
    panels, fronts = mesh.shape["panel"], mesh.shape["front"]
    sizes = (panels, fronts, math.isqrt(panels))
    return jax.shard_map(
        lambda *arrays: on_device(sizes, *arrays),
        mesh=mesh,
        in_specs=in_specs,
        out_specs=out_specs,
        check_vma=False,
    )
```

```python
import math

import jax
import jax.numpy as jnp
from jax import lax
from jax.experimental import pallas as pl
from jax.experimental.pallas import tpu as pltpu
from jax.sharding import PartitionSpec as P

K = 512
NB = 128
PIV = 1024
HIGHEST = lax.Precision.HIGHEST
HIGH = lax.Precision.HIGH
MESH = pl.DeviceIdType.MESH
F32 = jnp.float32
BF16 = jnp.bfloat16


def product(left, right, left_dim, right_dim, precision=HIGHEST):
    dims = (((left_dim,), (right_dim,)), ((), ()))
    return lax.dot_general(left, right, dims, precision=precision, preferred_element_type=F32)


def base_inverse(work, inverse):
    sub = lax.broadcasted_iota(jnp.int32, (8, NB), 0)
    lane = lax.broadcasted_iota(jnp.int32, (NB, NB), 1)
    row = lax.broadcasted_iota(jnp.int32, (NB, NB), 0)
    inverse[...] = (lane == row).astype(F32)
    for step in range(NB // 8):
        low = 8 * step
        left = work[low : low + 8, :]
        right = inverse[low : low + 8, :]
        columns = [jnp.broadcast_to(left[:, low + i : low + i + 1], (8, NB)) for i in range(8)]
        pivots = jnp.ones((8, NB), F32)
        recips, splats, rows = [], [], []
        for i in range(8):
            pivot = columns[i][i : i + 1, :]
            recip = 1.0 / pivot
            recips.append(recip)
            pivots = jnp.where(sub == i, pivot, pivots)
            ratio = jnp.where(sub > i, columns[i] * recip, 0.0)
            splat = {}
            for j in range(i + 1, 8):
                splat[j] = columns[j][i : i + 1, :]
                columns[j] = columns[j] - ratio * splat[j]
            splats.append(splat)
            rows.append((left[i : i + 1, :], right[i : i + 1, :]))
            left = left - ratio * rows[i][0]
            right = right - ratio * rows[i][1]
        at = low + 8
        while at < NB:
            size = min(32 - at % 32, NB - at)
            left_tile = work[at : at + size, :]
            right_tile = inverse[at : at + size, :]
            ratios = []
            for i in range(8):
                value = jnp.broadcast_to(left_tile[:, low + i : low + i + 1], (size, NB))
                for j in range(i):
                    value = value - ratios[j] * splats[j][i]
                ratios.append(value * recips[i])
            for i in range(8):
                left_tile = left_tile - ratios[i] * rows[i][0]
                right_tile = right_tile - ratios[i] * rows[i][1]
            work[at : at + size, :] = left_tile
            inverse[at : at + size, :] = right_tile
            at += size
        inverse[low : low + 8, :] = right * lax.rsqrt(pivots)


def symmetric_part(block):
    return (block + block.T) * 0.5


def factor_block(low, work, inverse, base_work, base_out):
    rows = pl.ds(low, NB)
    base_work[...] = work[rows, rows]
    base_inverse(base_work, base_out)
    base = base_out[...]
    upper = product(base, work[rows, :], 1, 0)
    lane = lax.broadcasted_iota(jnp.int32, upper.shape, 1)
    upper = jnp.where(lane >= low + NB, upper, 0.0)
    solved = product(base, inverse[rows, :], 1, 0)
    work[...] = work[...] - product(upper, upper, 0, 0)
    inverse[...] = inverse[...] - product(upper, solved, 0, 0)
    inverse[rows, :] = solved


def exchange_kernel(
    counts, rows, slots, early, late, table, own_table, send_a, recv_a, send_b, recv_b, send_s, recv_s,
    front_send, front_recv, front_send_s, front_recv_s, own_send, own_recv, local_sem
):
    panels, fronts = counts
    me = lax.axis_index("panel")
    front = lax.axis_index("front")
    tiles = early.shape[1]
    barrier = pltpu.get_barrier_semaphore()
    for shift in range(1, panels):
        peer = lax.rem(me + shift, panels)
        pl.semaphore_signal(barrier, inc=1, device_id={"panel": peer}, device_id_type=MESH)
    for shift in range(1, fronts):
        peer = lax.rem(front + shift, fronts)
        pl.semaphore_signal(barrier, inc=1, device_id={"front": peer}, device_id_type=MESH)
    pl.semaphore_wait(barrier, panels + fronts - 2)

    def to_panel(source, target, send, recv, shift):
        peer = lax.rem(me + shift, panels)
        return pltpu.make_async_remote_copy(
            src_ref=source(peer),
            dst_ref=target,
            send_sem=send.at[shift],
            recv_sem=recv.at[shift],
            device_id={"panel": peer},
            device_id_type=MESH,
        )

    def early_copy(shift):
        return to_panel(lambda p: rows.at[p, pl.ds(0, tiles)], early.at[front, :, me], send_a, recv_a, shift)

    def slot_copy(shift):
        return to_panel(lambda p: slots.at[p], table.at[front, me], send_s, recv_s, shift)

    def late_copy(shift):
        return to_panel(lambda p: rows.at[p, pl.ds(tiles, late.shape[0])], late.at[:, me], send_b, recv_b, shift)

    lead = own_table.shape[1]

    def own_copy(shift):
        peer = lax.rem(front + shift, fronts)
        return pltpu.make_async_remote_copy(
            src_ref=slots.at[pl.ds(0, lead)],
            dst_ref=own_table.at[front],
            send_sem=own_send.at[shift],
            recv_sem=own_recv.at[shift],
            device_id={"front": peer},
            device_id_type=MESH,
        )

    for shift in range(1, panels):
        slot_copy(shift).start()
        early_copy(shift).start()
    for shift in range(1, fronts):
        own_copy(shift).start()
    own = [
        pltpu.make_async_copy(slots.at[pl.ds(0, lead)], own_table.at[front], local_sem.at[3]),
        pltpu.make_async_copy(rows.at[me, pl.ds(0, tiles)], early.at[front, :, me], local_sem.at[0]),
        pltpu.make_async_copy(slots.at[me], table.at[front, me], local_sem.at[1]),
        pltpu.make_async_copy(rows.at[me, pl.ds(tiles, late.shape[0])], late.at[:, me], local_sem.at[2]),
    ]
    for copy in own:
        copy.start()
    for shift in range(1, panels):
        late_copy(shift).start()
    for copy in own:
        copy.wait()
    for shift in range(1, panels):
        slot_copy(shift).wait_recv()
        early_copy(shift).wait_recv()

    def to_front(array, send, recv, shift):
        peer = lax.rem(front + shift, fronts)
        return pltpu.make_async_remote_copy(
            src_ref=array.at[front],
            dst_ref=array.at[front],
            send_sem=send.at[shift],
            recv_sem=recv.at[shift],
            device_id={"front": peer},
            device_id_type=MESH,
        )

    for shift in range(1, fronts):
        to_front(table, front_send_s, front_recv_s, shift).start()
        to_front(early, front_send, front_recv, shift).start()
    for shift in range(1, panels):
        slot_copy(shift).wait_send()
        early_copy(shift).wait_send()
        late_copy(shift).wait()
    for shift in range(1, fronts):
        to_front(table, front_send_s, front_recv_s, shift).wait()
        to_front(early, front_send, front_recv, shift).wait()
        own_copy(shift).wait()


def exchange_rows(panels, fronts, lead, rows, slots, tiles):
    _, all_tiles, cap, lanes = rows.shape
    sem = pltpu.SemaphoreType.DMA
    return pl.pallas_call(
        lambda *refs: exchange_kernel((panels, fronts), *refs),
        name="exchange",
        out_shape=(
            jax.ShapeDtypeStruct((fronts, tiles, panels, cap, lanes), BF16),
            jax.ShapeDtypeStruct((all_tiles - tiles, panels, cap, lanes), BF16),
            jax.ShapeDtypeStruct((fronts, panels, cap, lanes), jnp.int32),
            jax.ShapeDtypeStruct((fronts, lead, cap, lanes), jnp.int32),
        ),
        in_specs=[pl.BlockSpec(memory_space=pl.ANY)] * 2,
        out_specs=[pl.BlockSpec(memory_space=pl.ANY)] * 4,
        scratch_shapes=[sem((panels,))] * 6 + [sem((fronts,))] * 6 + [sem((4,))],
        compiler_params=pltpu.CompilerParams(collective_id=1, has_side_effects=True),
    )(rows, slots)


def assembly_kernel(parents, table, own_table, early, piv_cols, known, columns, halves, onehot, pick, picked):
    front = lax.axis_index("front")
    fronts, _, each, lanes = early.shape
    owners = [parents[child] == front for child in range(fronts)]

    def masked(ref, size):
        return jnp.concatenate(
            [jnp.where(owners[c], ref[c * size : (c + 1) * size, :], -1) for c in range(fronts)], axis=0
        )

    kept = masked(table, each)
    lane = lax.broadcasted_iota(jnp.int32, kept.shape, 1)
    chosen = jnp.concatenate(
        [(kept == lane + t * lanes).astype(F32) for t in range(known.shape[0] // lanes)], axis=1
    )
    small = chosen.astype(BF16)
    onehot[...] = small
    half = piv_cols.shape[1] // 2
    for h in range(2):
        tiles = half // lanes
        rows = jnp.concatenate(
            [early[:, h * tiles + t].reshape(fronts * each, lanes) for t in range(tiles)], axis=1
        )
        value = piv_cols[:, h * half : (h + 1) * half] + product(small, rows, 0, 0, None)
        columns[:, h * half : (h + 1) * half] = value
        halves[h] = value.astype(BF16)
    picked[...] = product(chosen, known[...], 1, 0)
    size = own_table.shape[0] // fronts
    own = masked(own_table, size)
    cap = size * K // piv_cols.shape[1]
    where = lax.rem(lax.broadcasted_iota(jnp.int32, own.shape, 0), size) // cap
    target = jnp.where(own >= 0, own + where * K, -1)
    lane = lax.broadcasted_iota(jnp.int32, own.shape, 1)
    for t in range(pick.shape[1] // lanes):
        pick[:, t * lanes : (t + 1) * lanes] = (target == lane + t * lanes).astype(F32)


def assemble(parents, table, own_table, early, piv_cols, known):
    rows, pivots = piv_cols.shape
    vmem = pl.BlockSpec(memory_space=pltpu.VMEM)
    return pl.pallas_call(
        assembly_kernel,
        name="assemble",
        out_shape=(
            jax.ShapeDtypeStruct((rows, pivots), F32),
            jax.ShapeDtypeStruct((2, rows, pivots // 2), BF16),
            jax.ShapeDtypeStruct((table.shape[0], rows), BF16),
            jax.ShapeDtypeStruct((own_table.shape[0], pivots), F32),
            jax.ShapeDtypeStruct((table.shape[0], known.shape[1]), F32),
        ),
        in_specs=[pl.BlockSpec(memory_space=pltpu.SMEM)] + [vmem] * 5,
        out_specs=[vmem] * 5,
        compiler_params=pltpu.CompilerParams(vmem_limit_bytes=40 << 20),
    )(parents, table, own_table, early, piv_cols, known)


def panel_kernel(
    counts, side, halves, columns, known, right_side, pick, picked, late,
    blocks, late_all, factor, weights, front_values, child_values,
    inverses, factor10, partial, sums, solved, chosen, chosen_in, from_fronts, onward, inward,
    top, chunk, pieces, work, base_work, base_out,
    scatter_send, scatter_recv, whole_send, whole_recv, half_send, half_recv,
    far_send, far_recv, farther_send, farther_recv,
    piece_send, piece_recv, sum_send, sum_recv, inward_send, inward_recv,
    late_send, late_recv, over_send, over_recv, pick_send, pick_recv, local_sem,
):
    panels, fronts = counts
    me = lax.axis_index("panel")
    front = lax.axis_index("front")
    across, along = me // side, lax.rem(me, side)
    part = top.shape[1] // panels
    barrier = pltpu.get_barrier_semaphore()
    for shift in range(1, panels):
        peer = lax.rem(me + shift, panels)
        pl.semaphore_signal(barrier, inc=1, device_id={"panel": peer}, device_id_type=MESH)
    for shift in range(1, fronts):
        peer = lax.rem(front + shift, fronts)
        pl.semaphore_signal(barrier, inc=1, device_id={"front": peer}, device_id_type=MESH)
    pl.semaphore_wait(barrier, panels + fronts - 2)

    def chunk_rows(who):
        return pl.ds(pl.multiple_of(who * part, 8), part)

    def scatter(shift, index):
        peer = lax.rem(me + shift, panels)
        lanes = pl.ds(K if index == 2 else 0, K)
        return pltpu.make_async_remote_copy(
            src_ref=columns.at[chunk_rows(peer), lanes],
            dst_ref=chunk.at[index],
            send_sem=scatter_send.at[index, shift],
            recv_sem=scatter_recv.at[index],
            device_id={"panel": peer},
            device_id_type=MESH,
        )

    def own_chunk(index):
        lanes = pl.ds(K if index == 2 else 0, K)
        return pltpu.make_async_copy(columns.at[chunk_rows(me), lanes], chunk.at[index], local_sem.at[index])

    roots = ((0, (0,)), (1, (1, 2)))
    for root, indices in roots:

        @pl.when(me == root)
        def _():
            for shift in range(1, panels):
                for index in indices:
                    scatter(shift, index).start()
            for index in indices:
                own_chunk(index).start()

    def place(half, first, second):
        first, second = lax.rem(first + side, side), lax.rem(second + side, side)
        return first * side + second if half == 0 else second * side + first

    spots = (across, along), (along, across)

    def view(kind, half, who, rows):
        if kind == 0:
            size = part if rows is None else part // 2
            low = who * part + (part // 2 if rows == 1 else 0)
            return top.at[:, pl.ds(pl.multiple_of(low, 8), size), pl.ds(half * (K // 2), K // 2)]
        ref = blocks.at[half, who]
        return ref if rows is None else ref.at[pl.ds(rows * (K // 2), K // 2)]

    def move(kind, half, who, rows, target, send, recv, slot):
        ref = view(kind, half, who, rows)
        return pltpu.make_async_remote_copy(
            src_ref=ref,
            dst_ref=ref,
            send_sem=send.at[slot],
            recv_sem=recv.at[slot],
            device_id={"panel": target},
            device_id_type=MESH,
        )

    def whole(kind, half, way):
        u, v = spots[half]
        step = 1 if way == 0 else -1
        copy = move(kind, half, me, None, place(half, u + step, v), whole_send, whole_recv, (kind, half, way))
        return kind, copy, me, place(half, u - step, v)

    def halved(kind, half, way):
        u, v = spots[half]
        step = 1 if way == 0 else -1
        who = place(half, u - step, v)
        copy = move(kind, half, who, way, place(half, u + step, v), half_send, half_recv, (kind, half, way))
        return kind, copy, who, place(half, u + 2, v)

    def far(kind, half, offset, way):
        u, v = spots[half]
        step = 1 if way == 0 else -1
        who = place(half, u + offset, v)
        copy = move(kind, half, who, None, place(half, u, v + step), far_send, far_recv, (kind, half, offset, way))
        return kind, copy, who, place(half, u + offset, v - step)

    def farther(kind, half, offset, way):
        u, v = spots[half]
        step = 1 if way == 0 else -1
        who = place(half, u + offset, v - step)
        copy = move(
            kind, half, who, way, place(half, u, v + step), farther_send, farther_recv, (kind, half, offset, way)
        )
        return kind, copy, who, place(half, u + offset, v + 2)

    def guarded(kind, who, act):
        if kind == 0:
            act()
        else:
            pl.when(who >= 2)(act)

    def start(hop):
        guarded(hop[0], hop[2], hop[1].start)

    def sent(hop):
        guarded(hop[0], hop[2], hop[1].wait_send)

    def arrived(hop):
        guarded(hop[0], hop[3], hop[1].wait_recv)

    both = [(half, way) for half in range(2) for way in range(2)]

    def begin(kind):
        for half, way in both:
            start(whole(kind, half, way))
        for half, way in both:
            start(far(kind, half, 0, way))

    def second(kind):
        for half, way in both:
            arrived(whole(kind, half, way))
            start(halved(kind, half, way))
        for half, way in both:
            start(far(kind, half, 1, way))
            start(far(kind, half, 3, way))

    def third(kind):
        for half in range(2):
            for way in range(2):
                arrived(halved(kind, half, way))
            for way in range(2):
                start(far(kind, half, 2, way))

    def relay(kind, offset):
        for half, way in both:
            arrived(far(kind, half, offset, way))
            start(farther(kind, half, offset, way))

    def finish(kind):
        for half, way in both:
            for offset in range(4):
                arrived(farther(kind, half, offset, way))

    def drain(kind):
        for half, way in both:
            sent(whole(kind, half, way))
            sent(halved(kind, half, way))
            for offset in range(4):
                sent(far(kind, half, offset, way))
                sent(farther(kind, half, offset, way))

    def over_copy(shift):
        peer = lax.rem(front + shift, fronts)
        return pltpu.make_async_remote_copy(
            src_ref=picked.at[peer],
            dst_ref=from_fronts.at[front],
            send_sem=over_send.at[shift],
            recv_sem=over_recv.at[shift],
            device_id={"front": peer},
            device_id_type=MESH,
        )

    def inward_copy(shift):
        peer = lax.rem(me + shift, panels)
        return pltpu.make_async_remote_copy(
            src_ref=onward.at[peer],
            dst_ref=inward.at[me],
            send_sem=inward_send.at[shift],
            recv_sem=inward_recv.at[shift],
            device_id={"panel": peer},
            device_id_type=MESH,
        )

    def pick_copy(shift):
        peer = lax.rem(front + shift, fronts)
        return pltpu.make_async_remote_copy(
            src_ref=chosen.at[peer],
            dst_ref=chosen_in.at[front],
            send_sem=pick_send.at[shift],
            recv_sem=pick_recv.at[shift],
            device_id={"front": peer},
            device_id_type=MESH,
        )

    def late_copy(shift):
        peer = lax.rem(front + shift, fronts)
        return pltpu.make_async_remote_copy(
            src_ref=late,
            dst_ref=late_all.at[front],
            send_sem=late_send.at[shift],
            recv_sem=late_recv.at[shift],
            device_id={"front": peer},
            device_id_type=MESH,
        )

    def piece_copy(shift):
        peer = lax.rem(me + shift, panels)
        return pltpu.make_async_remote_copy(
            src_ref=partial.at[peer],
            dst_ref=pieces.at[me],
            send_sem=piece_send.at[shift],
            recv_sem=piece_recv.at[shift],
            device_id={"panel": peer},
            device_id_type=MESH,
        )

    def sum_copy(shift):
        peer = lax.rem(me + shift, panels)
        return pltpu.make_async_remote_copy(
            src_ref=sums.at[me],
            dst_ref=sums.at[me],
            send_sem=sum_send.at[shift],
            recv_sem=sum_recv.at[shift],
            device_id={"panel": peer},
            device_id_type=MESH,
        )

    own = [
        pltpu.make_async_copy(halves, blocks.at[:, me], local_sem.at[3]),
        pltpu.make_async_copy(picked.at[front], from_fronts.at[front], local_sem.at[4]),
        pltpu.make_async_copy(late, late_all.at[front], local_sem.at[5]),
    ]
    for copy in own:
        copy.start()
    for shift in range(1, fronts):
        over_copy(shift).start()
    for copy in own:
        copy.wait()
    begin(1)
    for shift in range(1, fronts):
        late_copy(shift).start()
    for root, indices in roots:
        for index in indices:

            @pl.when(me == root)
            def _():
                own_chunk(index).wait()

            @pl.when(me != root)
            def _():
                scatter(1, index).wait_recv()

    top[:, chunk_rows(me), :] = chunk[...]
    begin(0)
    below = me >= 2
    boundary = jnp.where(below, known[...], 0.0)
    width = partial.shape[1]
    for half in range(2):
        value = product(columns[:, half * K : (half + 1) * K], boundary, 0, 0)
        for piece in range(panels // 2):
            partial[half * (panels // 2) + piece] = value[piece * width : (piece + 1) * width, :]
    for shift in range(1, panels):
        piece_copy(shift).start()
    pieces[me] = partial[me]
    second(0)
    third(0)
    for offset in (0, 1, 3, 2):
        relay(0, offset)
    finish(0)
    second(1)

    lane = lax.broadcasted_iota(jnp.int32, (K, K), 1)
    row = lax.broadcasted_iota(jnp.int32, (K, K), 0)

    def block_step(index, carry):
        which = index // (K // NB)

        @pl.when(index == 0)
        def _():
            work[...] = symmetric_part(top[0])
            inverses[0] = (lane == row).astype(F32)

        @pl.when(index == K // NB)
        def _():
            lower = product(top[1], inverses[0], 1, 1)
            factor10[...] = lower
            packed = lower.astype(BF16)
            work[...] = symmetric_part(top[2] - product(packed, packed, 1, 1, None))
            inverses[1] = (lane == row).astype(F32)

        low = pl.multiple_of((index - which * (K // NB)) * NB, NB)
        factor_block(low, work, inverses.at[which], base_work, base_out)

        @pl.when(index == 1)
        def _():
            third(1)
            relay(1, 0)
            for shift in range(1, fronts):
                over_copy(shift).wait_recv()
            total = from_fronts[0]
            for who in range(1, fronts):
                total = total + from_fronts[who]
            onward[...] = total
            for shift in range(1, panels):
                inward_copy(shift).start()

        @pl.when(index == 2)
        def _():
            for shift in range(1, panels):
                piece_copy(shift).wait_recv()
            total = pieces[0]
            for who in range(1, panels):
                total = total + pieces[who]
            sums[me] = total
            for shift in range(1, panels):
                sum_copy(shift).start()

        @pl.when(index == 3)
        def _():
            relay(1, 1)
            relay(1, 3)

        @pl.when(index == 5)
        def _():
            relay(1, 2)

        return carry

    lax.fori_loop(0, 2 * (K // NB), block_step, 0)

    for shift in range(1, panels):
        sum_copy(shift).wait_recv()
    inverse0, inverse1, lower = inverses[0], inverses[1], factor10[...]
    count = panels // 2
    sums0 = jnp.concatenate([sums[piece] for piece in range(count)], axis=0)
    sums1 = jnp.concatenate([sums[count + piece] for piece in range(count)], axis=0)
    carried0 = product(inverse0, sums0, 1, 0)
    carried1 = product(inverse1, sums1 - product(lower, carried0, 1, 0), 1, 0)
    solved1 = product(inverse1, right_side[K:, :] - carried1, 0, 0)
    solved0 = product(inverse0, right_side[0:K, :] - carried0 - product(lower, solved1, 0, 0), 0, 0)
    solved[0:K, :] = solved0
    solved[K:, :] = solved1
    values = product(pick[...], solved[...], 1, 0)
    size = chosen.shape[1]
    for child in range(fronts):
        chosen[child] = values[child * size : (child + 1) * size, :]
    for shift in range(1, fronts):
        pick_copy(shift).start()
    chosen_in[front] = chosen[front]
    front_values[...] = jnp.where(below, known[...], jnp.where(me == 0, solved0, solved1))

    factor0 = product(columns[:, 0:K], inverse0, 1, 1)
    current = columns[:, K:] - product(factor0.astype(BF16), lower.astype(BF16), 1, 1, None)
    factor1 = jnp.where(me >= 1, product(current, inverse1, 1, 1), 0.0)
    factor[:, 0:K] = factor0
    factor[:, K:] = factor1
    weight1 = product(factor1, inverse1, 1, 0)
    weight0 = product(factor0 - product(weight1, lower, 1, 0), inverse0, 1, 0)
    weights[0] = weight0.astype(BF16)
    weights[1] = weight1.astype(BF16)

    for shift in range(1, panels):
        inward_copy(shift).wait_recv()
    child_values[...] = inward[...]
    child_values[me] = onward[me]
    for shift in range(1, fronts):
        pick_copy(shift).wait_recv()
    total = chosen_in[0]
    for who in range(1, fronts):
        total = total + chosen_in[who]
    cap = child_values.shape[1]
    for lead in range(size // cap):
        child_values[lead] = total[lead * cap : (lead + 1) * cap, :]
    finish(1)
    drain(0)
    drain(1)
    for shift in range(1, panels):
        piece_copy(shift).wait_send()
        sum_copy(shift).wait_send()
        inward_copy(shift).wait_send()
    for shift in range(1, fronts):
        over_copy(shift).wait_send()
        pick_copy(shift).wait_send()
    for shift in range(1, fronts):
        late_copy(shift).wait()
    for root, indices in roots:

        @pl.when(me == root)
        def _():
            for shift in range(1, panels):
                for index in indices:
                    scatter(shift, index).wait_send()


def panel_step(sizes, halves, columns, known, right_side, pick, picked, late):
    panels, fronts, side = sizes
    sem = pltpu.SemaphoreType.DMA
    part = K // panels
    rows, pivots = columns.shape
    rhs = known.shape[1]
    cap = picked.shape[2]
    anywhere = pl.BlockSpec(memory_space=pl.ANY)
    vmem = pl.BlockSpec(memory_space=pltpu.VMEM)
    wide = pltpu.VMEM((panels, pivots // panels, rhs), F32)
    few = pltpu.VMEM((fronts, pick.shape[0] // fronts, rhs), F32)
    slot = pltpu.VMEM((panels, cap, rhs), F32)
    square = pltpu.VMEM((K, K), F32)
    tile = pltpu.VMEM((NB, NB), F32)
    return pl.pallas_call(
        lambda *refs: panel_kernel((panels, fronts), side, *refs),
        name="panel_step",
        out_shape=(
            jax.ShapeDtypeStruct((2, panels, K, K), BF16),
            jax.ShapeDtypeStruct((fronts,) + late.shape, BF16),
            jax.ShapeDtypeStruct((rows, pivots), F32),
            jax.ShapeDtypeStruct((2, K, K), BF16),
            jax.ShapeDtypeStruct((rows, rhs), F32),
            jax.ShapeDtypeStruct((panels, cap, rhs), F32),
        ),
        in_specs=[anywhere] + [vmem] * 5 + [anywhere],
        out_specs=[anywhere] * 2 + [vmem] * 4,
        scratch_shapes=[
            pltpu.VMEM((2, K, K), F32),
            square,
            wide,
            wide,
            pltpu.VMEM((pivots, rhs), F32),
            few,
            few,
            pltpu.VMEM((fronts, panels, cap, rhs), F32),
            slot,
            slot,
            pltpu.VMEM((3, K, K), F32),
            pltpu.VMEM((3, part, K), F32),
            wide,
            square,
            tile,
            tile,
            sem((3, panels)),
            sem((3,)),
        ]
        + [sem((2, 2, 2))] * 4
        + [sem((2, 2, 4, 2))] * 4
        + [sem((panels,))] * 6
        + [sem((fronts,))] * 6
        + [sem((6,))],
        compiler_params=pltpu.CompilerParams(
            collective_id=2, has_side_effects=True, vmem_limit_bytes=50 << 20
        ),
    )(halves, columns, known, right_side, pick, picked, late)


def update_kernel(late, blocks, weights, onehot, factor, front_values, child_values, update, *rest):
    outs, sem = rest[:3], rest[3]
    step = pl.program_id(0)
    results = (factor, front_values, child_values)

    @pl.when(step == 0)
    def _():
        for i in range(3):
            pltpu.make_async_copy(results[i], outs[i], sem.at[i]).start()

    fronts, tiles, each, lanes = late.shape
    rows = jnp.concatenate([late[:, t].reshape(fronts * each, lanes) for t in range(tiles)], axis=1)
    value = product(onehot[...], rows, 0, 0, None)
    for half in range(2):
        value = value - product(weights[half], blocks[half, 0], 1, 1, None)
    update[...] = jnp.where(lax.axis_index("panel") >= 2, value, 0.0).astype(BF16)

    @pl.when(step == pl.num_programs(0) - 1)
    def _():
        for i in range(3):
            pltpu.make_async_copy(results[i], outs[i], sem.at[i]).wait()


def update_step(late_all, blocks, weights, onehot, factor, front_values, child_values):
    fronts, all_tiles, each, lanes = late_all.shape
    tiles = K // lanes
    steps = all_tiles // tiles
    first = blocks.shape[1] - steps
    rows = weights.shape[1]
    anywhere = pl.BlockSpec(memory_space=pl.ANY)
    fixed = pl.BlockSpec(memory_space=pltpu.VMEM)
    like = [jax.ShapeDtypeStruct(x.shape, x.dtype) for x in (factor, front_values, child_values)]
    return pl.pallas_call(
        update_kernel,
        name="update",
        grid=(steps,),
        out_shape=[jax.ShapeDtypeStruct((rows, steps * K), BF16)] + like,
        in_specs=[
            pl.BlockSpec((fronts, tiles, each, lanes), lambda j: (0, j, 0, 0)),
            pl.BlockSpec((2, 1, K, K), lambda j: (0, j + first, 0, 0)),
            fixed,
            fixed,
            anywhere,
            anywhere,
            anywhere,
        ],
        out_specs=[pl.BlockSpec((rows, K), lambda j: (0, j))] + [anywhere] * 3,
        scratch_shapes=[pltpu.SemaphoreType.DMA((3,))],
        compiler_params=pltpu.CompilerParams(vmem_limit_bytes=40 << 20),
    )(late_all, blocks, weights, onehot, factor, front_values, child_values)


def on_device(sizes, pivot_columns, child_rows, slot_rows, parents, pivot_rhs, boundary_solution):
    panels, fronts, _ = sizes
    piv_cols = pivot_columns[0]
    pivots = piv_cols.shape[1]
    rows_out = child_rows[0, 0]
    cap, width = rows_out.shape[1:]
    lanes = NB
    lead = pivots // K
    each = panels * cap
    known = boundary_solution[0]

    rows_tiled = rows_out.reshape(panels, cap, width // lanes, lanes).transpose(0, 2, 1, 3)
    slots_wide = jnp.broadcast_to(slot_rows[0, 0][:, :, None], (panels, cap, lanes))
    early, late, table, own_table = exchange_rows(panels, fronts, lead, rows_tiled, slots_wide, pivots // lanes)
    columns, halves, onehot, pick, picked = assemble(
        parents,
        table.reshape(fronts * each, lanes),
        own_table.reshape(fronts * lead * cap, lanes),
        early.reshape(fronts, pivots // lanes, each, lanes),
        piv_cols,
        known,
    )
    blocks, late_all, factor, weights, front_values, child_values = panel_step(
        sizes, halves, columns, known, pivot_rhs[0], pick, picked.reshape(fronts, panels, cap, -1), late
    )
    update_matrix, factor, front_values, child_values = update_step(
        late_all.reshape(fronts, -1, each, lanes), blocks, weights, onehot, factor, front_values, child_values
    )
    return (factor[None], update_matrix[None], front_values[None], child_values[None, None])


def solution(mesh):
    in_specs = (
        P("front", "panel", None),
        P("front", "panel", None, None, None),
        P("front", "panel", None, None),
        P(),
        P("front", None, None),
        P("front", "panel", None),
    )
    out_specs = (
        P("front", "panel", None),
        P("front", "panel", None),
        P("front", "panel", None),
        P("front", "panel", None, None, None),
    )
    panels, fronts = mesh.shape["panel"], mesh.shape["front"]
    sizes = (panels, fronts, math.isqrt(panels))
    return jax.shard_map(
        lambda *arrays: on_device(sizes, *arrays),
        mesh=mesh,
        in_specs=in_specs,
        out_specs=out_specs,
        check_vma=False,
    )
```

```python
import math

import jax
import jax.numpy as jnp
from jax import lax
from jax.experimental import pallas as pl
from jax.experimental.pallas import tpu as pltpu
from jax.sharding import PartitionSpec as P

K = 512
NB = 128
PIV = 1024
HIGHEST = lax.Precision.HIGHEST
HIGH = lax.Precision.HIGH
MESH = pl.DeviceIdType.MESH
F32 = jnp.float32
BF16 = jnp.bfloat16


def product(left, right, left_dim, right_dim, precision=HIGHEST):
    dims = (((left_dim,), (right_dim,)), ((), ()))
    return lax.dot_general(left, right, dims, precision=precision, preferred_element_type=F32)


def base_inverse(work, inverse):
    sub = lax.broadcasted_iota(jnp.int32, (8, NB), 0)
    lane = lax.broadcasted_iota(jnp.int32, (NB, NB), 1)
    row = lax.broadcasted_iota(jnp.int32, (NB, NB), 0)
    inverse[...] = (lane == row).astype(F32)
    for step in range(NB // 8):
        low = 8 * step
        left = work[low : low + 8, :]
        right = inverse[low : low + 8, :]
        columns = [jnp.broadcast_to(left[:, low + i : low + i + 1], (8, NB)) for i in range(8)]
        pivots = jnp.ones((8, NB), F32)
        recips, splats, rows = [], [], []
        for i in range(8):
            pivot = columns[i][i : i + 1, :]
            recip = 1.0 / pivot
            recips.append(recip)
            pivots = jnp.where(sub == i, pivot, pivots)
            ratio = jnp.where(sub > i, columns[i] * recip, 0.0)
            splat = {}
            for j in range(i + 1, 8):
                splat[j] = columns[j][i : i + 1, :]
                columns[j] = columns[j] - ratio * splat[j]
            splats.append(splat)
            rows.append((left[i : i + 1, :], right[i : i + 1, :]))
            left = left - ratio * rows[i][0]
            right = right - ratio * rows[i][1]
        at = low + 8
        while at < NB:
            size = min(32 - at % 32, NB - at)
            left_tile = work[at : at + size, :]
            right_tile = inverse[at : at + size, :]
            ratios = []
            for i in range(8):
                value = jnp.broadcast_to(left_tile[:, low + i : low + i + 1], (size, NB))
                for j in range(i):
                    value = value - ratios[j] * splats[j][i]
                ratios.append(value * recips[i])
            for i in range(8):
                left_tile = left_tile - ratios[i] * rows[i][0]
                right_tile = right_tile - ratios[i] * rows[i][1]
            work[at : at + size, :] = left_tile
            inverse[at : at + size, :] = right_tile
            at += size
        inverse[low : low + 8, :] = right * lax.rsqrt(pivots)


def symmetric_part(block):
    return (block + block.T) * 0.5


def factor_block(low, joined, staged, base_work, base_out):
    rows = pl.ds(low, NB)
    high = low + NB
    base_work[...] = joined[rows, rows]
    base_inverse(base_work, base_out)
    base = base_out[...]
    solved = product(base, joined[rows, :], 1, 0)
    lane = lax.broadcasted_iota(jnp.int32, solved.shape, 1)
    upper = jnp.where(lane >= high, solved, 0.0)
    staged[...] = solved
    staged[:, rows] = base
    strip = joined[:, rows]
    joined[:, rows] = jnp.where(lax.broadcasted_iota(jnp.int32, strip.shape, 0) >= high, 0.0, strip)
    joined[...] = joined[...] - product(upper, staged[...], 0, 0)
    joined[rows, :] = jnp.where(lane < high, staged[...], 0.0)


def exchange_kernel(
    counts, rows, slots, early, late, table, own_table, send_a, recv_a, send_b, recv_b, send_s, recv_s,
    front_send, front_recv, front_send_s, front_recv_s, own_send, own_recv, local_sem
):
    panels, fronts = counts
    me = lax.axis_index("panel")
    front = lax.axis_index("front")
    tiles = early.shape[1]
    barrier = pltpu.get_barrier_semaphore()
    for shift in range(1, panels):
        peer = lax.rem(me + shift, panels)
        pl.semaphore_signal(barrier, inc=1, device_id={"panel": peer}, device_id_type=MESH)
    for shift in range(1, fronts):
        peer = lax.rem(front + shift, fronts)
        pl.semaphore_signal(barrier, inc=1, device_id={"front": peer}, device_id_type=MESH)
    pl.semaphore_wait(barrier, panels + fronts - 2)

    def to_panel(source, target, send, recv, shift):
        peer = lax.rem(me + shift, panels)
        return pltpu.make_async_remote_copy(
            src_ref=source(peer),
            dst_ref=target,
            send_sem=send.at[shift],
            recv_sem=recv.at[shift],
            device_id={"panel": peer},
            device_id_type=MESH,
        )

    def early_copy(shift):
        return to_panel(lambda p: rows.at[p, pl.ds(0, tiles)], early.at[front, :, me], send_a, recv_a, shift)

    def slot_copy(shift):
        return to_panel(lambda p: slots.at[p], table.at[front, me], send_s, recv_s, shift)

    def late_copy(shift):
        return to_panel(lambda p: rows.at[p, pl.ds(tiles, late.shape[0])], late.at[:, me], send_b, recv_b, shift)

    lead = own_table.shape[1]

    def own_copy(shift):
        peer = lax.rem(front + shift, fronts)
        return pltpu.make_async_remote_copy(
            src_ref=slots.at[pl.ds(0, lead)],
            dst_ref=own_table.at[front],
            send_sem=own_send.at[shift],
            recv_sem=own_recv.at[shift],
            device_id={"front": peer},
            device_id_type=MESH,
        )

    for shift in range(1, panels):
        slot_copy(shift).start()
        early_copy(shift).start()
    for shift in range(1, fronts):
        own_copy(shift).start()
    own = [
        pltpu.make_async_copy(slots.at[pl.ds(0, lead)], own_table.at[front], local_sem.at[3]),
        pltpu.make_async_copy(rows.at[me, pl.ds(0, tiles)], early.at[front, :, me], local_sem.at[0]),
        pltpu.make_async_copy(slots.at[me], table.at[front, me], local_sem.at[1]),
        pltpu.make_async_copy(rows.at[me, pl.ds(tiles, late.shape[0])], late.at[:, me], local_sem.at[2]),
    ]
    for copy in own:
        copy.start()
    for shift in range(1, panels):
        late_copy(shift).start()
    for copy in own:
        copy.wait()
    for shift in range(1, panels):
        slot_copy(shift).wait_recv()
        early_copy(shift).wait_recv()

    def to_front(array, send, recv, shift):
        peer = lax.rem(front + shift, fronts)
        return pltpu.make_async_remote_copy(
            src_ref=array.at[front],
            dst_ref=array.at[front],
            send_sem=send.at[shift],
            recv_sem=recv.at[shift],
            device_id={"front": peer},
            device_id_type=MESH,
        )

    for shift in range(1, fronts):
        to_front(table, front_send_s, front_recv_s, shift).start()
        to_front(early, front_send, front_recv, shift).start()
    for shift in range(1, panels):
        slot_copy(shift).wait_send()
        early_copy(shift).wait_send()
        late_copy(shift).wait()
    for shift in range(1, fronts):
        to_front(table, front_send_s, front_recv_s, shift).wait()
        to_front(early, front_send, front_recv, shift).wait()
        own_copy(shift).wait()


def exchange_rows(panels, fronts, lead, rows, slots, tiles):
    _, all_tiles, cap, lanes = rows.shape
    sem = pltpu.SemaphoreType.DMA
    return pl.pallas_call(
        lambda *refs: exchange_kernel((panels, fronts), *refs),
        name="exchange",
        out_shape=(
            jax.ShapeDtypeStruct((fronts, tiles, panels, cap, lanes), BF16),
            jax.ShapeDtypeStruct((all_tiles - tiles, panels, cap, lanes), BF16),
            jax.ShapeDtypeStruct((fronts, panels, cap, lanes), jnp.int32),
            jax.ShapeDtypeStruct((fronts, lead, cap, lanes), jnp.int32),
        ),
        in_specs=[pl.BlockSpec(memory_space=pl.ANY)] * 2,
        out_specs=[pl.BlockSpec(memory_space=space) for space in (pltpu.VMEM, pl.ANY, pltpu.VMEM, pltpu.VMEM)],
        scratch_shapes=[sem((panels,))] * 6 + [sem((fronts,))] * 6 + [sem((4,))],
        compiler_params=pltpu.CompilerParams(collective_id=1, has_side_effects=True, vmem_limit_bytes=8 << 20),
    )(rows, slots)


def assemble(parents, table, own_table, early, piv_cols, known, columns, halves, onehot, pick, picked):
    front = lax.axis_index("front")
    fronts, _, each, lanes = early.shape
    owners = [parents[child] == front for child in range(fronts)]

    def masked(ref, size):
        return jnp.concatenate(
            [jnp.where(owners[c], ref[c * size : (c + 1) * size, :], -1) for c in range(fronts)], axis=0
        )

    kept = masked(table, each)
    lane = lax.broadcasted_iota(jnp.int32, kept.shape, 1)
    chosen = jnp.concatenate(
        [(kept == lane + t * lanes).astype(F32) for t in range(known.shape[0] // lanes)], axis=1
    )
    small = chosen.astype(BF16)
    onehot[...] = small
    half = piv_cols.shape[1] // 2
    for h in range(2):
        tiles = half // lanes
        rows = jnp.concatenate(
            [early[:, h * tiles + t].reshape(fronts * each, lanes) for t in range(tiles)], axis=1
        )
        value = piv_cols[:, h * half : (h + 1) * half] + product(small, rows, 0, 0, None)
        columns[:, h * half : (h + 1) * half] = value
        halves[h] = value.astype(BF16)
    found = product(chosen, known[...], 1, 0)
    for child in range(fronts):
        picked[child] = found[child * each : (child + 1) * each, :]
    size = own_table.shape[0] // fronts
    own = masked(own_table, size)
    cap = size * K // piv_cols.shape[1]
    where = lax.rem(lax.broadcasted_iota(jnp.int32, own.shape, 0), size) // cap
    target = jnp.where(own >= 0, own + where * K, -1)
    lane = lax.broadcasted_iota(jnp.int32, own.shape, 1)
    for t in range(pick.shape[1] // lanes):
        pick[:, t * lanes : (t + 1) * lanes] = (target == lane + t * lanes).astype(F32)


def panel_kernel(
    counts, side, parents, table, own_table, early, piv_cols, known, right_side, late,
    blocks, late_all, factor, weights, front_values, child_values, onehot,
    columns, halves, pick, picked,
    inverses, factor10, partial, sums, solved, chosen, chosen_in, from_fronts, onward, inward,
    top, chunk, pieces, staged, base_work, base_out,
    scatter_send, scatter_recv, whole_send, whole_recv, half_send, half_recv,
    far_send, far_recv, farther_send, farther_recv,
    piece_send, piece_recv, sum_send, sum_recv, inward_send, inward_recv,
    late_send, late_recv, over_send, over_recv, pick_send, pick_recv, local_sem,
):
    panels, fronts = counts
    me = lax.axis_index("panel")
    front = lax.axis_index("front")
    across, along = me // side, lax.rem(me, side)
    part = top.shape[1] // panels
    barrier = pltpu.get_barrier_semaphore()
    for shift in range(1, panels):
        peer = lax.rem(me + shift, panels)
        pl.semaphore_signal(barrier, inc=1, device_id={"panel": peer}, device_id_type=MESH)
    for shift in range(1, fronts):
        peer = lax.rem(front + shift, fronts)
        pl.semaphore_signal(barrier, inc=1, device_id={"front": peer}, device_id_type=MESH)
    assemble(parents, table, own_table, early, piv_cols, known, columns, halves, onehot, pick, picked)
    below = me >= 2
    boundary = jnp.where(below, known[...], 0.0)
    width = partial.shape[1]
    for half in range(2):
        value = product(columns[:, half * K : (half + 1) * K], boundary, 0, 0, HIGH)
        for piece in range(panels // 2):
            partial[half * (panels // 2) + piece] = value[piece * width : (piece + 1) * width, :]
    pieces[me] = partial[me]
    pl.semaphore_wait(barrier, panels + fronts - 2)

    def chunk_rows(who):
        return pl.ds(pl.multiple_of(who * part, 8), part)

    def scatter(shift, index):
        peer = lax.rem(me + shift, panels)
        lanes = pl.ds(K if index == 2 else 0, K)
        return pltpu.make_async_remote_copy(
            src_ref=columns.at[chunk_rows(peer), lanes],
            dst_ref=chunk.at[index],
            send_sem=scatter_send.at[index, shift],
            recv_sem=scatter_recv.at[index],
            device_id={"panel": peer},
            device_id_type=MESH,
        )

    def own_chunk(index):
        lanes = pl.ds(K if index == 2 else 0, K)
        return pltpu.make_async_copy(columns.at[chunk_rows(me), lanes], chunk.at[index], local_sem.at[index])

    roots = ((0, (0,)), (1, (1, 2)))
    for root, indices in roots:

        @pl.when(me == root)
        def _():
            for shift in range(1, panels):
                for index in indices:
                    scatter(shift, index).start()
            for index in indices:
                own_chunk(index).start()

    def place(half, first, second):
        first, second = lax.rem(first + side, side), lax.rem(second + side, side)
        return first * side + second if half == 0 else second * side + first

    spots = (across, along), (along, across)

    def view(kind, half, who, rows):
        if kind != 1:
            size = part if rows is None else part // 2
            low = who * part + (part // 2 if rows == 1 else 0)
            return top.at[pl.ds(kind // 2, kind // 2 + 1), pl.ds(pl.multiple_of(low, 8), size), pl.ds(half * (K // 2), K // 2)]
        ref = blocks.at[half, who]
        return ref if rows is None else ref.at[pl.ds(rows * (K // 2), K // 2)]

    def move(kind, half, who, rows, target, send, recv, slot):
        ref = view(kind, half, who, rows)
        return pltpu.make_async_remote_copy(
            src_ref=ref,
            dst_ref=ref,
            send_sem=send.at[slot],
            recv_sem=recv.at[slot],
            device_id={"panel": target},
            device_id_type=MESH,
        )

    def whole(kind, half, way):
        u, v = spots[half]
        step = 1 if way == 0 else -1
        copy = move(kind, half, me, None, place(half, u + step, v), whole_send, whole_recv, (kind, half, way))
        return kind, copy, me, place(half, u - step, v)

    def halved(kind, half, way):
        u, v = spots[half]
        step = 1 if way == 0 else -1
        who = place(half, u - step, v)
        copy = move(kind, half, who, way, place(half, u + step, v), half_send, half_recv, (kind, half, way))
        return kind, copy, who, place(half, u + 2, v)

    def far(kind, half, offset, way):
        u, v = spots[half]
        step = 1 if way == 0 else -1
        who = place(half, u + offset, v)
        copy = move(kind, half, who, None, place(half, u, v + step), far_send, far_recv, (kind, half, offset, way))
        return kind, copy, who, place(half, u + offset, v - step)

    def farther(kind, half, offset, way):
        u, v = spots[half]
        step = 1 if way == 0 else -1
        who = place(half, u + offset, v - step)
        copy = move(
            kind, half, who, way, place(half, u, v + step), farther_send, farther_recv, (kind, half, offset, way)
        )
        return kind, copy, who, place(half, u + offset, v + 2)

    def guarded(kind, who, act):
        if kind != 1:
            act()
        else:
            pl.when(who >= 2)(act)

    def start(hop):
        guarded(hop[0], hop[2], hop[1].start)

    def sent(hop):
        guarded(hop[0], hop[2], hop[1].wait_send)

    def arrived(hop):
        guarded(hop[0], hop[3], hop[1].wait_recv)

    both = [(half, way) for half in range(2) for way in range(2)]

    def near(kind):
        for half, way in both:
            start(whole(kind, half, way))

    def own_far(kind):
        for half, way in both:
            start(far(kind, half, 0, way))

    def second(kind):
        for half, way in both:
            arrived(whole(kind, half, way))
            start(halved(kind, half, way))
        for half, way in both:
            start(far(kind, half, 1, way))
            start(far(kind, half, 3, way))

    def third(kind):
        for half in range(2):
            for way in range(2):
                arrived(halved(kind, half, way))
            for way in range(2):
                start(far(kind, half, 2, way))

    def relay(kind, offset):
        for half, way in both:
            arrived(far(kind, half, offset, way))
            start(farther(kind, half, offset, way))

    def finish(kind):
        for half, way in both:
            for offset in range(4):
                arrived(farther(kind, half, offset, way))

    def drain(kind):
        for half, way in both:
            sent(whole(kind, half, way))
            sent(halved(kind, half, way))
            for offset in range(4):
                sent(far(kind, half, offset, way))
                sent(farther(kind, half, offset, way))

    def over_copy(shift):
        peer = lax.rem(front + shift, fronts)
        return pltpu.make_async_remote_copy(
            src_ref=picked.at[peer],
            dst_ref=from_fronts.at[front],
            send_sem=over_send.at[shift],
            recv_sem=over_recv.at[shift],
            device_id={"front": peer},
            device_id_type=MESH,
        )

    def inward_copy(shift):
        peer = lax.rem(me + shift, panels)
        return pltpu.make_async_remote_copy(
            src_ref=onward.at[peer],
            dst_ref=inward.at[me],
            send_sem=inward_send.at[shift],
            recv_sem=inward_recv.at[shift],
            device_id={"panel": peer},
            device_id_type=MESH,
        )

    def pick_copy(shift):
        peer = lax.rem(front + shift, fronts)
        return pltpu.make_async_remote_copy(
            src_ref=chosen.at[peer],
            dst_ref=chosen_in.at[front],
            send_sem=pick_send.at[shift],
            recv_sem=pick_recv.at[shift],
            device_id={"front": peer},
            device_id_type=MESH,
        )

    def late_copy(shift):
        peer = lax.rem(front + shift, fronts)
        return pltpu.make_async_remote_copy(
            src_ref=late,
            dst_ref=late_all.at[front],
            send_sem=late_send.at[shift],
            recv_sem=late_recv.at[shift],
            device_id={"front": peer},
            device_id_type=MESH,
        )

    def piece_copy(shift):
        peer = lax.rem(me + shift, panels)
        return pltpu.make_async_remote_copy(
            src_ref=partial.at[peer],
            dst_ref=pieces.at[me],
            send_sem=piece_send.at[shift],
            recv_sem=piece_recv.at[shift],
            device_id={"panel": peer},
            device_id_type=MESH,
        )

    def sum_copy(shift):
        peer = lax.rem(me + shift, panels)
        return pltpu.make_async_remote_copy(
            src_ref=sums.at[me],
            dst_ref=sums.at[me],
            send_sem=sum_send.at[shift],
            recv_sem=sum_recv.at[shift],
            device_id={"panel": peer},
            device_id_type=MESH,
        )

    own = [
        pltpu.make_async_copy(halves, blocks.at[:, me], local_sem.at[3]),
        pltpu.make_async_copy(picked.at[front], from_fronts.at[front], local_sem.at[4]),
        pltpu.make_async_copy(late, late_all.at[front], local_sem.at[5]),
    ]
    for copy in own:
        copy.start()
    for shift in range(1, fronts):
        over_copy(shift).start()
    for copy in own:
        copy.wait()
    for shift in range(1, fronts):
        late_copy(shift).start()
    for shift in range(1, panels):
        piece_copy(shift).start()

    def own_rows(root, index):

        @pl.when(me == root)
        def _():
            own_chunk(index).wait()

        @pl.when(me != root)
        def _():
            scatter(1, index).wait_recv()

        top[index, chunk_rows(me), :] = chunk[index]

    own_rows(0, 0)
    near(0)
    own_far(0)
    own_rows(1, 1)
    own_rows(1, 2)
    second(0)
    third(0)
    for offset in (0, 1, 3, 2):
        relay(0, offset)
    near(2)
    own_far(2)
    near(1)
    finish(0)

    def block_step(index, carry):
        which = index // (K // NB)

        @pl.when(index == 0)
        def _():
            inverses[0] = symmetric_part(top[0])

        @pl.when(index == K // NB)
        def _():
            finish(2)
            lower = product(top[1], inverses[0], 1, 1)
            factor10[...] = lower
            packed = lower.astype(BF16)
            inverses[1] = symmetric_part(top[2] - product(packed, packed, 1, 1, None))

        low = pl.multiple_of((index - which * (K // NB)) * NB, NB)
        factor_block(low, inverses.at[which], staged, base_work, base_out)

        @pl.when(index == 0)
        def _():
            second(2)

        @pl.when(index == 2)
        def _():
            third(2)
            for offset in (0, 1):
                relay(2, offset)
            second(1)
            own_far(1)

        @pl.when(index == 3)
        def _():
            relay(2, 3)
            relay(2, 2)
            for shift in range(1, fronts):
                over_copy(shift).wait_recv()
            total = from_fronts[0]
            for who in range(1, fronts):
                total = total + from_fronts[who]
            cap = onward.shape[1]
            for who in range(panels):
                onward[who] = total[who * cap : (who + 1) * cap, :]
            for shift in range(1, panels):
                inward_copy(shift).start()

        @pl.when(index == 4)
        def _():
            third(1)
            for shift in range(1, panels):
                piece_copy(shift).wait_recv()
            total = pieces[0]
            for who in range(1, panels):
                total = total + pieces[who]
            sums[me] = total
            for shift in range(1, panels):
                sum_copy(shift).start()

        @pl.when(index == 6)
        def _():
            relay(1, 0)

        return carry

    lax.fori_loop(0, 2 * (K // NB), block_step, 0)

    for shift in range(1, panels):
        sum_copy(shift).wait_recv()
    inverse0, inverse1, lower = inverses[0], inverses[1], factor10[...]
    count = panels // 2
    sums0 = jnp.concatenate([sums[piece] for piece in range(count)], axis=0)
    sums1 = jnp.concatenate([sums[count + piece] for piece in range(count)], axis=0)
    carried0 = product(inverse0, sums0, 1, 0, HIGH)
    carried1 = product(inverse1, sums1 - product(lower, carried0, 1, 0, HIGH), 1, 0, HIGH)
    solved1 = product(inverse1, right_side[K:, :] - carried1, 0, 0, HIGH)
    solved0 = product(inverse0, right_side[0:K, :] - carried0 - product(lower, solved1, 0, 0, HIGH), 0, 0, HIGH)
    solved[0:K, :] = solved0
    solved[K:, :] = solved1
    values = product(pick[...], solved[...], 1, 0)
    size = chosen.shape[1]
    for child in range(fronts):
        chosen[child] = values[child * size : (child + 1) * size, :]
    for shift in range(1, fronts):
        pick_copy(shift).start()
    chosen_in[front] = chosen[front]
    front_values[...] = jnp.where(below, known[...], jnp.where(me == 0, solved0, solved1))

    relay(1, 1)
    factor0 = product(columns[:, 0:K], inverse0, 1, 1, HIGH)
    current = columns[:, K:] - product(factor0.astype(BF16), lower.astype(BF16), 1, 1, None)
    factor1 = jnp.where(me >= 1, product(current, inverse1, 1, 1, HIGH), 0.0)
    factor[:, 0:K] = factor0
    factor[:, K:] = factor1
    relay(1, 3)
    weight1 = product(factor1, inverse1, 1, 0, HIGH)
    weight0 = product(factor0 - product(weight1, lower, 1, 0, HIGH), inverse0, 1, 0, HIGH)
    weights[0] = weight0.astype(BF16)
    weights[1] = weight1.astype(BF16)
    relay(1, 2)

    for shift in range(1, panels):
        inward_copy(shift).wait_recv()
    child_values[...] = inward[...]
    child_values[me] = onward[me]
    for shift in range(1, fronts):
        pick_copy(shift).wait_recv()
    total = chosen_in[0]
    for who in range(1, fronts):
        total = total + chosen_in[who]
    cap = child_values.shape[1]
    for lead in range(size // cap):
        child_values[lead] = total[lead * cap : (lead + 1) * cap, :]
    finish(1)
    for kind in range(3):
        drain(kind)
    for shift in range(1, panels):
        piece_copy(shift).wait_send()
        sum_copy(shift).wait_send()
        inward_copy(shift).wait_send()
    for shift in range(1, fronts):
        over_copy(shift).wait_send()
        pick_copy(shift).wait_send()
    for shift in range(1, fronts):
        late_copy(shift).wait()
    for root, indices in roots:

        @pl.when(me == root)
        def _():
            for shift in range(1, panels):
                for index in indices:
                    scatter(shift, index).wait_send()


def panel_step(sizes, parents, table, own_table, early, piv_cols, known, right_side, late):
    panels, fronts, side = sizes
    sem = pltpu.SemaphoreType.DMA
    part = K // panels
    rows, pivots = piv_cols.shape
    rhs = known.shape[1]
    cap = early.shape[2] // panels
    anywhere = pl.BlockSpec(memory_space=pl.ANY)
    vmem = pl.BlockSpec(memory_space=pltpu.VMEM)
    wide = pltpu.VMEM((panels, pivots // panels, rhs), F32)
    few = pltpu.VMEM((fronts, own_table.shape[0] // fronts, rhs), F32)
    over = pltpu.VMEM((fronts, panels * cap, rhs), F32)
    slot = pltpu.VMEM((panels, cap, rhs), F32)
    square = pltpu.VMEM((K, K), F32)
    tile = pltpu.VMEM((NB, NB), F32)
    return pl.pallas_call(
        lambda *refs: panel_kernel((panels, fronts), side, *refs),
        name="panel_step",
        out_shape=(
            jax.ShapeDtypeStruct((2, panels, K, K), BF16),
            jax.ShapeDtypeStruct((fronts,) + late.shape, BF16),
            jax.ShapeDtypeStruct((rows, pivots), F32),
            jax.ShapeDtypeStruct((2, K, K), BF16),
            jax.ShapeDtypeStruct((rows, rhs), F32),
            jax.ShapeDtypeStruct((panels, cap, rhs), F32),
            jax.ShapeDtypeStruct((table.shape[0], rows), BF16),
        ),
        in_specs=[pl.BlockSpec(memory_space=pltpu.SMEM)] + [vmem] * 6 + [anywhere],
        out_specs=[anywhere] * 2 + [vmem] * 5,
        scratch_shapes=[
            pltpu.VMEM((rows, pivots), F32),
            pltpu.VMEM((2, rows, K), BF16),
            pltpu.VMEM((own_table.shape[0], pivots), F32),
            over,
            pltpu.VMEM((2, K, K), F32),
            square,
            wide,
            wide,
            pltpu.VMEM((pivots, rhs), F32),
            few,
            few,
            over,
            slot,
            slot,
            pltpu.VMEM((3, K, K), F32),
            pltpu.VMEM((3, part, K), F32),
            wide,
            pltpu.VMEM((NB, K), F32),
            tile,
            tile,
            sem((3, panels)),
            sem((3,)),
        ]
        + [sem((3, 2, 2))] * 4
        + [sem((3, 2, 4, 2))] * 4
        + [sem((panels,))] * 6
        + [sem((fronts,))] * 6
        + [sem((6,))],
        compiler_params=pltpu.CompilerParams(
            collective_id=2, has_side_effects=True, vmem_limit_bytes=40 << 20
        ),
    )(parents, table, own_table, early, piv_cols, known, right_side, late)


def update_kernel(late, blocks, weights, onehot, factor, front_values, child_values, update, *rest):
    outs, sem = rest[:3], rest[3]
    step = pl.program_id(0)
    results = (factor, front_values, child_values)

    @pl.when(step == 0)
    def _():
        for i in range(3):
            pltpu.make_async_copy(results[i], outs[i], sem.at[i]).start()

    fronts, tiles, each, lanes = late.shape
    rows = jnp.concatenate([late[:, t].reshape(fronts * each, lanes) for t in range(tiles)], axis=1)
    value = product(onehot[...], rows, 0, 0, None)
    for half in range(2):
        value = value - product(weights[half], blocks[half, 0], 1, 1, None)
    update[...] = jnp.where(lax.axis_index("panel") >= 2, value, 0.0).astype(BF16)

    @pl.when(step == pl.num_programs(0) - 1)
    def _():
        for i in range(3):
            pltpu.make_async_copy(results[i], outs[i], sem.at[i]).wait()


def update_step(late_all, blocks, weights, onehot, factor, front_values, child_values):
    fronts, all_tiles, each, lanes = late_all.shape
    tiles = K // lanes
    steps = all_tiles // tiles
    first = blocks.shape[1] - steps
    rows = weights.shape[1]
    anywhere = pl.BlockSpec(memory_space=pl.ANY)
    fixed = pl.BlockSpec(memory_space=pltpu.VMEM)
    like = [jax.ShapeDtypeStruct(x.shape, x.dtype) for x in (factor, front_values, child_values)]
    return pl.pallas_call(
        update_kernel,
        name="update",
        grid=(steps,),
        out_shape=[jax.ShapeDtypeStruct((rows, steps * K), BF16)] + like,
        in_specs=[
            pl.BlockSpec((fronts, tiles, each, lanes), lambda j: (0, j, 0, 0)),
            pl.BlockSpec((2, 1, K, K), lambda j: (0, j + first, 0, 0)),
            fixed,
            fixed,
            anywhere,
            anywhere,
            anywhere,
        ],
        out_specs=[pl.BlockSpec((rows, K), lambda j: (0, j))] + [anywhere] * 3,
        scratch_shapes=[pltpu.SemaphoreType.DMA((3,))],
        compiler_params=pltpu.CompilerParams(vmem_limit_bytes=56 << 20),
    )(late_all, blocks, weights, onehot, factor, front_values, child_values)


def on_device(sizes, pivot_columns, child_rows, slot_rows, parents, pivot_rhs, boundary_solution):
    panels, fronts, _ = sizes
    piv_cols = pivot_columns[0]
    pivots = piv_cols.shape[1]
    rows_out = child_rows[0, 0]
    cap, width = rows_out.shape[1:]
    lanes = NB
    lead = pivots // K
    each = panels * cap
    known = boundary_solution[0]

    rows_tiled = rows_out.reshape(panels, cap, width // lanes, lanes).transpose(0, 2, 1, 3)
    slots_wide = jnp.broadcast_to(slot_rows[0, 0][:, :, None], (panels, cap, lanes))
    early, late, table, own_table = exchange_rows(panels, fronts, lead, rows_tiled, slots_wide, pivots // lanes)
    blocks, late_all, factor, weights, front_values, child_values, onehot = panel_step(
        sizes,
        parents,
        table.reshape(fronts * each, lanes),
        own_table.reshape(fronts * lead * cap, lanes),
        early.reshape(fronts, pivots // lanes, each, lanes),
        piv_cols,
        known,
        pivot_rhs[0],
        late,
    )
    update_matrix, factor, front_values, child_values = update_step(
        late_all.reshape(fronts, -1, each, lanes), blocks, weights, onehot, factor, front_values, child_values
    )
    return (factor[None], update_matrix[None], front_values[None], child_values[None, None])


def solution(mesh):
    in_specs = (
        P("front", "panel", None),
        P("front", "panel", None, None, None),
        P("front", "panel", None, None),
        P(),
        P("front", None, None),
        P("front", "panel", None),
    )
    out_specs = (
        P("front", "panel", None),
        P("front", "panel", None),
        P("front", "panel", None),
        P("front", "panel", None, None, None),
    )
    panels, fronts = mesh.shape["panel"], mesh.shape["front"]
    sizes = (panels, fronts, math.isqrt(panels))
    return jax.shard_map(
        lambda *arrays: on_device(sizes, *arrays),
        mesh=mesh,
        in_specs=in_specs,
        out_specs=out_specs,
        check_vma=False,
    )
```

```python
import math

import jax
import jax.numpy as jnp
from jax import lax
from jax.experimental import pallas as pl
from jax.experimental.pallas import tpu as pltpu
from jax.sharding import PartitionSpec as P

K = 512
NB = 128
PIV = 1024
HIGHEST = lax.Precision.HIGHEST
HIGH = lax.Precision.HIGH
MESH = pl.DeviceIdType.MESH
F32 = jnp.float32
BF16 = jnp.bfloat16


def product(left, right, left_dim, right_dim, precision=HIGHEST):
    dims = (((left_dim,), (right_dim,)), ((), ()))
    return lax.dot_general(left, right, dims, precision=precision, preferred_element_type=F32)


def base_inverse(work, inverse):
    sub = lax.broadcasted_iota(jnp.int32, (8, NB), 0)
    lane = lax.broadcasted_iota(jnp.int32, (NB, NB), 1)
    row = lax.broadcasted_iota(jnp.int32, (NB, NB), 0)
    inverse[...] = (lane == row).astype(F32)
    for step in range(NB // 8):
        low = 8 * step
        left = work[low : low + 8, :]
        right = inverse[low : low + 8, :]
        columns = [jnp.broadcast_to(left[:, low + i : low + i + 1], (8, NB)) for i in range(8)]
        pivots = jnp.ones((8, NB), F32)
        recips, splats, rows = [], [], []
        for i in range(8):
            pivot = columns[i][i : i + 1, :]
            recip = 1.0 / pivot
            recips.append(recip)
            pivots = jnp.where(sub == i, pivot, pivots)
            ratio = jnp.where(sub > i, columns[i] * recip, 0.0)
            splat = {}
            for j in range(i + 1, 8):
                splat[j] = columns[j][i : i + 1, :]
                columns[j] = columns[j] - ratio * splat[j]
            splats.append(splat)
            rows.append((left[i : i + 1, :], right[i : i + 1, :]))
            left = left - ratio * rows[i][0]
            right = right - ratio * rows[i][1]
        at = low + 8
        while at < NB:
            size = min(32 - at % 32, NB - at)
            left_tile = work[at : at + size, :]
            right_tile = inverse[at : at + size, :]
            ratios = []
            for i in range(8):
                value = jnp.broadcast_to(left_tile[:, low + i : low + i + 1], (size, NB))
                for j in range(i):
                    value = value - ratios[j] * splats[j][i]
                ratios.append(value * recips[i])
            for i in range(8):
                left_tile = left_tile - ratios[i] * rows[i][0]
                right_tile = right_tile - ratios[i] * rows[i][1]
            work[at : at + size, :] = left_tile
            inverse[at : at + size, :] = right_tile
            at += size
        inverse[low : low + 8, :] = right * lax.rsqrt(pivots)


def symmetric_part(block):
    return (block + block.T) * 0.5


def factor_block(low, joined, staged, base_work, base_out):
    rows = pl.ds(low, NB)
    high = low + NB
    base_work[...] = joined[rows, rows]
    base_inverse(base_work, base_out)
    base = base_out[...]
    solved = product(base, joined[rows, :], 1, 0)
    lane = lax.broadcasted_iota(jnp.int32, solved.shape, 1)
    upper = jnp.where(lane >= high, solved, 0.0)
    staged[...] = solved
    staged[:, rows] = base
    strip = joined[:, rows]
    joined[:, rows] = jnp.where(lax.broadcasted_iota(jnp.int32, strip.shape, 0) >= high, 0.0, strip)
    joined[...] = joined[...] - product(upper, staged[...], 0, 0)
    joined[rows, :] = jnp.where(lane < high, staged[...], 0.0)


def exchange_kernel(
    counts, rows, slots, early, late, table, own_table, send_a, recv_a, send_b, recv_b, send_s, recv_s,
    front_send, front_recv, front_send_s, front_recv_s, own_send, own_recv, local_sem
):
    panels, fronts = counts
    me = lax.axis_index("panel")
    front = lax.axis_index("front")
    tiles = early.shape[1]
    barrier = pltpu.get_barrier_semaphore()
    for shift in range(1, panels):
        peer = lax.rem(me + shift, panels)
        pl.semaphore_signal(barrier, inc=1, device_id={"panel": peer}, device_id_type=MESH)
    for shift in range(1, fronts):
        peer = lax.rem(front + shift, fronts)
        pl.semaphore_signal(barrier, inc=1, device_id={"front": peer}, device_id_type=MESH)
    pl.semaphore_wait(barrier, panels + fronts - 2)

    def to_panel(source, target, send, recv, shift):
        peer = lax.rem(me + shift, panels)
        return pltpu.make_async_remote_copy(
            src_ref=source(peer),
            dst_ref=target,
            send_sem=send.at[shift],
            recv_sem=recv.at[shift],
            device_id={"panel": peer},
            device_id_type=MESH,
        )

    def early_copy(shift):
        return to_panel(lambda p: rows.at[p, pl.ds(0, tiles)], early.at[front, :, me], send_a, recv_a, shift)

    def slot_copy(shift):
        return to_panel(lambda p: slots.at[p], table.at[front, me], send_s, recv_s, shift)

    def late_copy(shift):
        return to_panel(lambda p: rows.at[p, pl.ds(tiles, late.shape[0])], late.at[:, me], send_b, recv_b, shift)

    lead = own_table.shape[1]

    def own_copy(shift):
        peer = lax.rem(front + shift, fronts)
        return pltpu.make_async_remote_copy(
            src_ref=slots.at[pl.ds(0, lead)],
            dst_ref=own_table.at[front],
            send_sem=own_send.at[shift],
            recv_sem=own_recv.at[shift],
            device_id={"front": peer},
            device_id_type=MESH,
        )

    for shift in range(1, panels):
        slot_copy(shift).start()
        early_copy(shift).start()
    for shift in range(1, fronts):
        own_copy(shift).start()
    own = [
        pltpu.make_async_copy(slots.at[pl.ds(0, lead)], own_table.at[front], local_sem.at[3]),
        pltpu.make_async_copy(rows.at[me, pl.ds(0, tiles)], early.at[front, :, me], local_sem.at[0]),
        pltpu.make_async_copy(slots.at[me], table.at[front, me], local_sem.at[1]),
        pltpu.make_async_copy(rows.at[me, pl.ds(tiles, late.shape[0])], late.at[:, me], local_sem.at[2]),
    ]
    for copy in own:
        copy.start()
    for shift in range(1, panels):
        late_copy(shift).start()
    for copy in own:
        copy.wait()
    for shift in range(1, panels):
        slot_copy(shift).wait_recv()
        early_copy(shift).wait_recv()

    def to_front(array, send, recv, shift):
        peer = lax.rem(front + shift, fronts)
        return pltpu.make_async_remote_copy(
            src_ref=array.at[front],
            dst_ref=array.at[front],
            send_sem=send.at[shift],
            recv_sem=recv.at[shift],
            device_id={"front": peer},
            device_id_type=MESH,
        )

    for shift in range(1, fronts):
        to_front(table, front_send_s, front_recv_s, shift).start()
        to_front(early, front_send, front_recv, shift).start()
    for shift in range(1, panels):
        slot_copy(shift).wait_send()
        early_copy(shift).wait_send()
        late_copy(shift).wait()
    for shift in range(1, fronts):
        to_front(table, front_send_s, front_recv_s, shift).wait()
        to_front(early, front_send, front_recv, shift).wait()
        own_copy(shift).wait()


def exchange_rows(panels, fronts, lead, rows, slots, tiles):
    _, all_tiles, cap, lanes = rows.shape
    sem = pltpu.SemaphoreType.DMA
    return pl.pallas_call(
        lambda *refs: exchange_kernel((panels, fronts), *refs),
        name="exchange",
        out_shape=(
            jax.ShapeDtypeStruct((fronts, tiles, panels, cap, lanes), BF16),
            jax.ShapeDtypeStruct((all_tiles - tiles, panels, cap, lanes), BF16),
            jax.ShapeDtypeStruct((fronts, panels, cap, lanes), jnp.int32),
            jax.ShapeDtypeStruct((fronts, lead, cap, lanes), jnp.int32),
        ),
        in_specs=[pl.BlockSpec(memory_space=pl.ANY)] * 2,
        out_specs=[pl.BlockSpec(memory_space=space) for space in (pltpu.VMEM, pl.ANY, pltpu.VMEM, pltpu.VMEM)],
        scratch_shapes=[sem((panels,))] * 6 + [sem((fronts,))] * 6 + [sem((4,))],
        compiler_params=pltpu.CompilerParams(collective_id=1, has_side_effects=True, vmem_limit_bytes=8 << 20),
    )(rows, slots)


def assemble(parents, table, own_table, early, piv_cols, known, columns, halves, onehot, pick, picked):
    front = lax.axis_index("front")
    fronts, _, each, lanes = early.shape
    owners = [parents[child] == front for child in range(fronts)]

    def masked(ref, size):
        return jnp.concatenate(
            [jnp.where(owners[c], ref[c * size : (c + 1) * size, :], -1) for c in range(fronts)], axis=0
        )

    kept = masked(table, each)
    lane = lax.broadcasted_iota(jnp.int32, kept.shape, 1)
    chosen = jnp.concatenate(
        [(kept == lane + t * lanes).astype(F32) for t in range(known.shape[0] // lanes)], axis=1
    )
    small = chosen.astype(BF16)
    onehot[...] = small
    half = piv_cols.shape[1] // 2
    for h in range(2):
        tiles = half // lanes
        rows = jnp.concatenate(
            [early[:, h * tiles + t].reshape(fronts * each, lanes) for t in range(tiles)], axis=1
        )
        value = piv_cols[:, h * half : (h + 1) * half] + product(small, rows, 0, 0, None)
        columns[:, h * half : (h + 1) * half] = value
        halves[h] = value.astype(BF16)
    found = product(chosen, known[...], 1, 0)
    for child in range(fronts):
        picked[child] = found[child * each : (child + 1) * each, :]
    size = own_table.shape[0] // fronts
    own = masked(own_table, size)
    cap = size * K // piv_cols.shape[1]
    where = lax.rem(lax.broadcasted_iota(jnp.int32, own.shape, 0), size) // cap
    target = jnp.where(own >= 0, own + where * K, -1)
    lane = lax.broadcasted_iota(jnp.int32, own.shape, 1)
    for t in range(pick.shape[1] // lanes):
        pick[:, t * lanes : (t + 1) * lanes] = (target == lane + t * lanes).astype(F32)


def panel_kernel(
    counts, side, parents, table, own_table, early, piv_cols, known, right_side, late,
    blocks, late_all, factor, weights, front_values, child_values, onehot,
    columns, halves, pick, picked,
    inverses, factor10, partial, sums, solved, chosen, chosen_in, from_fronts, onward, inward,
    top, chunk, pieces, staged, base_work, base_out,
    scatter_send, scatter_recv, whole_send, whole_recv, half_send, half_recv,
    far_send, far_recv, farther_send, farther_recv,
    piece_send, piece_recv, sum_send, sum_recv, inward_send, inward_recv,
    late_send, late_recv, over_send, over_recv, pick_send, pick_recv, local_sem,
):
    panels, fronts = counts
    me = lax.axis_index("panel")
    front = lax.axis_index("front")
    across, along = me // side, lax.rem(me, side)
    part = top.shape[1] // panels
    barrier = pltpu.get_barrier_semaphore()
    for shift in range(1, panels):
        peer = lax.rem(me + shift, panels)
        pl.semaphore_signal(barrier, inc=1, device_id={"panel": peer}, device_id_type=MESH)
    for shift in range(1, fronts):
        peer = lax.rem(front + shift, fronts)
        pl.semaphore_signal(barrier, inc=1, device_id={"front": peer}, device_id_type=MESH)
    assemble(parents, table, own_table, early, piv_cols, known, columns, halves, onehot, pick, picked)
    below = me >= 2
    boundary = jnp.where(below, known[...], 0.0)
    width = partial.shape[1]
    for half in range(2):
        value = product(columns[:, half * K : (half + 1) * K], boundary, 0, 0, HIGH)
        for piece in range(panels // 2):
            partial[half * (panels // 2) + piece] = value[piece * width : (piece + 1) * width, :]
    pieces[me] = partial[me]
    pl.semaphore_wait(barrier, panels + fronts - 2)

    def chunk_rows(who):
        return pl.ds(pl.multiple_of(who * part, 8), part)

    def scatter(shift, index):
        peer = lax.rem(me + shift, panels)
        lanes = pl.ds(K if index == 2 else 0, K)
        return pltpu.make_async_remote_copy(
            src_ref=columns.at[chunk_rows(peer), lanes],
            dst_ref=chunk.at[index],
            send_sem=scatter_send.at[index, shift],
            recv_sem=scatter_recv.at[index],
            device_id={"panel": peer},
            device_id_type=MESH,
        )

    def own_chunk(index):
        lanes = pl.ds(K if index == 2 else 0, K)
        return pltpu.make_async_copy(columns.at[chunk_rows(me), lanes], chunk.at[index], local_sem.at[index])

    roots = ((0, (0,)), (1, (1, 2)))
    for root, indices in roots:

        @pl.when(me == root)
        def _():
            for shift in range(1, panels):
                for index in indices:
                    scatter(shift, index).start()
            for index in indices:
                own_chunk(index).start()

    coords = [[lax.rem(at + step, side) for step in range(side)] for at in (across, along)]

    def place(half, first, second):
        near_axis, far_axis = (coords[0], coords[1]) if half == 0 else (coords[1], coords[0])
        first, second = near_axis[first % side], far_axis[second % side]
        return first * side + second if half == 0 else second * side + first

    def view(kind, half, who, rows):
        if kind == 0:
            size = part if rows is None else part // 2
            low = who * part + (part // 2 if rows == 1 else 0)
            return top.at[:, pl.ds(pl.multiple_of(low, 8), size), pl.ds(half * (K // 2), K // 2)]
        ref = blocks.at[half, who]
        return ref if rows is None else ref.at[pl.ds(rows * (K // 2), K // 2)]

    def move(kind, half, who, rows, target, send, recv, slot):
        ref = view(kind, half, who, rows)
        return pltpu.make_async_remote_copy(
            src_ref=ref,
            dst_ref=ref,
            send_sem=send.at[slot],
            recv_sem=recv.at[slot],
            device_id={"panel": target},
            device_id_type=MESH,
        )

    def whole(kind, half, way):
        step = 1 if way == 0 else -1
        copy = move(kind, half, me, None, place(half, step, 0), whole_send, whole_recv, (kind, half, way))
        return kind, copy, me, place(half, -step, 0)

    def halved(kind, half, way):
        step = 1 if way == 0 else -1
        who = place(half, -step, 0)
        copy = move(kind, half, who, way, place(half, step, 0), half_send, half_recv, (kind, half, way))
        return kind, copy, who, place(half, 2, 0)

    def far(kind, half, offset, way):
        step = 1 if way == 0 else -1
        who = place(half, offset, 0)
        copy = move(kind, half, who, None, place(half, 0, step), far_send, far_recv, (kind, half, offset, way))
        return kind, copy, who, place(half, offset, -step)

    def farther(kind, half, offset, way):
        step = 1 if way == 0 else -1
        who = place(half, offset, -step)
        copy = move(
            kind, half, who, way, place(half, 0, step), farther_send, farther_recv, (kind, half, offset, way)
        )
        return kind, copy, who, place(half, offset, 2)

    def guarded(kind, who, act):
        if kind == 0:
            act()
        else:
            pl.when(who >= 2)(act)

    def start(hop):
        guarded(hop[0], hop[2], hop[1].start)

    def sent(hop):
        guarded(hop[0], hop[2], hop[1].wait_send)

    def arrived(hop):
        guarded(hop[0], hop[3], hop[1].wait_recv)

    both = [(half, way) for half in range(2) for way in range(2)]

    def near(kind):
        for half, way in both:
            start(whole(kind, half, way))

    def own_far(kind):
        for half, way in both:
            start(far(kind, half, 0, way))

    def halves_on(kind):
        for half, way in both:
            arrived(whole(kind, half, way))
            start(halved(kind, half, way))

    def far_on(kind, offset):
        for half, way in both:
            start(far(kind, half, offset, way))

    def last_far_on(kind):
        for half in range(2):
            for way in range(2):
                arrived(halved(kind, half, way))
            for way in range(2):
                start(far(kind, half, 2, way))

    def relay(kind, offset):
        for half, way in both:
            arrived(far(kind, half, offset, way))
            start(farther(kind, half, offset, way))

    def finish(kind):
        for half, way in both:
            for offset in range(4):
                arrived(farther(kind, half, offset, way))

    def drain(kind):
        for half, way in both:
            sent(whole(kind, half, way))
            sent(halved(kind, half, way))
            for offset in range(4):
                sent(far(kind, half, offset, way))
                sent(farther(kind, half, offset, way))

    def over_copy(shift):
        peer = lax.rem(front + shift, fronts)
        return pltpu.make_async_remote_copy(
            src_ref=picked.at[peer],
            dst_ref=from_fronts.at[front],
            send_sem=over_send.at[shift],
            recv_sem=over_recv.at[shift],
            device_id={"front": peer},
            device_id_type=MESH,
        )

    def inward_copy(shift):
        peer = lax.rem(me + shift, panels)
        return pltpu.make_async_remote_copy(
            src_ref=onward.at[peer],
            dst_ref=inward.at[me],
            send_sem=inward_send.at[shift],
            recv_sem=inward_recv.at[shift],
            device_id={"panel": peer},
            device_id_type=MESH,
        )

    def pick_copy(shift):
        peer = lax.rem(front + shift, fronts)
        return pltpu.make_async_remote_copy(
            src_ref=chosen.at[peer],
            dst_ref=chosen_in.at[front],
            send_sem=pick_send.at[shift],
            recv_sem=pick_recv.at[shift],
            device_id={"front": peer},
            device_id_type=MESH,
        )

    def late_copy(shift):
        peer = lax.rem(front + shift, fronts)
        return pltpu.make_async_remote_copy(
            src_ref=late,
            dst_ref=late_all.at[front],
            send_sem=late_send.at[shift],
            recv_sem=late_recv.at[shift],
            device_id={"front": peer},
            device_id_type=MESH,
        )

    def piece_copy(shift):
        peer = lax.rem(me + shift, panels)
        return pltpu.make_async_remote_copy(
            src_ref=partial.at[peer],
            dst_ref=pieces.at[me],
            send_sem=piece_send.at[shift],
            recv_sem=piece_recv.at[shift],
            device_id={"panel": peer},
            device_id_type=MESH,
        )

    def sum_copy(shift):
        peer = lax.rem(me + shift, panels)
        return pltpu.make_async_remote_copy(
            src_ref=sums.at[me],
            dst_ref=sums.at[me],
            send_sem=sum_send.at[shift],
            recv_sem=sum_recv.at[shift],
            device_id={"panel": peer},
            device_id_type=MESH,
        )

    own = [
        pltpu.make_async_copy(halves, blocks.at[:, me], local_sem.at[3]),
        pltpu.make_async_copy(picked.at[front], from_fronts.at[front], local_sem.at[4]),
    ]
    own_late = pltpu.make_async_copy(late, late_all.at[front], local_sem.at[5])
    for copy in own:
        copy.start()
    own_late.start()
    for shift in range(1, fronts):
        over_copy(shift).start()
    for copy in own:
        copy.wait()
    near(1)
    own_far(1)
    for shift in range(1, fronts):
        late_copy(shift).start()

    def own_rows(root, index):

        @pl.when(me == root)
        def _():
            own_chunk(index).wait()

        @pl.when(me != root)
        def _():
            scatter(1, index).wait_recv()

        top[index, chunk_rows(me), :] = chunk[index]

    own_rows(0, 0)
    own_rows(1, 1)
    own_rows(1, 2)
    near(0)
    own_far(0)
    for shift in range(1, panels):
        piece_copy(shift).start()
    halves_on(1)
    halves_on(0)
    far_on(0, 1)
    far_on(0, 3)
    far_on(1, 1)
    last_far_on(0)
    for offset in (0, 1, 3, 2):
        relay(0, offset)
    far_on(1, 3)
    last_far_on(1)
    relay(1, 0)
    finish(0)

    def block_step(index, carry):
        which = index // (K // NB)

        @pl.when(index == 0)
        def _():
            inverses[0] = symmetric_part(top[0])

        @pl.when(index == K // NB)
        def _():
            lower = product(top[1], inverses[0], 1, 1)
            factor10[...] = lower
            packed = lower.astype(BF16)
            inverses[1] = symmetric_part(top[2] - product(packed, packed, 1, 1, None))

        low = pl.multiple_of((index - which * (K // NB)) * NB, NB)
        factor_block(low, inverses.at[which], staged, base_work, base_out)

        @pl.when(index == 1)
        def _():
            for shift in range(1, fronts):
                over_copy(shift).wait_recv()
            total = from_fronts[0]
            for who in range(1, fronts):
                total = total + from_fronts[who]
            cap = onward.shape[1]
            for who in range(panels):
                onward[who] = total[who * cap : (who + 1) * cap, :]
            for shift in range(1, panels):
                inward_copy(shift).start()

        @pl.when(index == 2)
        def _():
            for shift in range(1, panels):
                piece_copy(shift).wait_recv()
            total = pieces[0]
            for who in range(1, panels):
                total = total + pieces[who]
            sums[me] = total
            for shift in range(1, panels):
                sum_copy(shift).start()

        @pl.when(index == 3)
        def _():
            relay(1, 1)

        @pl.when(index == 5)
        def _():
            relay(1, 3)

        @pl.when(index == 6)
        def _():
            relay(1, 2)

        return carry

    lax.fori_loop(0, 2 * (K // NB), block_step, 0)

    for shift in range(1, panels):
        sum_copy(shift).wait_recv()
    inverse0, inverse1, lower = inverses[0], inverses[1], factor10[...]
    count = panels // 2
    sums0 = jnp.concatenate([sums[piece] for piece in range(count)], axis=0)
    sums1 = jnp.concatenate([sums[count + piece] for piece in range(count)], axis=0)
    carried0 = product(inverse0, sums0, 1, 0, HIGH)
    carried1 = product(inverse1, sums1 - product(lower, carried0, 1, 0, HIGH), 1, 0, HIGH)
    solved1 = product(inverse1, right_side[K:, :] - carried1, 0, 0, HIGH)
    solved0 = product(inverse0, right_side[0:K, :] - carried0 - product(lower, solved1, 0, 0, HIGH), 0, 0, HIGH)
    solved[0:K, :] = solved0
    solved[K:, :] = solved1
    values = product(pick[...], solved[...], 1, 0)
    size = chosen.shape[1]
    for child in range(fronts):
        chosen[child] = values[child * size : (child + 1) * size, :]
    for shift in range(1, fronts):
        pick_copy(shift).start()
    chosen_in[front] = chosen[front]
    front_values[...] = jnp.where(below, known[...], jnp.where(me == 0, solved0, solved1))

    factor0 = product(columns[:, 0:K], inverse0, 1, 1, HIGH)
    current = columns[:, K:] - product(factor0.astype(BF16), lower.astype(BF16), 1, 1, None)
    factor1 = jnp.where(me >= 1, product(current, inverse1, 1, 1, HIGH), 0.0)
    factor[:, 0:K] = factor0
    factor[:, K:] = factor1
    weight1 = product(factor1, inverse1, 1, 0, HIGH)
    weight0 = product(factor0 - product(weight1, lower, 1, 0, HIGH), inverse0, 1, 0, HIGH)
    weights[0] = weight0.astype(BF16)
    weights[1] = weight1.astype(BF16)

    for shift in range(1, panels):
        inward_copy(shift).wait_recv()
    child_values[...] = inward[...]
    child_values[me] = onward[me]
    for shift in range(1, fronts):
        pick_copy(shift).wait_recv()
    total = chosen_in[0]
    for who in range(1, fronts):
        total = total + chosen_in[who]
    cap = child_values.shape[1]
    for lead in range(size // cap):
        child_values[lead] = total[lead * cap : (lead + 1) * cap, :]
    own_late.wait()
    finish(1)
    for kind in range(2):
        drain(kind)
    for shift in range(1, panels):
        piece_copy(shift).wait_send()
        sum_copy(shift).wait_send()
        inward_copy(shift).wait_send()
    for shift in range(1, fronts):
        over_copy(shift).wait_send()
        pick_copy(shift).wait_send()
    for shift in range(1, fronts):
        late_copy(shift).wait()
    for root, indices in roots:

        @pl.when(me == root)
        def _():
            for shift in range(1, panels):
                for index in indices:
                    scatter(shift, index).wait_send()


def panel_step(sizes, parents, table, own_table, early, piv_cols, known, right_side, late):
    panels, fronts, side = sizes
    sem = pltpu.SemaphoreType.DMA
    part = K // panels
    rows, pivots = piv_cols.shape
    rhs = known.shape[1]
    cap = early.shape[2] // panels
    anywhere = pl.BlockSpec(memory_space=pl.ANY)
    vmem = pl.BlockSpec(memory_space=pltpu.VMEM)
    wide = pltpu.VMEM((panels, pivots // panels, rhs), F32)
    few = pltpu.VMEM((fronts, own_table.shape[0] // fronts, rhs), F32)
    over = pltpu.VMEM((fronts, panels * cap, rhs), F32)
    slot = pltpu.VMEM((panels, cap, rhs), F32)
    square = pltpu.VMEM((K, K), F32)
    tile = pltpu.VMEM((NB, NB), F32)
    return pl.pallas_call(
        lambda *refs: panel_kernel((panels, fronts), side, *refs),
        name="panel_step",
        out_shape=(
            jax.ShapeDtypeStruct((2, panels, K, K), BF16),
            jax.ShapeDtypeStruct((fronts,) + late.shape, BF16),
            jax.ShapeDtypeStruct((rows, pivots), F32),
            jax.ShapeDtypeStruct((2, K, K), BF16),
            jax.ShapeDtypeStruct((rows, rhs), F32),
            jax.ShapeDtypeStruct((panels, cap, rhs), F32),
            jax.ShapeDtypeStruct((table.shape[0], rows), BF16),
        ),
        in_specs=[pl.BlockSpec(memory_space=pltpu.SMEM)] + [vmem] * 6 + [anywhere],
        out_specs=[anywhere] * 2 + [vmem] * 5,
        scratch_shapes=[
            pltpu.VMEM((rows, pivots), F32),
            pltpu.VMEM((2, rows, K), BF16),
            pltpu.VMEM((own_table.shape[0], pivots), F32),
            over,
            pltpu.VMEM((2, K, K), F32),
            square,
            wide,
            wide,
            pltpu.VMEM((pivots, rhs), F32),
            few,
            few,
            over,
            slot,
            slot,
            pltpu.VMEM((3, K, K), F32),
            pltpu.VMEM((3, part, K), F32),
            wide,
            pltpu.VMEM((NB, K), F32),
            tile,
            tile,
            sem((3, panels)),
            sem((3,)),
        ]
        + [sem((2, 2, 2))] * 4
        + [sem((2, 2, 4, 2))] * 4
        + [sem((panels,))] * 6
        + [sem((fronts,))] * 6
        + [sem((6,))],
        compiler_params=pltpu.CompilerParams(
            collective_id=2, has_side_effects=True, vmem_limit_bytes=40 << 20
        ),
    )(parents, table, own_table, early, piv_cols, known, right_side, late)


def update_kernel(late, blocks, weights, onehot, factor, front_values, child_values, update, *rest):
    outs, sem = rest[:3], rest[3]
    step = pl.program_id(0)
    results = (factor, front_values, child_values)

    @pl.when(step == 0)
    def _():
        for i in range(3):
            pltpu.make_async_copy(results[i], outs[i], sem.at[i]).start()

    fronts, tiles, each, lanes = late.shape
    rows = jnp.concatenate([late[:, t].reshape(fronts * each, lanes) for t in range(tiles)], axis=1)
    value = product(onehot[...], rows, 0, 0, None)
    for half in range(2):
        value = value - product(weights[half], blocks[half, 0], 1, 1, None)
    update[...] = jnp.where(lax.axis_index("panel") >= 2, value, 0.0).astype(BF16)

    @pl.when(step == pl.num_programs(0) - 1)
    def _():
        for i in range(3):
            pltpu.make_async_copy(results[i], outs[i], sem.at[i]).wait()


def update_step(late_all, blocks, weights, onehot, factor, front_values, child_values):
    fronts, all_tiles, each, lanes = late_all.shape
    tiles = K // lanes
    steps = all_tiles // tiles
    first = blocks.shape[1] - steps
    rows = weights.shape[1]
    anywhere = pl.BlockSpec(memory_space=pl.ANY)
    fixed = pl.BlockSpec(memory_space=pltpu.VMEM)
    like = [jax.ShapeDtypeStruct(x.shape, x.dtype) for x in (factor, front_values, child_values)]
    return pl.pallas_call(
        update_kernel,
        name="update",
        grid=(steps,),
        out_shape=[jax.ShapeDtypeStruct((rows, steps * K), BF16)] + like,
        in_specs=[
            pl.BlockSpec((fronts, tiles, each, lanes), lambda j: (0, j, 0, 0)),
            pl.BlockSpec((2, 1, K, K), lambda j: (0, j + first, 0, 0)),
            fixed,
            fixed,
            anywhere,
            anywhere,
            anywhere,
        ],
        out_specs=[pl.BlockSpec((rows, K), lambda j: (0, j))] + [anywhere] * 3,
        scratch_shapes=[pltpu.SemaphoreType.DMA((3,))],
        compiler_params=pltpu.CompilerParams(vmem_limit_bytes=40 << 20),
    )(late_all, blocks, weights, onehot, factor, front_values, child_values)


def on_device(sizes, pivot_columns, child_rows, slot_rows, parents, pivot_rhs, boundary_solution):
    panels, fronts, _ = sizes
    piv_cols = pivot_columns[0]
    pivots = piv_cols.shape[1]
    rows_out = child_rows[0, 0]
    cap, width = rows_out.shape[1:]
    lanes = NB
    lead = pivots // K
    each = panels * cap
    known = boundary_solution[0]

    rows_tiled = rows_out.reshape(panels, cap, width // lanes, lanes).transpose(0, 2, 1, 3)
    slots_wide = jnp.broadcast_to(slot_rows[0, 0][:, :, None], (panels, cap, lanes))
    early, late, table, own_table = exchange_rows(panels, fronts, lead, rows_tiled, slots_wide, pivots // lanes)
    blocks, late_all, factor, weights, front_values, child_values, onehot = panel_step(
        sizes,
        parents,
        table.reshape(fronts * each, lanes),
        own_table.reshape(fronts * lead * cap, lanes),
        early.reshape(fronts, pivots // lanes, each, lanes),
        piv_cols,
        known,
        pivot_rhs[0],
        late,
    )
    update_matrix, factor, front_values, child_values = update_step(
        late_all.reshape(fronts, -1, each, lanes), blocks, weights, onehot, factor, front_values, child_values
    )
    return (factor[None], update_matrix[None], front_values[None], child_values[None, None])


def solution(mesh):
    in_specs = (
        P("front", "panel", None),
        P("front", "panel", None, None, None),
        P("front", "panel", None, None),
        P(),
        P("front", None, None),
        P("front", "panel", None),
    )
    out_specs = (
        P("front", "panel", None),
        P("front", "panel", None),
        P("front", "panel", None),
        P("front", "panel", None, None, None),
    )
    panels, fronts = mesh.shape["panel"], mesh.shape["front"]
    sizes = (panels, fronts, math.isqrt(panels))
    return jax.shard_map(
        lambda *arrays: on_device(sizes, *arrays),
        mesh=mesh,
        in_specs=in_specs,
        out_specs=out_specs,
        check_vma=False,
    )
```

```python
import math

import jax
import jax.numpy as jnp
from jax import lax
from jax.experimental import pallas as pl
from jax.experimental.pallas import tpu as pltpu
from jax.sharding import PartitionSpec as P

K = 512
NB = 128
PIV = 1024
HIGHEST = lax.Precision.HIGHEST
HIGH = lax.Precision.HIGH
MESH = pl.DeviceIdType.MESH
F32 = jnp.float32
BF16 = jnp.bfloat16


def product(left, right, left_dim, right_dim, precision=HIGHEST):
    dims = (((left_dim,), (right_dim,)), ((), ()))
    return lax.dot_general(left, right, dims, precision=precision, preferred_element_type=F32)


def base_inverse(work, inverse):
    sub = lax.broadcasted_iota(jnp.int32, (8, NB), 0)
    lane = lax.broadcasted_iota(jnp.int32, (NB, NB), 1)
    row = lax.broadcasted_iota(jnp.int32, (NB, NB), 0)
    inverse[...] = (lane == row).astype(F32)
    for step in range(NB // 8):
        low = 8 * step
        left = work[low : low + 8, :]
        right = inverse[low : low + 8, :]
        columns = [jnp.broadcast_to(left[:, low + i : low + i + 1], (8, NB)) for i in range(8)]
        pivots = jnp.ones((8, NB), F32)
        recips, splats, rows = [], [], []
        for i in range(8):
            pivot = columns[i][i : i + 1, :]
            recip = 1.0 / pivot
            recips.append(recip)
            pivots = jnp.where(sub == i, pivot, pivots)
            ratio = jnp.where(sub > i, columns[i] * recip, 0.0)
            splat = {}
            for j in range(i + 1, 8):
                splat[j] = columns[j][i : i + 1, :]
                columns[j] = columns[j] - ratio * splat[j]
            splats.append(splat)
            rows.append((left[i : i + 1, :], right[i : i + 1, :]))
            left = left - ratio * rows[i][0]
            right = right - ratio * rows[i][1]
        at = low + 8
        while at < NB:
            size = min(32 - at % 32, NB - at)
            left_tile = work[at : at + size, :]
            right_tile = inverse[at : at + size, :]
            ratios = []
            for i in range(8):
                value = jnp.broadcast_to(left_tile[:, low + i : low + i + 1], (size, NB))
                for j in range(i):
                    value = value - ratios[j] * splats[j][i]
                ratios.append(value * recips[i])
            for i in range(8):
                left_tile = left_tile - ratios[i] * rows[i][0]
                right_tile = right_tile - ratios[i] * rows[i][1]
            work[at : at + size, :] = left_tile
            inverse[at : at + size, :] = right_tile
            at += size
        inverse[low : low + 8, :] = right * lax.rsqrt(pivots)


def symmetric_part(block):
    return (block + block.T) * 0.5


def factor_block(low, joined, staged, base_work, base_out):
    rows = pl.ds(low, NB)
    high = low + NB
    base_work[...] = joined[rows, rows]
    base_inverse(base_work, base_out)
    base = base_out[...]
    solved = product(base, joined[rows, :], 1, 0, HIGH)
    lane = lax.broadcasted_iota(jnp.int32, solved.shape, 1)
    upper = jnp.where(lane >= high, solved, 0.0)
    staged[...] = solved
    staged[:, rows] = base
    strip = joined[:, rows]
    joined[:, rows] = jnp.where(lax.broadcasted_iota(jnp.int32, strip.shape, 0) >= high, 0.0, strip)
    joined[...] = joined[...] - product(upper, staged[...], 0, 0, HIGH)
    joined[rows, :] = jnp.where(lane < high, staged[...], 0.0)


def exchange_kernel(
    counts, rows, slots, early, late, table, own_table, send_a, recv_a, send_b, recv_b, send_s, recv_s,
    front_send, front_recv, front_send_s, front_recv_s, own_send, own_recv, local_sem
):
    panels, fronts = counts
    me = lax.axis_index("panel")
    front = lax.axis_index("front")
    tiles = early.shape[1]
    barrier = pltpu.get_barrier_semaphore()
    for shift in range(1, panels):
        peer = lax.rem(me + shift, panels)
        pl.semaphore_signal(barrier, inc=1, device_id={"panel": peer}, device_id_type=MESH)
    for shift in range(1, fronts):
        peer = lax.rem(front + shift, fronts)
        pl.semaphore_signal(barrier, inc=1, device_id={"front": peer}, device_id_type=MESH)
    pl.semaphore_wait(barrier, panels + fronts - 2)

    def to_panel(source, target, send, recv, shift):
        peer = lax.rem(me + shift, panels)
        return pltpu.make_async_remote_copy(
            src_ref=source(peer),
            dst_ref=target,
            send_sem=send.at[shift],
            recv_sem=recv.at[shift],
            device_id={"panel": peer},
            device_id_type=MESH,
        )

    def early_copy(shift):
        return to_panel(lambda p: rows.at[p, pl.ds(0, tiles)], early.at[front, :, me], send_a, recv_a, shift)

    def slot_copy(shift):
        return to_panel(lambda p: slots.at[p], table.at[front, me], send_s, recv_s, shift)

    def late_copy(shift):
        return to_panel(lambda p: rows.at[p, pl.ds(tiles, late.shape[0])], late.at[:, me], send_b, recv_b, shift)

    lead = own_table.shape[1]

    def own_copy(shift):
        peer = lax.rem(front + shift, fronts)
        return pltpu.make_async_remote_copy(
            src_ref=slots.at[pl.ds(0, lead)],
            dst_ref=own_table.at[front],
            send_sem=own_send.at[shift],
            recv_sem=own_recv.at[shift],
            device_id={"front": peer},
            device_id_type=MESH,
        )

    for shift in range(1, panels):
        slot_copy(shift).start()
        early_copy(shift).start()
    for shift in range(1, fronts):
        own_copy(shift).start()
    own = [
        pltpu.make_async_copy(slots.at[pl.ds(0, lead)], own_table.at[front], local_sem.at[3]),
        pltpu.make_async_copy(rows.at[me, pl.ds(0, tiles)], early.at[front, :, me], local_sem.at[0]),
        pltpu.make_async_copy(slots.at[me], table.at[front, me], local_sem.at[1]),
        pltpu.make_async_copy(rows.at[me, pl.ds(tiles, late.shape[0])], late.at[:, me], local_sem.at[2]),
    ]
    for copy in own:
        copy.start()
    for shift in range(1, panels):
        late_copy(shift).start()
    for copy in own:
        copy.wait()
    for shift in range(1, panels):
        slot_copy(shift).wait_recv()
        early_copy(shift).wait_recv()

    def to_front(array, send, recv, shift):
        peer = lax.rem(front + shift, fronts)
        return pltpu.make_async_remote_copy(
            src_ref=array.at[front],
            dst_ref=array.at[front],
            send_sem=send.at[shift],
            recv_sem=recv.at[shift],
            device_id={"front": peer},
            device_id_type=MESH,
        )

    for shift in range(1, fronts):
        to_front(table, front_send_s, front_recv_s, shift).start()
        to_front(early, front_send, front_recv, shift).start()
    for shift in range(1, panels):
        slot_copy(shift).wait_send()
        early_copy(shift).wait_send()
        late_copy(shift).wait()
    for shift in range(1, fronts):
        to_front(table, front_send_s, front_recv_s, shift).wait()
        to_front(early, front_send, front_recv, shift).wait()
        own_copy(shift).wait()


def exchange_rows(panels, fronts, lead, rows, slots, tiles):
    _, all_tiles, cap, lanes = rows.shape
    sem = pltpu.SemaphoreType.DMA
    return pl.pallas_call(
        lambda *refs: exchange_kernel((panels, fronts), *refs),
        name="exchange",
        out_shape=(
            jax.ShapeDtypeStruct((fronts, tiles, panels, cap, lanes), BF16),
            jax.ShapeDtypeStruct((all_tiles - tiles, panels, cap, lanes), BF16),
            jax.ShapeDtypeStruct((fronts, panels, cap, lanes), jnp.int32),
            jax.ShapeDtypeStruct((fronts, lead, cap, lanes), jnp.int32),
        ),
        in_specs=[pl.BlockSpec(memory_space=pltpu.HBM)] * 2,
        out_specs=[pl.BlockSpec(memory_space=space) for space in (pltpu.VMEM, pl.ANY, pltpu.VMEM, pltpu.VMEM)],
        scratch_shapes=[sem((panels,))] * 6 + [sem((fronts,))] * 6 + [sem((4,))],
        compiler_params=pltpu.CompilerParams(collective_id=1, has_side_effects=True, vmem_limit_bytes=8 << 20),
    )(rows, slots)


def assemble(parents, table, own_table, early, piv_cols, known, columns, halves, onehot, pick, picked):
    front = lax.axis_index("front")
    fronts, _, each, lanes = early.shape
    owners = [parents[child] == front for child in range(fronts)]

    def masked(ref, size):
        return jnp.concatenate(
            [jnp.where(owners[c], ref[c * size : (c + 1) * size, :], -1) for c in range(fronts)], axis=0
        )

    kept = masked(table, each)
    lane = lax.broadcasted_iota(jnp.int32, kept.shape, 1)
    chosen = jnp.concatenate(
        [(kept == lane + t * lanes).astype(F32) for t in range(known.shape[0] // lanes)], axis=1
    )
    small = chosen.astype(BF16)
    onehot[...] = chosen.T.astype(BF16)
    half = piv_cols.shape[1] // 2
    for h in range(2):
        tiles = half // lanes
        rows = jnp.concatenate(
            [early[:, h * tiles + t].reshape(fronts * each, lanes) for t in range(tiles)], axis=1
        )
        value = piv_cols[:, h * half : (h + 1) * half] + product(small, rows, 0, 0, None)
        columns[:, h * half : (h + 1) * half] = value
        halves[h] = value.astype(BF16)
    found = product(chosen, known[...], 1, 0)
    for child in range(fronts):
        picked[child] = found[child * each : (child + 1) * each, :]
    size = own_table.shape[0] // fronts
    own = masked(own_table, size)
    cap = size * K // piv_cols.shape[1]
    where = lax.rem(lax.broadcasted_iota(jnp.int32, own.shape, 0), size) // cap
    target = jnp.where(own >= 0, own + where * K, -1)
    lane = lax.broadcasted_iota(jnp.int32, own.shape, 1)
    for t in range(pick.shape[1] // lanes):
        pick[:, t * lanes : (t + 1) * lanes] = (target == lane + t * lanes).astype(F32)


def panel_kernel(
    counts, side, parents, table, own_table, early, own_columns, known, right_side, late,
    blocks, late_all, factor, weights, front_values, child_values, onehot,
    piv_cols, columns, halves, pick, picked,
    inverses, factor10, partial, sums, solved, chosen, chosen_in, from_fronts, onward, inward,
    top, chunk, pieces, staged, base_work, base_out,
    scatter_send, scatter_recv, whole_send, whole_recv, half_send, half_recv,
    far_send, far_recv, farther_send, farther_recv,
    piece_send, piece_recv, sum_send, sum_recv, inward_send, inward_recv,
    late_send, late_recv, over_send, over_recv, pick_send, pick_recv, local_sem,
):
    panels, fronts = counts
    me = lax.axis_index("panel")
    front = lax.axis_index("front")
    across, along = me // side, lax.rem(me, side)
    part = top.shape[1] // panels
    load = pltpu.make_async_copy(own_columns, piv_cols, local_sem.at[6])
    load.start()
    barrier = pltpu.get_barrier_semaphore()
    for shift in range(1, panels):
        peer = lax.rem(me + shift, panels)
        pl.semaphore_signal(barrier, inc=1, device_id={"panel": peer}, device_id_type=MESH)
    for shift in range(1, fronts):
        peer = lax.rem(front + shift, fronts)
        pl.semaphore_signal(barrier, inc=1, device_id={"front": peer}, device_id_type=MESH)
    load.wait()
    assemble(parents, table, own_table, early, piv_cols, known, columns, halves, onehot, pick, picked)
    below = me >= 2
    boundary = jnp.where(below, known[...], 0.0)
    width = partial.shape[1]
    for half in range(2):
        value = product(columns[:, half * K : (half + 1) * K], boundary, 0, 0, HIGH)
        for piece in range(panels // 2):
            partial[half * (panels // 2) + piece] = value[piece * width : (piece + 1) * width, :]
    pieces[me] = partial[me]
    pl.semaphore_wait(barrier, panels + fronts - 2)

    def chunk_rows(who):
        return pl.ds(pl.multiple_of(who * part, 8), part)

    def scatter(shift, index):
        peer = lax.rem(me + shift, panels)
        lanes = pl.ds(K if index == 2 else 0, K)
        return pltpu.make_async_remote_copy(
            src_ref=columns.at[chunk_rows(peer), lanes],
            dst_ref=chunk.at[index],
            send_sem=scatter_send.at[index, shift],
            recv_sem=scatter_recv.at[index],
            device_id={"panel": peer},
            device_id_type=MESH,
        )

    def own_chunk(index):
        lanes = pl.ds(K if index == 2 else 0, K)
        return pltpu.make_async_copy(columns.at[chunk_rows(me), lanes], chunk.at[index], local_sem.at[index])

    roots = ((0, (0,)), (1, (1, 2)))
    for root, indices in roots:

        @pl.when(me == root)
        def _():
            for shift in range(1, panels):
                for index in indices:
                    scatter(shift, index).start()
            for index in indices:
                own_chunk(index).start()

    coords = [[lax.rem(at + step, side) for step in range(side)] for at in (across, along)]

    def place(half, first, second):
        near_axis, far_axis = (coords[0], coords[1]) if half == 0 else (coords[1], coords[0])
        first, second = near_axis[first % side], far_axis[second % side]
        return first * side + second if half == 0 else second * side + first

    def view(kind, half, who, rows):
        if kind != 1:
            size = part if rows is None else part // 2
            low = who * part + (part // 2 if rows == 1 else 0)
            return top.at[pl.ds(kind // 2, kind // 2 + 1), pl.ds(pl.multiple_of(low, 8), size), pl.ds(half * (K // 2), K // 2)]
        ref = blocks.at[half, who]
        return ref if rows is None else ref.at[pl.ds(rows * (K // 2), K // 2)]

    def move(kind, half, who, rows, target, send, recv, slot):
        ref = view(kind, half, who, rows)
        return pltpu.make_async_remote_copy(
            src_ref=ref,
            dst_ref=ref,
            send_sem=send.at[slot],
            recv_sem=recv.at[slot],
            device_id={"panel": target},
            device_id_type=MESH,
        )

    def whole(kind, half, way):
        step = 1 if way == 0 else -1
        copy = move(kind, half, me, None, place(half, step, 0), whole_send, whole_recv, (kind, half, way))
        return kind, copy, me, place(half, -step, 0)

    def halved(kind, half, way):
        step = 1 if way == 0 else -1
        who = place(half, -step, 0)
        copy = move(kind, half, who, way, place(half, step, 0), half_send, half_recv, (kind, half, way))
        return kind, copy, who, place(half, 2, 0)

    def far(kind, half, offset, way):
        step = 1 if way == 0 else -1
        who = place(half, offset, 0)
        copy = move(kind, half, who, None, place(half, 0, step), far_send, far_recv, (kind, half, offset, way))
        return kind, copy, who, place(half, offset, -step)

    def farther(kind, half, offset, way):
        step = 1 if way == 0 else -1
        who = place(half, offset, -step)
        copy = move(
            kind, half, who, way, place(half, 0, step), farther_send, farther_recv, (kind, half, offset, way)
        )
        return kind, copy, who, place(half, offset, 2)

    def guarded(kind, who, act):
        if kind != 1:
            act()
        else:
            pl.when(who >= 2)(act)

    def start(hop):
        guarded(hop[0], hop[2], hop[1].start)

    def sent(hop):
        guarded(hop[0], hop[2], hop[1].wait_send)

    def arrived(hop):
        guarded(hop[0], hop[3], hop[1].wait_recv)

    both = [(half, way) for half in range(2) for way in range(2)]

    def near(kind):
        for half, way in both:
            start(whole(kind, half, way))

    def own_far(kind):
        for half, way in both:
            start(far(kind, half, 0, way))

    def halves_on(kind):
        for half, way in both:
            arrived(whole(kind, half, way))
            start(halved(kind, half, way))

    def far_on(kind, offset):
        for half, way in both:
            start(far(kind, half, offset, way))

    def last_far_on(kind):
        for half in range(2):
            for way in range(2):
                arrived(halved(kind, half, way))
            for way in range(2):
                start(far(kind, half, 2, way))

    def relay(kind, offset):
        for half, way in both:
            arrived(far(kind, half, offset, way))
            start(farther(kind, half, offset, way))

    def finish(kind):
        for half, way in both:
            for offset in range(4):
                arrived(farther(kind, half, offset, way))

    def drain(kind):
        for half, way in both:
            sent(whole(kind, half, way))
            sent(halved(kind, half, way))
            for offset in range(4):
                sent(far(kind, half, offset, way))
                sent(farther(kind, half, offset, way))

    def over_copy(shift):
        peer = lax.rem(front + shift, fronts)
        return pltpu.make_async_remote_copy(
            src_ref=picked.at[peer],
            dst_ref=from_fronts.at[front],
            send_sem=over_send.at[shift],
            recv_sem=over_recv.at[shift],
            device_id={"front": peer},
            device_id_type=MESH,
        )

    def inward_copy(shift):
        peer = lax.rem(me + shift, panels)
        return pltpu.make_async_remote_copy(
            src_ref=onward.at[peer],
            dst_ref=inward.at[me],
            send_sem=inward_send.at[shift],
            recv_sem=inward_recv.at[shift],
            device_id={"panel": peer},
            device_id_type=MESH,
        )

    def pick_copy(shift):
        peer = lax.rem(front + shift, fronts)
        return pltpu.make_async_remote_copy(
            src_ref=chosen.at[peer],
            dst_ref=chosen_in.at[front],
            send_sem=pick_send.at[shift],
            recv_sem=pick_recv.at[shift],
            device_id={"front": peer},
            device_id_type=MESH,
        )

    def late_copy(shift):
        peer = lax.rem(front + shift, fronts)
        return pltpu.make_async_remote_copy(
            src_ref=late,
            dst_ref=late_all.at[front],
            send_sem=late_send.at[shift],
            recv_sem=late_recv.at[shift],
            device_id={"front": peer},
            device_id_type=MESH,
        )

    def piece_copy(shift):
        peer = lax.rem(me + shift, panels)
        return pltpu.make_async_remote_copy(
            src_ref=partial.at[peer],
            dst_ref=pieces.at[me],
            send_sem=piece_send.at[shift],
            recv_sem=piece_recv.at[shift],
            device_id={"panel": peer},
            device_id_type=MESH,
        )

    def sum_copy(shift):
        peer = lax.rem(me + shift, panels)
        return pltpu.make_async_remote_copy(
            src_ref=sums.at[me],
            dst_ref=sums.at[me],
            send_sem=sum_send.at[shift],
            recv_sem=sum_recv.at[shift],
            device_id={"panel": peer},
            device_id_type=MESH,
        )

    own = [
        pltpu.make_async_copy(halves, blocks.at[:, me], local_sem.at[3]),
        pltpu.make_async_copy(picked.at[front], from_fronts.at[front], local_sem.at[4]),
    ]
    own_late = pltpu.make_async_copy(late, late_all.at[front], local_sem.at[5])
    for copy in own:
        copy.start()
    own_late.start()
    for shift in range(1, fronts):
        over_copy(shift).start()
    for copy in own:
        copy.wait()
    near(1)
    for shift in range(1, fronts):
        late_copy(shift).start()

    def own_rows(root, index):

        @pl.when(me == root)
        def _():
            own_chunk(index).wait()

        @pl.when(me != root)
        def _():
            scatter(1, index).wait_recv()

        top[index, chunk_rows(me), :] = chunk[index]

    own_rows(0, 0)
    near(0)
    own_far(0)
    halves_on(1)
    halves_on(0)
    far_on(0, 1)
    far_on(0, 3)
    for shift in range(1, panels):
        piece_copy(shift).start()
    last_far_on(0)
    for offset in (0, 1, 3, 2):
        relay(0, offset)
    own_rows(1, 1)
    own_rows(1, 2)
    near(2)
    own_far(2)
    own_far(1)
    finish(0)

    def block_step(index, carry):
        which = index // (K // NB)

        @pl.when(index == 0)
        def _():
            inverses[0] = symmetric_part(top[0])

        @pl.when(index == K // NB)
        def _():
            finish(2)
            lower = product(top[1], inverses[0], 1, 1, HIGH)
            factor10[...] = lower
            packed = lower.astype(BF16)
            inverses[1] = symmetric_part(top[2] - product(packed, packed, 1, 1, None))

        low = pl.multiple_of((index - which * (K // NB)) * NB, NB)
        factor_block(low, inverses.at[which], staged, base_work, base_out)

        @pl.when(index == 0)
        def _():
            halves_on(2)
            far_on(2, 1)
            far_on(2, 3)
            far_on(1, 1)

        @pl.when(index == 1)
        def _():
            last_far_on(2)
            relay(2, 0)

        @pl.when(index == 2)
        def _():
            relay(2, 1)
            relay(2, 3)

        @pl.when(index == 3)
        def _():
            relay(2, 2)
            far_on(1, 3)
            last_far_on(1)
            relay(1, 0)

        @pl.when(index == 4)
        def _():
            relay(1, 1)
            for shift in range(1, panels):
                piece_copy(shift).wait_recv()
            total = pieces[0]
            for who in range(1, panels):
                total = total + pieces[who]
            sums[me] = total
            for shift in range(1, panels):
                sum_copy(shift).start()

        @pl.when(index == 5)
        def _():
            relay(1, 3)
            for shift in range(1, fronts):
                over_copy(shift).wait_recv()
            total = from_fronts[0]
            for who in range(1, fronts):
                total = total + from_fronts[who]
            cap = onward.shape[1]
            for who in range(panels):
                onward[who] = total[who * cap : (who + 1) * cap, :]
            for shift in range(1, panels):
                inward_copy(shift).start()

        @pl.when(index == 6)
        def _():
            relay(1, 2)

        return carry

    lax.fori_loop(0, 2 * (K // NB), block_step, 0)

    for shift in range(1, panels):
        sum_copy(shift).wait_recv()
    inverse0, inverse1, lower = inverses[0], inverses[1], factor10[...]
    count = panels // 2
    sums0 = jnp.concatenate([sums[piece] for piece in range(count)], axis=0)
    sums1 = jnp.concatenate([sums[count + piece] for piece in range(count)], axis=0)
    carried0 = product(inverse0, sums0, 1, 0, HIGH)
    carried1 = product(inverse1, sums1 - product(lower, carried0, 1, 0, HIGH), 1, 0, HIGH)
    solved1 = product(inverse1, right_side[K:, :] - carried1, 0, 0, HIGH)
    solved0 = product(inverse0, right_side[0:K, :] - carried0 - product(lower, solved1, 0, 0, HIGH), 0, 0, HIGH)
    solved[0:K, :] = solved0
    solved[K:, :] = solved1
    values = product(pick[...], solved[...], 1, 0)
    size = chosen.shape[1]
    for child in range(fronts):
        chosen[child] = values[child * size : (child + 1) * size, :]
    for shift in range(1, fronts):
        pick_copy(shift).start()
    chosen_in[front] = chosen[front]
    front_values[...] = jnp.where(below, known[...], jnp.where(me == 0, solved0, solved1))

    factor0 = product(columns[:, 0:K], inverse0, 1, 1, HIGH)
    current = columns[:, K:] - product(factor0.astype(BF16), lower.astype(BF16), 1, 1, None)
    factor1 = jnp.where(me >= 1, product(current, inverse1, 1, 1, HIGH), 0.0)
    factor[:, 0:K] = factor0
    factor[:, K:] = factor1
    weight1 = product(factor1, inverse1, 1, 0, HIGH)
    weight0 = product(factor0 - product(weight1, lower, 1, 0, HIGH), inverse0, 1, 0, HIGH)
    weights[0] = weight0.astype(BF16)
    weights[1] = weight1.astype(BF16)

    for shift in range(1, panels):
        inward_copy(shift).wait_recv()
    child_values[...] = inward[...]
    child_values[me] = onward[me]
    for shift in range(1, fronts):
        pick_copy(shift).wait_recv()
    total = chosen_in[0]
    for who in range(1, fronts):
        total = total + chosen_in[who]
    cap = child_values.shape[1]
    for lead in range(size // cap):
        child_values[lead] = total[lead * cap : (lead + 1) * cap, :]
    own_late.wait()
    finish(1)
    for kind in range(3):
        drain(kind)
    for shift in range(1, panels):
        piece_copy(shift).wait_send()
        sum_copy(shift).wait_send()
        inward_copy(shift).wait_send()
    for shift in range(1, fronts):
        over_copy(shift).wait_send()
        pick_copy(shift).wait_send()
    for shift in range(1, fronts):
        late_copy(shift).wait()
    for root, indices in roots:

        @pl.when(me == root)
        def _():
            for shift in range(1, panels):
                for index in indices:
                    scatter(shift, index).wait_send()


def panel_step(sizes, parents, table, own_table, early, piv_cols, known, right_side, late):
    panels, fronts, side = sizes
    sem = pltpu.SemaphoreType.DMA
    part = K // panels
    rows, pivots = piv_cols.shape
    rhs = known.shape[1]
    cap = early.shape[2] // panels
    anywhere = pl.BlockSpec(memory_space=pl.ANY)
    vmem = pl.BlockSpec(memory_space=pltpu.VMEM)
    wide = pltpu.VMEM((panels, pivots // panels, rhs), F32)
    few = pltpu.VMEM((fronts, own_table.shape[0] // fronts, rhs), F32)
    over = pltpu.VMEM((fronts, panels * cap, rhs), F32)
    slot = pltpu.VMEM((panels, cap, rhs), F32)
    square = pltpu.VMEM((K, K), F32)
    tile = pltpu.VMEM((NB, NB), F32)
    return pl.pallas_call(
        lambda *refs: panel_kernel((panels, fronts), side, *refs),
        name="panel_step",
        out_shape=(
            jax.ShapeDtypeStruct((2, panels, K, K), BF16),
            jax.ShapeDtypeStruct((fronts,) + late.shape, BF16),
            jax.ShapeDtypeStruct((rows, pivots), F32),
            jax.ShapeDtypeStruct((2, K, K), BF16),
            jax.ShapeDtypeStruct((rows, rhs), F32),
            jax.ShapeDtypeStruct((panels, cap, rhs), F32),
            jax.ShapeDtypeStruct((rows, table.shape[0]), BF16),
        ),
        in_specs=[pl.BlockSpec(memory_space=pltpu.SMEM)] + [vmem] * 3 + [pl.BlockSpec(memory_space=pltpu.HBM)] + [vmem] * 2 + [anywhere],
        out_specs=[anywhere] + [vmem] * 6,
        scratch_shapes=[
            pltpu.VMEM((rows, pivots), F32),
            pltpu.VMEM((rows, pivots), F32),
            pltpu.VMEM((2, rows, K), BF16),
            pltpu.VMEM((own_table.shape[0], pivots), F32),
            over,
            pltpu.VMEM((2, K, K), F32),
            square,
            wide,
            wide,
            pltpu.VMEM((pivots, rhs), F32),
            few,
            few,
            over,
            slot,
            slot,
            pltpu.VMEM((3, K, K), F32),
            pltpu.VMEM((3, part, K), F32),
            wide,
            pltpu.VMEM((NB, K), F32),
            tile,
            tile,
            sem((3, panels)),
            sem((3,)),
        ]
        + [sem((3, 2, 2))] * 4
        + [sem((3, 2, 4, 2))] * 4
        + [sem((panels,))] * 6
        + [sem((fronts,))] * 6
        + [sem((7,))],
        compiler_params=pltpu.CompilerParams(
            collective_id=2, has_side_effects=True, vmem_limit_bytes=28 << 20
        ),
    )(parents, table, own_table, early, piv_cols, known, right_side, late)


def update_kernel(late, blocks, weights, onehot, factor, front_values, child_values, update, *rest):
    outs, sem = rest[:3], rest[3]
    step = pl.program_id(0)
    results = (factor, front_values, child_values)

    @pl.when(step == 0)
    def _():
        for i in range(3):
            pltpu.make_async_copy(results[i], outs[i], sem.at[i]).start()

    fronts, tiles, each, lanes = late.shape
    below = lax.axis_index("panel") >= 2
    count = blocks.shape[1]
    for block in range(count):
        low = block * tiles // count
        rows = jnp.concatenate(
            [late[:, low + t].reshape(fronts * each, lanes) for t in range(tiles // count)], axis=1
        )
        value = product(onehot[...], rows, 1, 0, None)
        for half in range(2):
            value = value - product(weights[half], blocks[half, block], 1, 1, None)
        update[:, block * K : (block + 1) * K] = jnp.where(below, value, 0.0).astype(BF16)

    @pl.when(step == pl.num_programs(0) - 1)
    def _():
        for i in range(3):
            pltpu.make_async_copy(results[i], outs[i], sem.at[i]).wait()


def update_step(late_all, blocks, weights, onehot, factor, front_values, child_values):
    fronts, all_tiles, each, lanes = late_all.shape
    tiles = 2 * K // lanes
    steps = all_tiles // tiles
    first = blocks.shape[1] // 2 - steps
    rows = weights.shape[1]
    anywhere = pl.BlockSpec(memory_space=pl.ANY)
    fixed = pl.BlockSpec(memory_space=pltpu.VMEM)
    like = [jax.ShapeDtypeStruct(x.shape, x.dtype) for x in (factor, front_values, child_values)]
    return pl.pallas_call(
        update_kernel,
        name="update",
        grid=(steps,),
        out_shape=[jax.ShapeDtypeStruct((rows, steps * 2 * K), BF16)] + like,
        in_specs=[
            pl.BlockSpec((fronts, tiles, each, lanes), lambda j: (0, j, 0, 0)),
            pl.BlockSpec((2, 2, K, K), lambda j: (0, j + first, 0, 0)),
            fixed,
            fixed,
            anywhere,
            anywhere,
            anywhere,
        ],
        out_specs=[pl.BlockSpec((rows, 2 * K), lambda j: (0, j))] + [anywhere] * 3,
        scratch_shapes=[pltpu.SemaphoreType.DMA((3,))],
        compiler_params=pltpu.CompilerParams(vmem_limit_bytes=40 << 20),
    )(late_all, blocks, weights, onehot, factor, front_values, child_values)


def on_device(sizes, pivot_columns, child_rows, slot_rows, parents, pivot_rhs, boundary_solution):
    panels, fronts, _ = sizes
    piv_cols = pivot_columns[0]
    pivots = piv_cols.shape[1]
    rows_out = child_rows[0, 0]
    cap, width = rows_out.shape[1:]
    lanes = NB
    lead = pivots // K
    each = panels * cap
    known = boundary_solution[0]

    rows_tiled = rows_out.reshape(panels, cap, width // lanes, lanes).transpose(0, 2, 1, 3)
    slots_wide = jnp.broadcast_to(slot_rows[0, 0][:, :, None], (panels, cap, lanes))
    early, late, table, own_table = exchange_rows(panels, fronts, lead, rows_tiled, slots_wide, pivots // lanes)
    blocks, late_all, factor, weights, front_values, child_values, onehot = panel_step(
        sizes,
        parents,
        table.reshape(fronts * each, lanes),
        own_table.reshape(fronts * lead * cap, lanes),
        early.reshape(fronts, pivots // lanes, each, lanes),
        piv_cols,
        known,
        pivot_rhs[0],
        late,
    )
    update_matrix, factor, front_values, child_values = update_step(
        late_all.reshape(fronts, -1, each, lanes), blocks, weights, onehot, factor, front_values, child_values
    )
    return (factor[None], update_matrix[None], front_values[None], child_values[None, None])


def solution(mesh):
    in_specs = (
        P("front", "panel", None),
        P("front", "panel", None, None, None),
        P("front", "panel", None, None),
        P(),
        P("front", None, None),
        P("front", "panel", None),
    )
    out_specs = (
        P("front", "panel", None),
        P("front", "panel", None),
        P("front", "panel", None),
        P("front", "panel", None, None, None),
    )
    panels, fronts = mesh.shape["panel"], mesh.shape["front"]
    sizes = (panels, fronts, math.isqrt(panels))
    return jax.shard_map(
        lambda *arrays: on_device(sizes, *arrays),
        mesh=mesh,
        in_specs=in_specs,
        out_specs=out_specs,
        check_vma=False,
    )
```

```python
import math

import jax
import jax.numpy as jnp
from jax import lax
from jax.experimental import pallas as pl
from jax.experimental.pallas import tpu as pltpu
from jax.sharding import PartitionSpec as P

K = 512
NB = 128
PIV = 1024
HIGHEST = lax.Precision.HIGHEST
HIGH = lax.Precision.HIGH
MESH = pl.DeviceIdType.MESH
F32 = jnp.float32
BF16 = jnp.bfloat16


def product(left, right, left_dim, right_dim, precision=HIGHEST):
    dims = (((left_dim,), (right_dim,)), ((), ()))
    return lax.dot_general(left, right, dims, precision=precision, preferred_element_type=F32)


def base_inverse(work, inverse):
    sub = lax.broadcasted_iota(jnp.int32, (8, NB), 0)
    lane = lax.broadcasted_iota(jnp.int32, (NB, NB), 1)
    row = lax.broadcasted_iota(jnp.int32, (NB, NB), 0)
    inverse[...] = (lane == row).astype(F32)
    for step in range(NB // 8):
        low = 8 * step
        left = work[low : low + 8, :]
        right = inverse[low : low + 8, :]
        columns = [jnp.broadcast_to(left[:, low + i : low + i + 1], (8, NB)) for i in range(8)]
        pivots = jnp.ones((8, NB), F32)
        recips, splats, rows = [], [], []
        for i in range(8):
            pivot = columns[i][i : i + 1, :]
            recip = 1.0 / pivot
            recips.append(recip)
            pivots = jnp.where(sub == i, pivot, pivots)
            ratio = jnp.where(sub > i, columns[i] * recip, 0.0)
            splat = {}
            for j in range(i + 1, 8):
                splat[j] = columns[j][i : i + 1, :]
                columns[j] = columns[j] - ratio * splat[j]
            splats.append(splat)
            rows.append((left[i : i + 1, :], right[i : i + 1, :]))
            left = left - ratio * rows[i][0]
            right = right - ratio * rows[i][1]
        at = low + 8
        while at < NB:
            size = min(32 - at % 32, NB - at)
            left_tile = work[at : at + size, :]
            right_tile = inverse[at : at + size, :]
            ratios = []
            for i in range(8):
                value = jnp.broadcast_to(left_tile[:, low + i : low + i + 1], (size, NB))
                for j in range(i):
                    value = value - ratios[j] * splats[j][i]
                ratios.append(value * recips[i])
            for i in range(8):
                left_tile = left_tile - ratios[i] * rows[i][0]
                right_tile = right_tile - ratios[i] * rows[i][1]
            work[at : at + size, :] = left_tile
            inverse[at : at + size, :] = right_tile
            at += size
        inverse[low : low + 8, :] = right * lax.rsqrt(pivots)


def symmetric_part(block):
    return (block + block.T) * 0.5


def factor_block(low, joined, staged, base_work, base_out):
    rows = pl.ds(low, NB)
    high = low + NB
    base_work[...] = joined[rows, rows]
    base_inverse(base_work, base_out)
    base = base_out[...]
    solved = product(base, joined[rows, :], 1, 0, HIGH)
    lane = lax.broadcasted_iota(jnp.int32, solved.shape, 1)
    upper = jnp.where(lane >= high, solved, 0.0)
    staged[...] = solved
    staged[:, rows] = base
    strip = joined[:, rows]
    joined[:, rows] = jnp.where(lax.broadcasted_iota(jnp.int32, strip.shape, 0) >= high, 0.0, strip)
    joined[...] = joined[...] - product(upper, staged[...], 0, 0, HIGH)
    joined[rows, :] = jnp.where(lane < high, staged[...], 0.0)


def exchange_kernel(
    counts, rows, slots, early, late, table, own_table, send_a, recv_a, send_b, recv_b, send_s, recv_s,
    front_send, front_recv, front_send_s, front_recv_s, own_send, own_recv, local_sem
):
    panels, fronts = counts
    me = lax.axis_index("panel")
    front = lax.axis_index("front")
    tiles = early.shape[1]
    barrier = pltpu.get_barrier_semaphore()
    for shift in range(1, panels):
        peer = lax.rem(me + shift, panels)
        pl.semaphore_signal(barrier, inc=1, device_id={"panel": peer}, device_id_type=MESH)
    for shift in range(1, fronts):
        peer = lax.rem(front + shift, fronts)
        pl.semaphore_signal(barrier, inc=1, device_id={"front": peer}, device_id_type=MESH)
    pl.semaphore_wait(barrier, panels + fronts - 2)

    def to_panel(source, target, send, recv, shift):
        peer = lax.rem(me + shift, panels)
        return pltpu.make_async_remote_copy(
            src_ref=source(peer),
            dst_ref=target,
            send_sem=send.at[shift],
            recv_sem=recv.at[shift],
            device_id={"panel": peer},
            device_id_type=MESH,
        )

    def early_copy(shift):
        return to_panel(lambda p: rows.at[p, pl.ds(0, tiles)], early.at[front, :, me], send_a, recv_a, shift)

    def slot_copy(shift):
        return to_panel(lambda p: slots.at[p], table.at[front, me], send_s, recv_s, shift)

    def late_copy(shift):
        return to_panel(lambda p: rows.at[p, pl.ds(tiles, late.shape[0])], late.at[:, me], send_b, recv_b, shift)

    lead = own_table.shape[1]

    def own_copy(shift):
        peer = lax.rem(front + shift, fronts)
        return pltpu.make_async_remote_copy(
            src_ref=slots.at[pl.ds(0, lead)],
            dst_ref=own_table.at[front],
            send_sem=own_send.at[shift],
            recv_sem=own_recv.at[shift],
            device_id={"front": peer},
            device_id_type=MESH,
        )

    for shift in range(1, panels):
        slot_copy(shift).start()
        early_copy(shift).start()
    for shift in range(1, fronts):
        own_copy(shift).start()
    own = [
        pltpu.make_async_copy(slots.at[pl.ds(0, lead)], own_table.at[front], local_sem.at[3]),
        pltpu.make_async_copy(rows.at[me, pl.ds(0, tiles)], early.at[front, :, me], local_sem.at[0]),
        pltpu.make_async_copy(slots.at[me], table.at[front, me], local_sem.at[1]),
        pltpu.make_async_copy(rows.at[me, pl.ds(tiles, late.shape[0])], late.at[:, me], local_sem.at[2]),
    ]
    for copy in own:
        copy.start()
    for shift in range(1, panels):
        late_copy(shift).start()
    for copy in own:
        copy.wait()
    for shift in range(1, panels):
        slot_copy(shift).wait_recv()
        early_copy(shift).wait_recv()

    def to_front(array, send, recv, shift):
        peer = lax.rem(front + shift, fronts)
        return pltpu.make_async_remote_copy(
            src_ref=array.at[front],
            dst_ref=array.at[front],
            send_sem=send.at[shift],
            recv_sem=recv.at[shift],
            device_id={"front": peer},
            device_id_type=MESH,
        )

    for shift in range(1, fronts):
        to_front(table, front_send_s, front_recv_s, shift).start()
        to_front(early, front_send, front_recv, shift).start()
    for shift in range(1, panels):
        slot_copy(shift).wait_send()
        early_copy(shift).wait_send()
        late_copy(shift).wait()
    for shift in range(1, fronts):
        to_front(table, front_send_s, front_recv_s, shift).wait()
        to_front(early, front_send, front_recv, shift).wait()
        own_copy(shift).wait()


def exchange_rows(panels, fronts, lead, rows, slots, tiles):
    _, all_tiles, cap, lanes = rows.shape
    sem = pltpu.SemaphoreType.DMA
    return pl.pallas_call(
        lambda *refs: exchange_kernel((panels, fronts), *refs),
        name="exchange",
        out_shape=(
            jax.ShapeDtypeStruct((fronts, tiles, panels, cap, lanes), BF16),
            jax.ShapeDtypeStruct((all_tiles - tiles, panels, cap, lanes), BF16),
            jax.ShapeDtypeStruct((fronts, panels, cap, lanes), jnp.int32),
            jax.ShapeDtypeStruct((fronts, lead, cap, lanes), jnp.int32),
        ),
        in_specs=[pl.BlockSpec(memory_space=pltpu.HBM)] * 2,
        out_specs=[pl.BlockSpec(memory_space=space) for space in (pltpu.VMEM, pl.ANY, pltpu.VMEM, pltpu.VMEM)],
        scratch_shapes=[sem((panels,))] * 6 + [sem((fronts,))] * 6 + [sem((4,))],
        cost_estimate=pl.CostEstimate(flops=20_000_000_000, bytes_accessed=60_000_000, transcendentals=0),
        compiler_params=pltpu.CompilerParams(collective_id=1, has_side_effects=True, vmem_limit_bytes=8 << 20),
    )(rows, slots)


def masked_slots(parents, ref, fronts):
    front = lax.axis_index("front")
    size = ref.shape[0] // fronts
    return jnp.concatenate(
        [jnp.where(parents[c] == front, ref[c * size : (c + 1) * size, :], -1) for c in range(fronts)], axis=0
    )


def assemble(parents, table, early, piv_cols, columns, halves):
    fronts, _, each, lanes = early.shape
    kept = masked_slots(parents, table, fronts)
    lane = lax.broadcasted_iota(jnp.int32, kept.shape, 1)
    chosen = jnp.concatenate(
        [(kept == lane + t * lanes).astype(F32) for t in range(piv_cols.shape[0] // lanes)], axis=1
    )
    small = chosen.astype(BF16)
    half = piv_cols.shape[1] // 2
    for h in range(2):
        tiles = half // lanes
        rows = jnp.concatenate(
            [early[:, h * tiles + t].reshape(fronts * each, lanes) for t in range(tiles)], axis=1
        )
        value = piv_cols[:, h * half : (h + 1) * half] + product(small, rows, 0, 0, None)
        columns[:, h * half : (h + 1) * half] = value
        halves[h] = value.astype(BF16)
    return chosen


def select_values(parents, own_table, chosen, known, fronts, onehot, pick, picked):
    each = chosen.shape[0] // fronts
    lanes = own_table.shape[1]
    onehot[...] = chosen.T.astype(BF16)
    found = product(chosen, known[...], 1, 0)
    for child in range(fronts):
        picked[child] = found[child * each : (child + 1) * each, :]
    size = own_table.shape[0] // fronts
    own = masked_slots(parents, own_table, fronts)
    cap = size * K // pick.shape[1]
    where = lax.rem(lax.broadcasted_iota(jnp.int32, own.shape, 0), size) // cap
    target = jnp.where(own >= 0, own + where * K, -1)
    lane = lax.broadcasted_iota(jnp.int32, own.shape, 1)
    for t in range(pick.shape[1] // lanes):
        pick[:, t * lanes : (t + 1) * lanes] = (target == lane + t * lanes).astype(F32)


def panel_kernel(
    counts, side, parents, table, own_table, early, own_columns, known, right_side, late,
    blocks, late_all, factor, weights, front_values, child_values, onehot,
    piv_cols, columns, halves, pick, picked,
    inverses, factor10, partial, sums, solved, chosen, chosen_in, from_fronts, onward, inward,
    top, chunk, pieces, staged, base_work, base_out,
    scatter_send, scatter_recv, whole_send, whole_recv, half_send, half_recv,
    far_send, far_recv, farther_send, farther_recv,
    piece_send, piece_recv, sum_send, sum_recv, inward_send, inward_recv,
    late_send, late_recv, over_send, over_recv, pick_send, pick_recv, local_sem,
):
    panels, fronts = counts
    me = lax.axis_index("panel")
    front = lax.axis_index("front")
    across, along = me // side, lax.rem(me, side)
    part = top.shape[1] // panels
    load = pltpu.make_async_copy(own_columns, piv_cols, local_sem.at[6])
    load.start()
    barrier = pltpu.get_barrier_semaphore()
    for shift in range(1, panels):
        peer = lax.rem(me + shift, panels)
        pl.semaphore_signal(barrier, inc=1, device_id={"panel": peer}, device_id_type=MESH)
    for shift in range(1, fronts):
        peer = lax.rem(front + shift, fronts)
        pl.semaphore_signal(barrier, inc=1, device_id={"front": peer}, device_id_type=MESH)
    load.wait()
    chosen_rows = assemble(parents, table, early, piv_cols, columns, halves)
    pl.semaphore_wait(barrier, panels + fronts - 2)

    def chunk_rows(who):
        return pl.ds(pl.multiple_of(who * part, 8), part)

    def scatter(shift, index):
        peer = lax.rem(me + shift, panels)
        lanes = pl.ds(K if index == 2 else 0, K)
        return pltpu.make_async_remote_copy(
            src_ref=columns.at[chunk_rows(peer), lanes],
            dst_ref=chunk.at[index],
            send_sem=scatter_send.at[index, shift],
            recv_sem=scatter_recv.at[index],
            device_id={"panel": peer},
            device_id_type=MESH,
        )

    def own_chunk(index):
        lanes = pl.ds(K if index == 2 else 0, K)
        return pltpu.make_async_copy(columns.at[chunk_rows(me), lanes], chunk.at[index], local_sem.at[index])

    roots = ((0, (0,)), (1, (1, 2)))
    for root, indices in roots:

        @pl.when(me == root)
        def _():
            for shift in range(1, panels):
                for index in indices:
                    scatter(shift, index).start()
            for index in indices:
                own_chunk(index).start()

    coords = [[lax.rem(at + step, side) for step in range(side)] for at in (across, along)]

    def place(half, first, second):
        near_axis, far_axis = (coords[0], coords[1]) if half == 0 else (coords[1], coords[0])
        first, second = near_axis[first % side], far_axis[second % side]
        return first * side + second if half == 0 else second * side + first

    def view(kind, half, who, rows):
        if kind != 1:
            size = part if rows is None else part // 2
            low = who * part + (part // 2 if rows == 1 else 0)
            return top.at[pl.ds(kind // 2, kind // 2 + 1), pl.ds(pl.multiple_of(low, 8), size), pl.ds(half * (K // 2), K // 2)]
        ref = blocks.at[half, who]
        return ref if rows is None else ref.at[pl.ds(rows * (K // 2), K // 2)]

    def move(kind, half, who, rows, target, send, recv, slot):
        ref = view(kind, half, who, rows)
        return pltpu.make_async_remote_copy(
            src_ref=ref,
            dst_ref=ref,
            send_sem=send.at[slot],
            recv_sem=recv.at[slot],
            device_id={"panel": target},
            device_id_type=MESH,
        )

    def whole(kind, half, way):
        step = 1 if way == 0 else -1
        copy = move(kind, half, me, None, place(half, step, 0), whole_send, whole_recv, (kind, half, way))
        return kind, copy, me, place(half, -step, 0)

    def halved(kind, half, way):
        step = 1 if way == 0 else -1
        who = place(half, -step, 0)
        copy = move(kind, half, who, way, place(half, step, 0), half_send, half_recv, (kind, half, way))
        return kind, copy, who, place(half, 2, 0)

    def far(kind, half, offset, way):
        step = 1 if way == 0 else -1
        who = place(half, offset, 0)
        copy = move(kind, half, who, None, place(half, 0, step), far_send, far_recv, (kind, half, offset, way))
        return kind, copy, who, place(half, offset, -step)

    def farther(kind, half, offset, way):
        step = 1 if way == 0 else -1
        who = place(half, offset, -step)
        copy = move(
            kind, half, who, way, place(half, 0, step), farther_send, farther_recv, (kind, half, offset, way)
        )
        return kind, copy, who, place(half, offset, 2)

    def guarded(kind, who, act):
        if kind != 1:
            act()
        else:
            pl.when(who >= 2)(act)

    def start(hop):
        guarded(hop[0], hop[2], hop[1].start)

    def sent(hop):
        guarded(hop[0], hop[2], hop[1].wait_send)

    def arrived(hop):
        guarded(hop[0], hop[3], hop[1].wait_recv)

    both = [(half, way) for half in range(2) for way in range(2)]

    def near(kind):
        for half, way in both:
            start(whole(kind, half, way))

    def own_far(kind):
        for half, way in both:
            start(far(kind, half, 0, way))

    def halves_on(kind):
        for half, way in both:
            arrived(whole(kind, half, way))
            start(halved(kind, half, way))

    def far_on(kind, offset):
        for half, way in both:
            start(far(kind, half, offset, way))

    def last_far_on(kind):
        for half in range(2):
            for way in range(2):
                arrived(halved(kind, half, way))
            for way in range(2):
                start(far(kind, half, 2, way))

    def relay(kind, offset):
        for half, way in both:
            arrived(far(kind, half, offset, way))
            start(farther(kind, half, offset, way))

    def finish(kind):
        for half, way in both:
            for offset in range(4):
                arrived(farther(kind, half, offset, way))

    def drain(kind):
        for half, way in both:
            sent(whole(kind, half, way))
            sent(halved(kind, half, way))
            for offset in range(4):
                sent(far(kind, half, offset, way))
                sent(farther(kind, half, offset, way))

    def over_copy(shift):
        peer = lax.rem(front + shift, fronts)
        return pltpu.make_async_remote_copy(
            src_ref=picked.at[peer],
            dst_ref=from_fronts.at[front],
            send_sem=over_send.at[shift],
            recv_sem=over_recv.at[shift],
            device_id={"front": peer},
            device_id_type=MESH,
        )

    def inward_copy(shift):
        peer = lax.rem(me + shift, panels)
        return pltpu.make_async_remote_copy(
            src_ref=onward.at[peer],
            dst_ref=inward.at[me],
            send_sem=inward_send.at[shift],
            recv_sem=inward_recv.at[shift],
            device_id={"panel": peer},
            device_id_type=MESH,
        )

    def pick_copy(shift):
        peer = lax.rem(front + shift, fronts)
        return pltpu.make_async_remote_copy(
            src_ref=chosen.at[peer],
            dst_ref=chosen_in.at[front],
            send_sem=pick_send.at[shift],
            recv_sem=pick_recv.at[shift],
            device_id={"front": peer},
            device_id_type=MESH,
        )

    def late_copy(shift):
        peer = lax.rem(front + shift, fronts)
        return pltpu.make_async_remote_copy(
            src_ref=late,
            dst_ref=late_all.at[front],
            send_sem=late_send.at[shift],
            recv_sem=late_recv.at[shift],
            device_id={"front": peer},
            device_id_type=MESH,
        )

    def piece_copy(shift):
        peer = lax.rem(me + shift, panels)
        return pltpu.make_async_remote_copy(
            src_ref=partial.at[peer],
            dst_ref=pieces.at[me],
            send_sem=piece_send.at[shift],
            recv_sem=piece_recv.at[shift],
            device_id={"panel": peer},
            device_id_type=MESH,
        )

    def sum_copy(shift):
        peer = lax.rem(me + shift, panels)
        return pltpu.make_async_remote_copy(
            src_ref=sums.at[me],
            dst_ref=sums.at[me],
            send_sem=sum_send.at[shift],
            recv_sem=sum_recv.at[shift],
            device_id={"panel": peer},
            device_id_type=MESH,
        )

    own_halves = pltpu.make_async_copy(halves, blocks.at[:, me], local_sem.at[3])
    own_late = pltpu.make_async_copy(late, late_all.at[front], local_sem.at[5])
    own_halves.start()
    own_late.start()
    own_halves.wait()
    near(1)
    select_values(parents, own_table, chosen_rows, known, fronts, onehot, pick, picked)
    for shift in range(1, fronts):
        over_copy(shift).start()
    for shift in range(1, fronts):
        late_copy(shift).start()
    from_fronts[front] = picked[front]
    below = me >= 2
    boundary = jnp.where(below, known[...], 0.0)
    width = partial.shape[1]
    for half in range(2):
        value = product(columns[:, half * K : (half + 1) * K], boundary, 0, 0, HIGH)
        for piece in range(panels // 2):
            partial[half * (panels // 2) + piece] = value[piece * width : (piece + 1) * width, :]
    pieces[me] = partial[me]

    def own_rows(root, index):

        @pl.when(me == root)
        def _():
            own_chunk(index).wait()

        @pl.when(me != root)
        def _():
            scatter(1, index).wait_recv()

        top[index, chunk_rows(me), :] = chunk[index]

    own_rows(0, 0)
    near(0)
    own_far(0)
    halves_on(1)
    halves_on(0)
    far_on(0, 1)
    far_on(0, 3)
    for shift in range(1, panels):
        piece_copy(shift).start()
    last_far_on(0)
    for offset in (0, 1, 3, 2):
        relay(0, offset)
    own_rows(1, 1)
    own_rows(1, 2)
    near(2)
    own_far(2)
    own_far(1)
    finish(0)

    def block_step(index, carry):
        which = index // (K // NB)

        @pl.when(index == 0)
        def _():
            inverses[0] = symmetric_part(top[0])

        @pl.when(index == K // NB)
        def _():
            finish(2)
            lower = product(top[1], inverses[0], 1, 1, HIGH)
            factor10[...] = lower
            packed = lower.astype(BF16)
            inverses[1] = symmetric_part(top[2] - product(packed, packed, 1, 1, None))

        low = pl.multiple_of((index - which * (K // NB)) * NB, NB)
        factor_block(low, inverses.at[which], staged, base_work, base_out)

        @pl.when(index == 0)
        def _():
            halves_on(2)
            far_on(2, 1)
            far_on(2, 3)
            far_on(1, 1)

        @pl.when(index == 1)
        def _():
            last_far_on(2)
            relay(2, 0)

        @pl.when(index == 2)
        def _():
            relay(2, 1)
            relay(2, 3)

        @pl.when(index == 3)
        def _():
            relay(2, 2)
            far_on(1, 3)
            last_far_on(1)
            relay(1, 0)

        @pl.when(index == 4)
        def _():
            relay(1, 1)
            for shift in range(1, panels):
                piece_copy(shift).wait_recv()
            total = pieces[0]
            for who in range(1, panels):
                total = total + pieces[who]
            sums[me] = total
            for shift in range(1, panels):
                sum_copy(shift).start()

        @pl.when(index == 5)
        def _():
            relay(1, 3)
            for shift in range(1, fronts):
                over_copy(shift).wait_recv()
            total = from_fronts[0]
            for who in range(1, fronts):
                total = total + from_fronts[who]
            cap = onward.shape[1]
            for who in range(panels):
                onward[who] = total[who * cap : (who + 1) * cap, :]
            for shift in range(1, panels):
                inward_copy(shift).start()

        @pl.when(index == 6)
        def _():
            relay(1, 2)

        return carry

    lax.fori_loop(0, 2 * (K // NB), block_step, 0)

    for shift in range(1, panels):
        sum_copy(shift).wait_recv()
    inverse0, inverse1, lower = inverses[0], inverses[1], factor10[...]
    count = panels // 2
    sums0 = jnp.concatenate([sums[piece] for piece in range(count)], axis=0)
    sums1 = jnp.concatenate([sums[count + piece] for piece in range(count)], axis=0)
    carried0 = product(inverse0, sums0, 1, 0, HIGH)
    carried1 = product(inverse1, sums1 - product(lower, carried0, 1, 0, HIGH), 1, 0, HIGH)
    solved1 = product(inverse1, right_side[K:, :] - carried1, 0, 0, HIGH)
    solved0 = product(inverse0, right_side[0:K, :] - carried0 - product(lower, solved1, 0, 0, HIGH), 0, 0, HIGH)
    solved[0:K, :] = solved0
    solved[K:, :] = solved1
    values = product(pick[...], solved[...], 1, 0)
    size = chosen.shape[1]
    for child in range(fronts):
        chosen[child] = values[child * size : (child + 1) * size, :]
    for shift in range(1, fronts):
        pick_copy(shift).start()
    chosen_in[front] = chosen[front]
    front_values[...] = jnp.where(below, known[...], jnp.where(me == 0, solved0, solved1))

    factor0 = product(columns[:, 0:K], inverse0, 1, 1, HIGH)
    current = columns[:, K:] - product(factor0.astype(BF16), lower.astype(BF16), 1, 1, None)
    factor1 = jnp.where(me >= 1, product(current, inverse1, 1, 1, HIGH), 0.0)
    factor[:, 0:K] = factor0
    factor[:, K:] = factor1
    weight1 = product(factor1, inverse1, 1, 0, HIGH)
    weight0 = product(factor0 - product(weight1, lower, 1, 0, HIGH), inverse0, 1, 0, HIGH)
    weights[0] = weight0.astype(BF16)
    weights[1] = weight1.astype(BF16)

    for shift in range(1, panels):
        inward_copy(shift).wait_recv()
    child_values[...] = inward[...]
    child_values[me] = onward[me]
    for shift in range(1, fronts):
        pick_copy(shift).wait_recv()
    total = chosen_in[0]
    for who in range(1, fronts):
        total = total + chosen_in[who]
    cap = child_values.shape[1]
    for lead in range(size // cap):
        child_values[lead] = total[lead * cap : (lead + 1) * cap, :]
    own_late.wait()
    finish(1)
    for kind in range(3):
        drain(kind)
    for shift in range(1, panels):
        piece_copy(shift).wait_send()
        sum_copy(shift).wait_send()
        inward_copy(shift).wait_send()
    for shift in range(1, fronts):
        over_copy(shift).wait_send()
        pick_copy(shift).wait_send()
    for shift in range(1, fronts):
        late_copy(shift).wait()
    for root, indices in roots:

        @pl.when(me == root)
        def _():
            for shift in range(1, panels):
                for index in indices:
                    scatter(shift, index).wait_send()


def panel_step(sizes, parents, table, own_table, early, piv_cols, known, right_side, late):
    panels, fronts, side = sizes
    sem = pltpu.SemaphoreType.DMA
    part = K // panels
    rows, pivots = piv_cols.shape
    rhs = known.shape[1]
    cap = early.shape[2] // panels
    anywhere = pl.BlockSpec(memory_space=pl.ANY)
    vmem = pl.BlockSpec(memory_space=pltpu.VMEM)
    wide = pltpu.VMEM((panels, pivots // panels, rhs), F32)
    few = pltpu.VMEM((fronts, own_table.shape[0] // fronts, rhs), F32)
    over = pltpu.VMEM((fronts, panels * cap, rhs), F32)
    slot = pltpu.VMEM((panels, cap, rhs), F32)
    square = pltpu.VMEM((K, K), F32)
    tile = pltpu.VMEM((NB, NB), F32)
    return pl.pallas_call(
        lambda *refs: panel_kernel((panels, fronts), side, *refs),
        name="panel_step",
        out_shape=(
            jax.ShapeDtypeStruct((2, panels, K, K), BF16),
            jax.ShapeDtypeStruct((fronts,) + late.shape, BF16),
            jax.ShapeDtypeStruct((rows, pivots), F32),
            jax.ShapeDtypeStruct((2, K, K), BF16),
            jax.ShapeDtypeStruct((rows, rhs), F32),
            jax.ShapeDtypeStruct((panels, cap, rhs), F32),
            jax.ShapeDtypeStruct((rows, table.shape[0]), BF16),
        ),
        in_specs=[pl.BlockSpec(memory_space=pltpu.SMEM)] + [vmem] * 3 + [pl.BlockSpec(memory_space=pltpu.HBM)] + [vmem] * 2 + [anywhere],
        out_specs=[anywhere] + [vmem] * 6,
        scratch_shapes=[
            pltpu.VMEM((rows, pivots), F32),
            pltpu.VMEM((rows, pivots), F32),
            pltpu.VMEM((2, rows, K), BF16),
            pltpu.VMEM((own_table.shape[0], pivots), F32),
            over,
            pltpu.VMEM((2, K, K), F32),
            square,
            wide,
            wide,
            pltpu.VMEM((pivots, rhs), F32),
            few,
            few,
            over,
            slot,
            slot,
            pltpu.VMEM((3, K, K), F32),
            pltpu.VMEM((3, part, K), F32),
            wide,
            pltpu.VMEM((NB, K), F32),
            tile,
            tile,
            sem((3, panels)),
            sem((3,)),
        ]
        + [sem((3, 2, 2))] * 4
        + [sem((3, 2, 4, 2))] * 4
        + [sem((panels,))] * 6
        + [sem((fronts,))] * 6
        + [sem((7,))],
        compiler_params=pltpu.CompilerParams(
            collective_id=2, has_side_effects=True, vmem_limit_bytes=28 << 20
        ),
    )(parents, table, own_table, early, piv_cols, known, right_side, late)


def update_kernel(late, blocks, weights, onehot, factor, front_values, child_values, update, *rest):
    outs, sem = rest[:3], rest[3]
    step = pl.program_id(0)
    results = (factor, front_values, child_values)

    @pl.when(step == 0)
    def _():
        for i in range(3):
            pltpu.make_async_copy(results[i], outs[i], sem.at[i]).start()

    fronts, tiles, each, lanes = late.shape
    below = lax.axis_index("panel") >= 2
    count = blocks.shape[1]
    for block in range(count):
        low = block * tiles // count
        rows = jnp.concatenate(
            [late[:, low + t].reshape(fronts * each, lanes) for t in range(tiles // count)], axis=1
        )
        value = product(onehot[...], rows, 1, 0, None)
        for half in range(2):
            value = value - product(weights[half], blocks[half, block], 1, 1, None)
        update[:, block * K : (block + 1) * K] = jnp.where(below, value, 0.0).astype(BF16)

    @pl.when(step == pl.num_programs(0) - 1)
    def _():
        for i in range(3):
            pltpu.make_async_copy(results[i], outs[i], sem.at[i]).wait()


def update_step(late_all, blocks, weights, onehot, factor, front_values, child_values):
    fronts, all_tiles, each, lanes = late_all.shape
    tiles = 2 * K // lanes
    steps = all_tiles // tiles
    first = blocks.shape[1] // 2 - steps
    rows = weights.shape[1]
    anywhere = pl.BlockSpec(memory_space=pl.ANY)
    fixed = pl.BlockSpec(memory_space=pltpu.VMEM)
    like = [jax.ShapeDtypeStruct(x.shape, x.dtype) for x in (factor, front_values, child_values)]
    return pl.pallas_call(
        update_kernel,
        name="update",
        grid=(steps,),
        out_shape=[jax.ShapeDtypeStruct((rows, steps * 2 * K), BF16)] + like,
        in_specs=[
            pl.BlockSpec((fronts, tiles, each, lanes), lambda j: (0, j, 0, 0)),
            pl.BlockSpec((2, 2, K, K), lambda j: (0, j + first, 0, 0)),
            fixed,
            fixed,
            anywhere,
            anywhere,
            anywhere,
        ],
        out_specs=[pl.BlockSpec((rows, 2 * K), lambda j: (0, j))] + [anywhere] * 3,
        scratch_shapes=[pltpu.SemaphoreType.DMA((3,))],
        compiler_params=pltpu.CompilerParams(vmem_limit_bytes=40 << 20),
    )(late_all, blocks, weights, onehot, factor, front_values, child_values)


def on_device(sizes, pivot_columns, child_rows, slot_rows, parents, pivot_rhs, boundary_solution):
    panels, fronts, _ = sizes
    piv_cols = pivot_columns[0]
    pivots = piv_cols.shape[1]
    rows_out = child_rows[0, 0]
    cap, width = rows_out.shape[1:]
    lanes = NB
    lead = pivots // K
    each = panels * cap
    known = boundary_solution[0]

    rows_tiled = rows_out.reshape(panels, cap, width // lanes, lanes).transpose(0, 2, 1, 3)
    slots_wide = jnp.broadcast_to(slot_rows[0, 0][:, :, None], (panels, cap, lanes))
    early, late, table, own_table = exchange_rows(panels, fronts, lead, rows_tiled, slots_wide, pivots // lanes)
    blocks, late_all, factor, weights, front_values, child_values, onehot = panel_step(
        sizes,
        parents,
        table.reshape(fronts * each, lanes),
        own_table.reshape(fronts * lead * cap, lanes),
        early.reshape(fronts, pivots // lanes, each, lanes),
        piv_cols,
        known,
        pivot_rhs[0],
        late,
    )
    update_matrix, factor, front_values, child_values = update_step(
        late_all.reshape(fronts, -1, each, lanes), blocks, weights, onehot, factor, front_values, child_values
    )
    return (factor[None], update_matrix[None], front_values[None], child_values[None, None])


def solution(mesh):
    in_specs = (
        P("front", "panel", None),
        P("front", "panel", None, None, None),
        P("front", "panel", None, None),
        P(),
        P("front", None, None),
        P("front", "panel", None),
    )
    out_specs = (
        P("front", "panel", None),
        P("front", "panel", None),
        P("front", "panel", None),
        P("front", "panel", None, None, None),
    )
    panels, fronts = mesh.shape["panel"], mesh.shape["front"]
    sizes = (panels, fronts, math.isqrt(panels))
    return jax.shard_map(
        lambda *arrays: on_device(sizes, *arrays),
        mesh=mesh,
        in_specs=in_specs,
        out_specs=out_specs,
        check_vma=False,
    )
```

```python
import math

import jax
import jax.numpy as jnp
from jax import lax
from jax.experimental import pallas as pl
from jax.experimental.pallas import tpu as pltpu
from jax.sharding import PartitionSpec as P

K = 512
NB = 128
PIV = 1024
HIGHEST = lax.Precision.HIGHEST
HIGH = lax.Precision.HIGH
MESH = pl.DeviceIdType.MESH
F32 = jnp.float32
BF16 = jnp.bfloat16


def product(left, right, left_dim, right_dim, precision=HIGHEST):
    dims = (((left_dim,), (right_dim,)), ((), ()))
    return lax.dot_general(left, right, dims, precision=precision, preferred_element_type=F32)


def base_inverse(work, inverse):
    sub = lax.broadcasted_iota(jnp.int32, (8, NB), 0)
    lane = lax.broadcasted_iota(jnp.int32, (NB, NB), 1)
    row = lax.broadcasted_iota(jnp.int32, (NB, NB), 0)
    inverse[...] = (lane == row).astype(F32)
    for step in range(NB // 8):
        low = 8 * step
        left = work[low : low + 8, :]
        right = inverse[low : low + 8, :]
        columns = [jnp.broadcast_to(left[:, low + i : low + i + 1], (8, NB)) for i in range(8)]
        pivots = jnp.ones((8, NB), F32)
        recips, splats, rows = [], [], []
        for i in range(8):
            pivot = columns[i][i : i + 1, :]
            recip = 1.0 / pivot
            recips.append(recip)
            pivots = jnp.where(sub == i, pivot, pivots)
            ratio = jnp.where(sub > i, columns[i] * recip, 0.0)
            splat = {}
            for j in range(i + 1, 8):
                splat[j] = columns[j][i : i + 1, :]
                columns[j] = columns[j] - ratio * splat[j]
            splats.append(splat)
            rows.append((left[i : i + 1, :], right[i : i + 1, :]))
            left = left - ratio * rows[i][0]
            right = right - ratio * rows[i][1]
        at = low + 8
        while at < NB:
            size = min(32 - at % 32, NB - at)
            left_tile = work[at : at + size, :]
            right_tile = inverse[at : at + size, :]
            ratios = []
            for i in range(8):
                value = jnp.broadcast_to(left_tile[:, low + i : low + i + 1], (size, NB))
                for j in range(i):
                    value = value - ratios[j] * splats[j][i]
                ratios.append(value * recips[i])
            for i in range(8):
                left_tile = left_tile - ratios[i] * rows[i][0]
                right_tile = right_tile - ratios[i] * rows[i][1]
            work[at : at + size, :] = left_tile
            inverse[at : at + size, :] = right_tile
            at += size
        inverse[low : low + 8, :] = right * lax.rsqrt(pivots)


def symmetric_part(block):
    return (block + block.T) * 0.5


def factor_block(low, joined, staged, base_work, base_out):
    rows = pl.ds(low, NB)
    high = low + NB
    base_work[...] = joined[rows, rows]
    base_inverse(base_work, base_out)
    base = base_out[...]
    solved = product(base, joined[rows, :], 1, 0, HIGH)
    lane = lax.broadcasted_iota(jnp.int32, solved.shape, 1)
    upper = jnp.where(lane >= high, solved, 0.0)
    staged[...] = solved
    staged[:, rows] = base
    strip = joined[:, rows]
    joined[:, rows] = jnp.where(lax.broadcasted_iota(jnp.int32, strip.shape, 0) >= high, 0.0, strip)
    joined[...] = joined[...] - product(upper, staged[...], 0, 0, HIGH)
    joined[rows, :] = jnp.where(lane < high, staged[...], 0.0)


def exchange_kernel(
    counts, rows, slots, early, late, table, own_table, send_a, recv_a, send_b, recv_b, send_s, recv_s,
    front_send, front_recv, front_send_s, front_recv_s, own_send, own_recv, local_sem
):
    panels, fronts = counts
    me = lax.axis_index("panel")
    front = lax.axis_index("front")
    tiles = early.shape[1]
    barrier = pltpu.get_barrier_semaphore()
    for shift in range(1, panels):
        peer = lax.rem(me + shift, panels)
        pl.semaphore_signal(barrier, inc=1, device_id={"panel": peer}, device_id_type=MESH)
    for shift in range(1, fronts):
        peer = lax.rem(front + shift, fronts)
        pl.semaphore_signal(barrier, inc=1, device_id={"front": peer}, device_id_type=MESH)
    pl.semaphore_wait(barrier, panels + fronts - 2)

    def to_panel(source, target, send, recv, shift):
        peer = lax.rem(me + shift, panels)
        return pltpu.make_async_remote_copy(
            src_ref=source(peer),
            dst_ref=target,
            send_sem=send.at[shift],
            recv_sem=recv.at[shift],
            device_id={"panel": peer},
            device_id_type=MESH,
        )

    def early_copy(shift):
        return to_panel(lambda p: rows.at[p, pl.ds(0, tiles)], early.at[front, :, me], send_a, recv_a, shift)

    def slot_copy(shift):
        return to_panel(lambda p: slots.at[p], table.at[front, me], send_s, recv_s, shift)

    def late_copy(shift):
        return to_panel(lambda p: rows.at[p, pl.ds(tiles, late.shape[0])], late.at[:, me], send_b, recv_b, shift)

    lead = own_table.shape[1]

    def own_copy(shift):
        peer = lax.rem(front + shift, fronts)
        return pltpu.make_async_remote_copy(
            src_ref=slots.at[pl.ds(0, lead)],
            dst_ref=own_table.at[front],
            send_sem=own_send.at[shift],
            recv_sem=own_recv.at[shift],
            device_id={"front": peer},
            device_id_type=MESH,
        )

    for shift in range(1, panels):
        slot_copy(shift).start()
        early_copy(shift).start()
    for shift in range(1, fronts):
        own_copy(shift).start()
    own = [
        pltpu.make_async_copy(slots.at[pl.ds(0, lead)], own_table.at[front], local_sem.at[3]),
        pltpu.make_async_copy(rows.at[me, pl.ds(0, tiles)], early.at[front, :, me], local_sem.at[0]),
        pltpu.make_async_copy(slots.at[me], table.at[front, me], local_sem.at[1]),
        pltpu.make_async_copy(rows.at[me, pl.ds(tiles, late.shape[0])], late.at[:, me], local_sem.at[2]),
    ]
    for copy in own:
        copy.start()
    for copy in own:
        copy.wait()
    for shift in range(1, panels):
        slot_copy(shift).wait_recv()
        early_copy(shift).wait_recv()

    def to_front(array, send, recv, shift):
        peer = lax.rem(front + shift, fronts)
        return pltpu.make_async_remote_copy(
            src_ref=array.at[front],
            dst_ref=array.at[front],
            send_sem=send.at[shift],
            recv_sem=recv.at[shift],
            device_id={"front": peer},
            device_id_type=MESH,
        )

    for shift in range(1, fronts):
        to_front(table, front_send_s, front_recv_s, shift).start()
        to_front(early, front_send, front_recv, shift).start()
    for shift in range(1, panels):
        late_copy(shift).start()
    for shift in range(1, panels):
        slot_copy(shift).wait_send()
        early_copy(shift).wait_send()
        late_copy(shift).wait()
    for shift in range(1, fronts):
        to_front(table, front_send_s, front_recv_s, shift).wait()
        to_front(early, front_send, front_recv, shift).wait()
        own_copy(shift).wait()


def exchange_rows(panels, fronts, lead, rows, slots, tiles):
    _, all_tiles, cap, lanes = rows.shape
    sem = pltpu.SemaphoreType.DMA
    return pl.pallas_call(
        lambda *refs: exchange_kernel((panels, fronts), *refs),
        name="exchange",
        out_shape=(
            jax.ShapeDtypeStruct((fronts, tiles, panels, cap, lanes), BF16),
            jax.ShapeDtypeStruct((all_tiles - tiles, panels, cap, lanes), BF16),
            jax.ShapeDtypeStruct((fronts, panels, cap, lanes), jnp.int32),
            jax.ShapeDtypeStruct((fronts, lead, cap, lanes), jnp.int32),
        ),
        in_specs=[pl.BlockSpec(memory_space=pltpu.HBM)] * 2,
        out_specs=[pl.BlockSpec(memory_space=space) for space in (pltpu.VMEM, pl.ANY, pltpu.VMEM, pltpu.VMEM)],
        scratch_shapes=[sem((panels,))] * 6 + [sem((fronts,))] * 6 + [sem((4,))],
        cost_estimate=pl.CostEstimate(flops=20_000_000_000, bytes_accessed=60_000_000, transcendentals=0),
        compiler_params=pltpu.CompilerParams(collective_id=1, has_side_effects=True, vmem_limit_bytes=8 << 20),
    )(rows, slots)


def masked_slots(parents, ref, fronts):
    front = lax.axis_index("front")
    size = ref.shape[0] // fronts
    return jnp.concatenate(
        [jnp.where(parents[c] == front, ref[c * size : (c + 1) * size, :], -1) for c in range(fronts)], axis=0
    )


def assemble(parents, table, early, piv_cols, columns, halves):
    fronts, _, each, lanes = early.shape
    kept = masked_slots(parents, table, fronts)
    lane = lax.broadcasted_iota(jnp.int32, kept.shape, 1)
    chosen = jnp.concatenate(
        [(kept == lane + t * lanes).astype(F32) for t in range(piv_cols.shape[0] // lanes)], axis=1
    )
    small = chosen.astype(BF16)
    half = piv_cols.shape[1] // 2
    for h in range(2):
        tiles = half // lanes
        rows = jnp.concatenate(
            [early[:, h * tiles + t].reshape(fronts * each, lanes) for t in range(tiles)], axis=1
        )
        value = piv_cols[:, h * half : (h + 1) * half] + product(small, rows, 0, 0, None)
        columns[:, h * half : (h + 1) * half] = value
        halves[h] = value.astype(BF16)
    return chosen


def select_values(parents, own_table, chosen, known, fronts, onehot, pick, picked):
    each = chosen.shape[0] // fronts
    lanes = own_table.shape[1]
    onehot[...] = chosen.T.astype(BF16)
    found = product(chosen, known[...], 1, 0)
    for child in range(fronts):
        picked[child] = found[child * each : (child + 1) * each, :]
    size = own_table.shape[0] // fronts
    own = masked_slots(parents, own_table, fronts)
    cap = size * K // pick.shape[1]
    where = lax.rem(lax.broadcasted_iota(jnp.int32, own.shape, 0), size) // cap
    target = jnp.where(own >= 0, own + where * K, -1)
    lane = lax.broadcasted_iota(jnp.int32, own.shape, 1)
    for t in range(pick.shape[1] // lanes):
        pick[:, t * lanes : (t + 1) * lanes] = (target == lane + t * lanes).astype(F32)


def panel_kernel(
    counts, side, parents, table, own_table, early, own_columns, known, right_side, late,
    blocks, late_all, factor, weights, front_values, child_values, onehot,
    piv_cols, columns, halves, pick, picked,
    inverses, factor10, partial, sums, solved, chosen, chosen_in, from_fronts, onward, inward,
    top, chunk, pieces, staged, base_work, base_out,
    scatter_send, scatter_recv, whole_send, whole_recv, half_send, half_recv,
    far_send, far_recv, farther_send, farther_recv,
    piece_send, piece_recv, sum_send, sum_recv, inward_send, inward_recv,
    late_send, late_recv, over_send, over_recv, pick_send, pick_recv, local_sem,
):
    panels, fronts = counts
    me = lax.axis_index("panel")
    front = lax.axis_index("front")
    across, along = me // side, lax.rem(me, side)
    part = top.shape[1] // panels
    load = pltpu.make_async_copy(own_columns, piv_cols, local_sem.at[6])
    load.start()
    barrier = pltpu.get_barrier_semaphore()
    for shift in range(1, panels):
        peer = lax.rem(me + shift, panels)
        pl.semaphore_signal(barrier, inc=1, device_id={"panel": peer}, device_id_type=MESH)
    for shift in range(1, fronts):
        peer = lax.rem(front + shift, fronts)
        pl.semaphore_signal(barrier, inc=1, device_id={"front": peer}, device_id_type=MESH)
    load.wait()
    chosen_rows = assemble(parents, table, early, piv_cols, columns, halves)
    pl.semaphore_wait(barrier, panels + fronts - 2)

    def chunk_rows(who):
        return pl.ds(pl.multiple_of(who * part, 8), part)

    def scatter(shift, index):
        peer = lax.rem(me + shift, panels)
        lanes = pl.ds(K if index == 2 else 0, K)
        return pltpu.make_async_remote_copy(
            src_ref=columns.at[chunk_rows(peer), lanes],
            dst_ref=chunk.at[index],
            send_sem=scatter_send.at[index, shift],
            recv_sem=scatter_recv.at[index],
            device_id={"panel": peer},
            device_id_type=MESH,
        )

    def own_chunk(index):
        lanes = pl.ds(K if index == 2 else 0, K)
        return pltpu.make_async_copy(columns.at[chunk_rows(me), lanes], chunk.at[index], local_sem.at[index])

    roots = ((0, (0,)), (1, (1, 2)))
    for root, indices in roots:

        @pl.when(me == root)
        def _():
            for shift in range(1, panels):
                for index in indices:
                    scatter(shift, index).start()
            for index in indices:
                own_chunk(index).start()

    coords = [[lax.rem(at + step, side) for step in range(side)] for at in (across, along)]

    def place(half, first, second):
        near_axis, far_axis = (coords[0], coords[1]) if half == 0 else (coords[1], coords[0])
        first, second = near_axis[first % side], far_axis[second % side]
        return first * side + second if half == 0 else second * side + first

    def view(kind, half, who, rows):
        if kind != 1:
            size = part if rows is None else part // 2
            low = who * part + (part // 2 if rows == 1 else 0)
            return top.at[pl.ds(kind // 2, kind // 2 + 1), pl.ds(pl.multiple_of(low, 8), size), pl.ds(half * (K // 2), K // 2)]
        ref = blocks.at[half, who]
        return ref if rows is None else ref.at[pl.ds(rows * (K // 2), K // 2)]

    def move(kind, half, who, rows, target, send, recv, slot):
        ref = view(kind, half, who, rows)
        return pltpu.make_async_remote_copy(
            src_ref=ref,
            dst_ref=ref,
            send_sem=send.at[slot],
            recv_sem=recv.at[slot],
            device_id={"panel": target},
            device_id_type=MESH,
        )

    def whole(kind, half, way):
        step = 1 if way == 0 else -1
        copy = move(kind, half, me, None, place(half, step, 0), whole_send, whole_recv, (kind, half, way))
        return kind, copy, me, place(half, -step, 0)

    def halved(kind, half, way):
        step = 1 if way == 0 else -1
        who = place(half, -step, 0)
        copy = move(kind, half, who, way, place(half, step, 0), half_send, half_recv, (kind, half, way))
        return kind, copy, who, place(half, 2, 0)

    def far(kind, half, offset, way):
        step = 1 if way == 0 else -1
        who = place(half, offset, 0)
        copy = move(kind, half, who, None, place(half, 0, step), far_send, far_recv, (kind, half, offset, way))
        return kind, copy, who, place(half, offset, -step)

    def farther(kind, half, offset, way):
        step = 1 if way == 0 else -1
        who = place(half, offset, -step)
        copy = move(
            kind, half, who, way, place(half, 0, step), farther_send, farther_recv, (kind, half, offset, way)
        )
        return kind, copy, who, place(half, offset, 2)

    def guarded(kind, who, act):
        if kind != 1:
            act()
        else:
            pl.when(who >= 2)(act)

    def start(hop):
        guarded(hop[0], hop[2], hop[1].start)

    def sent(hop):
        guarded(hop[0], hop[2], hop[1].wait_send)

    def arrived(hop):
        guarded(hop[0], hop[3], hop[1].wait_recv)

    both = [(half, way) for half in range(2) for way in range(2)]

    def near(kind):
        for half, way in both:
            start(whole(kind, half, way))

    def own_far(kind):
        for half, way in both:
            start(far(kind, half, 0, way))

    def halves_on(kind):
        for half, way in both:
            arrived(whole(kind, half, way))
            start(halved(kind, half, way))

    def far_on(kind, offset):
        for half, way in both:
            start(far(kind, half, offset, way))

    def last_far_on(kind):
        for half in range(2):
            for way in range(2):
                arrived(halved(kind, half, way))
            for way in range(2):
                start(far(kind, half, 2, way))

    def relay(kind, offset):
        for half, way in both:
            arrived(far(kind, half, offset, way))
            start(farther(kind, half, offset, way))

    def finish(kind):
        for half, way in both:
            for offset in range(4):
                arrived(farther(kind, half, offset, way))

    def drain(kind):
        for half, way in both:
            sent(whole(kind, half, way))
            sent(halved(kind, half, way))
            for offset in range(4):
                sent(far(kind, half, offset, way))
                sent(farther(kind, half, offset, way))

    def over_copy(shift):
        peer = lax.rem(front + shift, fronts)
        return pltpu.make_async_remote_copy(
            src_ref=picked.at[peer],
            dst_ref=from_fronts.at[front],
            send_sem=over_send.at[shift],
            recv_sem=over_recv.at[shift],
            device_id={"front": peer},
            device_id_type=MESH,
        )

    def inward_copy(shift):
        peer = lax.rem(me + shift, panels)
        return pltpu.make_async_remote_copy(
            src_ref=onward.at[peer],
            dst_ref=inward.at[me],
            send_sem=inward_send.at[shift],
            recv_sem=inward_recv.at[shift],
            device_id={"panel": peer},
            device_id_type=MESH,
        )

    def pick_copy(shift):
        peer = lax.rem(front + shift, fronts)
        return pltpu.make_async_remote_copy(
            src_ref=chosen.at[peer],
            dst_ref=chosen_in.at[front],
            send_sem=pick_send.at[shift],
            recv_sem=pick_recv.at[shift],
            device_id={"front": peer},
            device_id_type=MESH,
        )

    def late_copy(shift):
        peer = lax.rem(front + shift, fronts)
        return pltpu.make_async_remote_copy(
            src_ref=late,
            dst_ref=late_all.at[front],
            send_sem=late_send.at[shift],
            recv_sem=late_recv.at[shift],
            device_id={"front": peer},
            device_id_type=MESH,
        )

    def piece_copy(shift):
        peer = lax.rem(me + shift, panels)
        return pltpu.make_async_remote_copy(
            src_ref=partial.at[peer],
            dst_ref=pieces.at[me],
            send_sem=piece_send.at[shift],
            recv_sem=piece_recv.at[shift],
            device_id={"panel": peer},
            device_id_type=MESH,
        )

    def sum_copy(shift):
        peer = lax.rem(me + shift, panels)
        return pltpu.make_async_remote_copy(
            src_ref=sums.at[me],
            dst_ref=sums.at[me],
            send_sem=sum_send.at[shift],
            recv_sem=sum_recv.at[shift],
            device_id={"panel": peer},
            device_id_type=MESH,
        )

    own_halves = pltpu.make_async_copy(halves, blocks.at[:, me], local_sem.at[3])
    own_late = pltpu.make_async_copy(late, late_all.at[front], local_sem.at[5])
    own_halves.start()
    own_late.start()
    own_halves.wait()
    near(1)
    select_values(parents, own_table, chosen_rows, known, fronts, onehot, pick, picked)
    for shift in range(1, fronts):
        over_copy(shift).start()
    for shift in range(1, fronts):
        late_copy(shift).start()
    from_fronts[front] = picked[front]
    below = me >= 2
    boundary = jnp.where(below, known[...], 0.0)
    width = partial.shape[1]
    for half in range(2):
        value = product(columns[:, half * K : (half + 1) * K], boundary, 0, 0, HIGH)
        for piece in range(panels // 2):
            partial[half * (panels // 2) + piece] = value[piece * width : (piece + 1) * width, :]
    pieces[me] = partial[me]

    def own_rows(root, index):

        @pl.when(me == root)
        def _():
            own_chunk(index).wait()

        @pl.when(me != root)
        def _():
            scatter(1, index).wait_recv()

        top[index, chunk_rows(me), :] = chunk[index]

    own_rows(0, 0)
    near(0)
    own_far(0)
    halves_on(1)
    halves_on(0)
    far_on(0, 1)
    far_on(0, 3)
    for shift in range(1, panels):
        piece_copy(shift).start()
    last_far_on(0)
    for offset in (0, 1, 3, 2):
        relay(0, offset)
    own_rows(1, 1)
    own_rows(1, 2)
    near(2)
    own_far(2)
    own_far(1)
    finish(0)

    def block_step(index, carry):
        which = index // (K // NB)

        @pl.when(index == 0)
        def _():
            inverses[0] = symmetric_part(top[0])

        @pl.when(index == K // NB)
        def _():
            finish(2)
            lower = product(top[1], inverses[0], 1, 1, HIGH)
            factor10[...] = lower
            packed = lower.astype(BF16)
            inverses[1] = symmetric_part(top[2] - product(packed, packed, 1, 1, None))

        low = pl.multiple_of((index - which * (K // NB)) * NB, NB)
        factor_block(low, inverses.at[which], staged, base_work, base_out)

        @pl.when(index == 0)
        def _():
            halves_on(2)
            far_on(2, 1)
            far_on(2, 3)
            far_on(1, 1)

        @pl.when(index == 1)
        def _():
            last_far_on(2)
            relay(2, 0)

        @pl.when(index == 2)
        def _():
            relay(2, 1)
            relay(2, 3)

        @pl.when(index == 3)
        def _():
            relay(2, 2)
            far_on(1, 3)
            last_far_on(1)
            relay(1, 0)

        @pl.when(index == 4)
        def _():
            relay(1, 1)
            for shift in range(1, panels):
                piece_copy(shift).wait_recv()
            total = pieces[0]
            for who in range(1, panels):
                total = total + pieces[who]
            sums[me] = total
            for shift in range(1, panels):
                sum_copy(shift).start()

        @pl.when(index == 5)
        def _():
            relay(1, 3)
            for shift in range(1, fronts):
                over_copy(shift).wait_recv()
            total = from_fronts[0]
            for who in range(1, fronts):
                total = total + from_fronts[who]
            cap = onward.shape[1]
            for who in range(panels):
                onward[who] = total[who * cap : (who + 1) * cap, :]
            for shift in range(1, panels):
                inward_copy(shift).start()

        @pl.when(index == 6)
        def _():
            relay(1, 2)

        return carry

    lax.fori_loop(0, 2 * (K // NB), block_step, 0)

    for shift in range(1, panels):
        sum_copy(shift).wait_recv()
    inverse0, inverse1, lower = inverses[0], inverses[1], factor10[...]
    count = panels // 2
    sums0 = jnp.concatenate([sums[piece] for piece in range(count)], axis=0)
    sums1 = jnp.concatenate([sums[count + piece] for piece in range(count)], axis=0)
    carried0 = product(inverse0, sums0, 1, 0, HIGH)
    carried1 = product(inverse1, sums1 - product(lower, carried0, 1, 0, HIGH), 1, 0, HIGH)
    solved1 = product(inverse1, right_side[K:, :] - carried1, 0, 0, HIGH)
    solved0 = product(inverse0, right_side[0:K, :] - carried0 - product(lower, solved1, 0, 0, HIGH), 0, 0, HIGH)
    solved[0:K, :] = solved0
    solved[K:, :] = solved1
    values = product(pick[...], solved[...], 1, 0)
    size = chosen.shape[1]
    for child in range(fronts):
        chosen[child] = values[child * size : (child + 1) * size, :]
    for shift in range(1, fronts):
        pick_copy(shift).start()
    chosen_in[front] = chosen[front]
    front_values[...] = jnp.where(below, known[...], jnp.where(me == 0, solved0, solved1))

    factor0 = product(columns[:, 0:K], inverse0, 1, 1, HIGH)
    current = columns[:, K:] - product(factor0.astype(BF16), lower.astype(BF16), 1, 1, None)
    factor1 = jnp.where(me >= 1, product(current, inverse1, 1, 1, HIGH), 0.0)
    factor[:, 0:K] = factor0
    factor[:, K:] = factor1
    weight1 = product(factor1, inverse1, 1, 0, HIGH)
    weight0 = product(factor0 - product(weight1, lower, 1, 0, HIGH), inverse0, 1, 0, HIGH)
    weights[0] = weight0.astype(BF16)
    weights[1] = weight1.astype(BF16)

    for shift in range(1, panels):
        inward_copy(shift).wait_recv()
    child_values[...] = inward[...]
    child_values[me] = onward[me]
    for shift in range(1, fronts):
        pick_copy(shift).wait_recv()
    total = chosen_in[0]
    for who in range(1, fronts):
        total = total + chosen_in[who]
    cap = child_values.shape[1]
    for lead in range(size // cap):
        child_values[lead] = total[lead * cap : (lead + 1) * cap, :]
    own_late.wait()
    finish(1)
    for kind in range(3):
        drain(kind)
    for shift in range(1, panels):
        piece_copy(shift).wait_send()
        sum_copy(shift).wait_send()
        inward_copy(shift).wait_send()
    for shift in range(1, fronts):
        over_copy(shift).wait_send()
        pick_copy(shift).wait_send()
    for shift in range(1, fronts):
        late_copy(shift).wait()
    for root, indices in roots:

        @pl.when(me == root)
        def _():
            for shift in range(1, panels):
                for index in indices:
                    scatter(shift, index).wait_send()


def panel_step(sizes, parents, table, own_table, early, piv_cols, known, right_side, late):
    panels, fronts, side = sizes
    sem = pltpu.SemaphoreType.DMA
    part = K // panels
    rows, pivots = piv_cols.shape
    rhs = known.shape[1]
    cap = early.shape[2] // panels
    anywhere = pl.BlockSpec(memory_space=pl.ANY)
    vmem = pl.BlockSpec(memory_space=pltpu.VMEM)
    wide = pltpu.VMEM((panels, pivots // panels, rhs), F32)
    few = pltpu.VMEM((fronts, own_table.shape[0] // fronts, rhs), F32)
    over = pltpu.VMEM((fronts, panels * cap, rhs), F32)
    slot = pltpu.VMEM((panels, cap, rhs), F32)
    square = pltpu.VMEM((K, K), F32)
    tile = pltpu.VMEM((NB, NB), F32)
    return pl.pallas_call(
        lambda *refs: panel_kernel((panels, fronts), side, *refs),
        name="panel_step",
        out_shape=(
            jax.ShapeDtypeStruct((2, panels, K, K), BF16),
            jax.ShapeDtypeStruct((fronts,) + late.shape, BF16),
            jax.ShapeDtypeStruct((rows, pivots), F32),
            jax.ShapeDtypeStruct((2, K, K), BF16),
            jax.ShapeDtypeStruct((rows, rhs), F32),
            jax.ShapeDtypeStruct((panels, cap, rhs), F32),
            jax.ShapeDtypeStruct((rows, table.shape[0]), BF16),
        ),
        in_specs=[pl.BlockSpec(memory_space=pltpu.SMEM)] + [vmem] * 3 + [pl.BlockSpec(memory_space=pltpu.HBM)] + [vmem] * 2 + [anywhere],
        out_specs=[anywhere] + [vmem] * 6,
        scratch_shapes=[
            pltpu.VMEM((rows, pivots), F32),
            pltpu.VMEM((rows, pivots), F32),
            pltpu.VMEM((2, rows, K), BF16),
            pltpu.VMEM((own_table.shape[0], pivots), F32),
            over,
            pltpu.VMEM((2, K, K), F32),
            square,
            wide,
            wide,
            pltpu.VMEM((pivots, rhs), F32),
            few,
            few,
            over,
            slot,
            slot,
            pltpu.VMEM((3, K, K), F32),
            pltpu.VMEM((3, part, K), F32),
            wide,
            pltpu.VMEM((NB, K), F32),
            tile,
            tile,
            sem((3, panels)),
            sem((3,)),
        ]
        + [sem((3, 2, 2))] * 4
        + [sem((3, 2, 4, 2))] * 4
        + [sem((panels,))] * 6
        + [sem((fronts,))] * 6
        + [sem((7,))],
        compiler_params=pltpu.CompilerParams(
            collective_id=2, has_side_effects=True, vmem_limit_bytes=28 << 20
        ),
    )(parents, table, own_table, early, piv_cols, known, right_side, late)


def update_kernel(late, blocks, weights, onehot, factor, front_values, child_values, update, *rest):
    outs, sem = rest[:3], rest[3]
    step = pl.program_id(0)
    results = (factor, front_values, child_values)

    @pl.when(step == 0)
    def _():
        for i in range(3):
            pltpu.make_async_copy(results[i], outs[i], sem.at[i]).start()

    fronts, tiles, each, lanes = late.shape
    below = lax.axis_index("panel") >= 2
    count = blocks.shape[1]
    for block in range(count):
        low = block * tiles // count
        rows = jnp.concatenate(
            [late[:, low + t].reshape(fronts * each, lanes) for t in range(tiles // count)], axis=1
        )
        value = product(onehot[...], rows, 1, 0, None)
        for half in range(2):
            value = value - product(weights[half], blocks[half, block], 1, 1, None)
        update[:, block * K : (block + 1) * K] = jnp.where(below, value, 0.0).astype(BF16)

    @pl.when(step == pl.num_programs(0) - 1)
    def _():
        for i in range(3):
            pltpu.make_async_copy(results[i], outs[i], sem.at[i]).wait()


def update_step(late_all, blocks, weights, onehot, factor, front_values, child_values):
    fronts, all_tiles, each, lanes = late_all.shape
    tiles = 2 * K // lanes
    steps = all_tiles // tiles
    first = blocks.shape[1] // 2 - steps
    rows = weights.shape[1]
    anywhere = pl.BlockSpec(memory_space=pl.ANY)
    fixed = pl.BlockSpec(memory_space=pltpu.VMEM)
    like = [jax.ShapeDtypeStruct(x.shape, x.dtype) for x in (factor, front_values, child_values)]
    return pl.pallas_call(
        update_kernel,
        name="update",
        grid=(steps,),
        out_shape=[jax.ShapeDtypeStruct((rows, steps * 2 * K), BF16)] + like,
        in_specs=[
            pl.BlockSpec((fronts, tiles, each, lanes), lambda j: (0, j, 0, 0)),
            pl.BlockSpec((2, 2, K, K), lambda j: (0, j + first, 0, 0)),
            fixed,
            fixed,
            anywhere,
            anywhere,
            anywhere,
        ],
        out_specs=[pl.BlockSpec((rows, 2 * K), lambda j: (0, j))] + [anywhere] * 3,
        scratch_shapes=[pltpu.SemaphoreType.DMA((3,))],
        compiler_params=pltpu.CompilerParams(vmem_limit_bytes=40 << 20),
    )(late_all, blocks, weights, onehot, factor, front_values, child_values)


def on_device(sizes, pivot_columns, child_rows, slot_rows, parents, pivot_rhs, boundary_solution):
    panels, fronts, _ = sizes
    piv_cols = pivot_columns[0]
    pivots = piv_cols.shape[1]
    rows_out = child_rows[0, 0]
    cap, width = rows_out.shape[1:]
    lanes = NB
    lead = pivots // K
    each = panels * cap
    known = boundary_solution[0]

    rows_tiled = rows_out.reshape(panels, cap, width // lanes, lanes).transpose(0, 2, 1, 3)
    slots_wide = jnp.broadcast_to(slot_rows[0, 0][:, :, None], (panels, cap, lanes))
    early, late, table, own_table = exchange_rows(panels, fronts, lead, rows_tiled, slots_wide, pivots // lanes)
    blocks, late_all, factor, weights, front_values, child_values, onehot = panel_step(
        sizes,
        parents,
        table.reshape(fronts * each, lanes),
        own_table.reshape(fronts * lead * cap, lanes),
        early.reshape(fronts, pivots // lanes, each, lanes),
        piv_cols,
        known,
        pivot_rhs[0],
        late,
    )
    update_matrix, factor, front_values, child_values = update_step(
        late_all.reshape(fronts, -1, each, lanes), blocks, weights, onehot, factor, front_values, child_values
    )
    return (factor[None], update_matrix[None], front_values[None], child_values[None, None])


def solution(mesh):
    in_specs = (
        P("front", "panel", None),
        P("front", "panel", None, None, None),
        P("front", "panel", None, None),
        P(),
        P("front", None, None),
        P("front", "panel", None),
    )
    out_specs = (
        P("front", "panel", None),
        P("front", "panel", None),
        P("front", "panel", None),
        P("front", "panel", None, None, None),
    )
    panels, fronts = mesh.shape["panel"], mesh.shape["front"]
    sizes = (panels, fronts, math.isqrt(panels))
    return jax.shard_map(
        lambda *arrays: on_device(sizes, *arrays),
        mesh=mesh,
        in_specs=in_specs,
        out_specs=out_specs,
        check_vma=False,
    )
```
